32 devices in a mesh: dp: 8 (over z, x), expert: 4 (over y, core).
Axes of the slice: x: 2, y: 2, z: 4, core: 2. Of those that a mesh axis runs over, the one named last changes fastest.
Arguments:
- tokens: bfloat16 [4096, 1024], P(('dp', 'expert')), may hold values from -6 to 6
- prefix_len: int32 [8], P('dp'), may hold values from 0 to 512
- routes: int32 [4096, 8], P(('dp', 'expert')), may hold values from 0 to 15, all different within a row; in each aligned block of 128 rows (0 to 127, 128 to 255, ...) at most 128 rows name the same one
- norm1_gain: float32 [1024], replicated, may hold values from 0.5 to 1.5
- w_query: bfloat16 [1024, 1024], replicated, may hold values from -0.1875 to 0.1875
- w_key: bfloat16 [1024, 512], replicated, may hold values from -0.1875 to 0.1875
- w_value: bfloat16 [1024, 512], replicated, may hold values from -0.1875 to 0.1875
- w_output: bfloat16 [1024, 1024], replicated, may hold values from -4 to 4
- norm2_gain: float32 [1024], replicated, may hold values from 0.5 to 1.5
- w_router: bfloat16 [1024, 16], replicated, may hold values from -0.09375 to 0.09375
- w_gate: bfloat16 [16, 1024, 512], P('expert'), may hold values from -0.1875 to 0.1875
- w_up: bfloat16 [16, 1024, 512], P('expert'), may hold values from -0.1875 to 0.1875
- w_down: bfloat16 [16, 512, 1024], P('expert'), may hold values from -1 to 1
- cotangent: bfloat16 [4096, 1024], P(('dp', 'expert')), may hold values from -6 to 6
Outputs:
- block_out: bfloat16 [4096, 1024], P(('dp', 'expert'))
- grad_tokens: bfloat16 [4096, 1024], P(('dp', 'expert'))
- grad_norm1: float32 [1024], P(('dp', 'expert'))
- grad_query_w: float32 [1024, 1024], P(('dp', 'expert'))
- grad_key_w: float32 [1024, 512], P(('dp', 'expert'))
- grad_value_w: float32 [1024, 512], P(('dp', 'expert'))
- grad_output_w: float32 [1024, 1024], P(('dp', 'expert'))
- grad_norm2: float32 [1024], P(('dp', 'expert'))
- grad_router: float32 [1024, 16], P(('dp', 'expert'))
- grad_gate_w: float32 [16, 1024, 512], P('expert', 'dp')
- grad_up_w: float32 [16, 1024, 512], P('expert', 'dp')
- grad_down_w: float32 [16, 512, 1024], P('expert', None, 'dp')
The draws below stay inside these ranges and needn't reach their ends.
Inputs may be any that keep to these rules, and one draw needn't show every extreme that they name: `routes`: among the 128 rows of one device no expert is named more than 128 times, and in every draw some device names some expert exactly 128 times.
All inputs are finite; a program needn't handle non-finite values.
Results may differ from the reference program's by a relative error of at most 0.018.
Values may be sent and summed in bfloat16 or wider, within the bound.
No kernel may reach another device: no remote copies, remote signals or barrier semaphores. Data moves between devices by JAX's collectives and lax.ppermute only.
A program may use at most 192 MiB of HBM per device.

```python
import math
import jax
import jax.numpy as jnp
import numpy as np
from jax import lax

D = 1024
H = 16
KV = 8
HD = 64
FE = 512
TOPK = 8
TOK_DEV = 128
EXPERTS = 16
CAP = 128
SEQ = 512
SEQS = 8
TOKENS = 4096
N_EXPERT = 4


def with_ends(drawn, own_key, smallest, largest):
    spot = [jax.random.randint(jax.random.fold_in(own_key, axis), (), 0, length) for axis, length in enumerate(drawn.shape)]
    main_axis = drawn.shape.index(max(drawn.shape))
    neighbour = spot[:main_axis] + [(spot[main_axis] + 1) % drawn.shape[main_axis]] + spot[main_axis + 1:]
    return drawn.at[tuple(spot)].set(smallest).at[tuple(neighbour)].set(largest)


def levels(own_key, dims, split, low, largest):
    def one(position, parts):
        steps = jax.random.uniform(jax.random.fold_in(jax.random.fold_in(own_key, 6), position), (parts,), jnp.float32, low / len(split), largest / len(split))
        return jnp.repeat(jnp.exp(steps), dims[position] // parts).reshape((-1,) + (1,) * (len(dims) - position - 1))

    loudness = one(*split[0])
    for cut in split[1:]:
        loudness = loudness * one(*cut)
    return loudness


def assign_block(stream_key, own, number, rows, count, top, limit, skew):
    order = jax.random.permutation(stream_key, count)
    crowded, ordinary = load_shares(count, rows * top, limit, skew, True), load_shares(count, rows * top, limit, skew, False)
    places = jnp.arange(count)

    def named(sizes, offset_by):
        used = int((sizes > 0).sum())
        fixed = max(1, used // 4)
        shifted = fixed + (places - fixed + offset_by * (used - fixed)) % max(1, count - fixed)
        return jnp.zeros((count,), jnp.int32).at[order[jnp.where(places < fixed, places, shifted)]].set(jnp.asarray(sizes, jnp.int32))

    sizes = jnp.where(number % 4 == 0, named(crowded, number // 4), named(ordinary, number - number // 4 - 1))
    mixed = jax.random.permutation(jax.random.fold_in(own, 3), count)
    giver, sink = mixed[0:count // 2 * 2:2], mixed[1:count // 2 * 2:2]
    room = jnp.minimum(sizes[giver] - 1, limit - sizes[sink]) // 2
    room = jnp.where((giver == order[0]) | (sink == order[0]) | (sizes[sink] == 0), 0, jnp.maximum(room, 0))
    shifted = jax.random.randint(jax.random.fold_in(own, 4), (count // 2,), 0, 1 << 20) % (room + 1)
    sizes = sizes.at[giver].add(-shifted).at[sink].add(shifted)
    labels = jnp.searchsorted(jnp.cumsum(sizes), jnp.arange(rows * top), side="right").astype(jnp.int32)
    grid = labels.reshape(top, rows).T
    grid = grid[jax.random.permutation(jax.random.fold_in(own, 1), rows)]
    offset_by = jax.random.randint(jax.random.fold_in(own, 2), (rows, 1), 0, top)
    return jnp.take_along_axis(grid, (jnp.arange(top)[None, :] + offset_by) % top, axis=1)


def load_shares(count, total, bound, slope, full):
    weights = [(1 << 20) // math.isqrt(grade ** slope) + 1 for grade in range(1, count + 1)]
    largest = bound if full else min(bound, max(-(-total // count), total * weights[0] // sum(weights)))
    least = 1 if total - largest >= count - 1 else 0
    counts, rest = [largest] + [least] * (count - 1), total - largest - least * (count - 1)
    while rest > 0:
        free = [i for i in range(1, count) if counts[i] < largest] or [i for i in range(1, count) if counts[i] < bound]
        pool, remaining = sum([weights[i] for i in free]), rest
        for i in free:
            extra = min(bound - counts[i], max(1, remaining * weights[i] // pool), rest)
            counts[i] = counts[i] + extra
            rest = rest - extra
    return np.array(counts)


def centred(key, dims, deviation, bound, split=(), kind=jnp.bfloat16):
    level = levels(key, dims, split, -0.22, 0.18) if split else 1.0
    drawn = jax.random.normal(key, dims, jnp.float32) * deviation * level
    return jnp.minimum(jnp.maximum(drawn, -bound), bound).astype(kind)


def setup_inputs(seed: int = 0) -> dict:
    key_list = jax.random.split(jax.random.key(seed), 15)
    tokens = centred(key_list[0], (TOKENS, D), 1.0, 6.0, ((0, 32),))
    prefix_len = with_ends(jax.random.randint(key_list[1], (SEQS,), 0, SEQ + 1), jax.random.fold_in(key_list[1], 1), 0, SEQ).astype(jnp.int32)
    routes_keys = jax.random.split(jax.random.fold_in(key_list[2], 1), TOKENS // TOK_DEV)
    routes_turns = jax.random.permutation(jax.random.fold_in(key_list[2], 3), TOKENS // TOK_DEV)
    routes = jax.vmap(lambda own, number: assign_block(jax.random.fold_in(key_list[2], 2), own, number, TOK_DEV, EXPERTS, TOPK, CAP, 1))(routes_keys, routes_turns).reshape((TOKENS, TOPK))
    norm1_gain = jnp.clip(1.0 + 0.1 * jax.random.normal(key_list[3], (D,), jnp.float32), 0.5, 1.5)
    w_query = centred(key_list[4], (D, H * HD), D ** -0.5, 0.1875)
    w_key = centred(key_list[5], (D, KV * HD), D ** -0.5, 0.1875)
    w_value = centred(key_list[6], (D, KV * HD), D ** -0.5, 0.1875)
    w_output = centred(key_list[7], (H * HD, D), (max(2, H * HD // 512)) ** -0.5, 4.0)
    norm2_gain = jnp.clip(1.0 + 0.1 * jax.random.normal(key_list[8], (D,), jnp.float32), 0.5, 1.5)
    w_router = centred(key_list[9], (D, EXPERTS), (4 * D) ** -0.5, 0.09375)
    w_gate = centred(key_list[10], (EXPERTS, D, FE), D ** -0.5, 0.1875, ((0, 4),))
    w_up = centred(key_list[11], (EXPERTS, D, FE), D ** -0.5, 0.1875, ((0, 4),))
    w_down = centred(key_list[12], (EXPERTS, FE, D), (FE // 16) ** -0.5, 1.0, ((0, 4),))
    cotangent = centred(key_list[13], (TOKENS, D), 1.0, 6.0, ((0, 32),))
    return dict(tokens=tokens, prefix_len=prefix_len, routes=routes, norm1_gain=norm1_gain, w_query=w_query, w_key=w_key, w_value=w_value, w_output=w_output, norm2_gain=norm2_gain, w_router=w_router, w_gate=w_gate, w_up=w_up, w_down=w_down, cotangent=cotangent)


norm_eps = 1e-05
masked_score = -1e+30

@jax.custom_vjp
def low(v):
    return lax.optimization_barrier(v.astype(jnp.bfloat16)).astype(jnp.float32)

@jax.custom_vjp
def low_back(v):
    return v

def low_keep(v):
    return (low(v), None)

def low_pass(kept, grad):
    return (grad,)

def back_keep(v):
    return (v, None)

def back_low(kept, grad):
    return (low(grad),)
low.defvjp(low_keep, low_pass)
low_back.defvjp(back_keep, back_low)

def matmul_hi(left, right):
    return jnp.dot(left, right, precision=lax.Precision.HIGHEST)

def rms_norm(source, gain_vec):
    return source * lax.rsqrt(lax.optimization_barrier(jnp.mean(source * source, axis=-1, keepdims=True)) + norm_eps) * gain_vec

def rope_tables(positions, head_width):
    half_width = head_width // 2
    frequency = jnp.exp(jnp.arange(half_width, dtype=jnp.float32) * (-2.0 * math.log(10000.0) / head_width))
    angles = positions.astype(jnp.float32)[:, None] * frequency[None, :]
    return (jnp.concatenate([jnp.cos(angles), jnp.cos(angles)], 1), jnp.concatenate([jnp.sin(angles), jnp.sin(angles)], 1))

def rotate(source):
    half_width = source.shape[-1] // 2
    return jnp.concatenate([-source[..., half_width:], source[..., :half_width]], -1)

def apply_rope(source, cosine_table, sine_table):
    return source * cosine_table[:, None, :] + rotate(source) * sine_table[:, None, :]

def attend(query_rows, key_seq, value_seq, block_start, prefix_here):
    row_count = query_rows.shape[0]
    query_groups = query_rows.reshape(row_count, KV, H // KV, HD)
    scores = jnp.einsum('qkgd,tkd->kgqt', query_groups, key_seq, precision=lax.Precision.HIGHEST) * (1.0 / math.sqrt(HD))
    scores = low_back(scores)
    query_pos = block_start + jnp.arange(row_count, dtype=jnp.int32)
    key_pos = jnp.arange(key_seq.shape[0], dtype=jnp.int32)
    allowed = (key_pos[None, :] <= query_pos[:, None]) | (key_pos[None, :] < prefix_here)
    row_max = lax.optimization_barrier(jnp.max(jnp.where(allowed, scores, masked_score), axis=-1, keepdims=True))
    row_total = lax.optimization_barrier(jnp.sum(jnp.where(allowed, jnp.exp(scores - row_max), 0.0), axis=-1, keepdims=True))
    log_total = row_max + jnp.log(row_total)
    prob_low = low(jnp.where(allowed, jnp.exp(scores - log_total), 0.0))
    attended = jnp.einsum('kgqt,tkd->qkgd', prob_low, value_seq, precision=lax.Precision.HIGHEST)
    return attended.reshape(row_count, H, HD)

def reference(tokens, prefix_len, routes, norm1_gain, w_query, w_key, w_value, w_output, norm2_gain, w_router, w_gate, w_up, w_down, cotangent):
    cosine_table, sine_table = rope_tables(jnp.arange(SEQ, dtype=jnp.int32), HD)
    query_block = min(512, SEQ)
    block_count = SEQ // query_block
    seq_rows = CAP * N_EXPERT

    def one_sequence(packed):
        query_seq, key_seq, value_seq, prefix_here = packed
        blocks = query_seq.reshape(block_count, query_block, H, HD)
        starts = jnp.arange(block_count, dtype=jnp.int32) * query_block

        def one_block(inner):
            return attend(inner[0], key_seq, value_seq, inner[1], prefix_here)
        return lax.map(jax.checkpoint(one_block), (blocks, starts)).reshape(SEQ, H, HD)

    def forward(tokens_in, gain_one, query_w, key_w, value_w, output_w, gain_two, router_w, gate_w, up_w, down_w):
        normed1 = low(rms_norm(tokens_in, gain_one))
        query_pre = low_back(matmul_hi(normed1, query_w)).reshape(SEQS, SEQ, H, HD)
        key_pre = low_back(matmul_hi(normed1, key_w)).reshape(SEQS, SEQ, KV, HD)
        value = low(low_back(matmul_hi(normed1, value_w))).reshape(SEQS, SEQ, KV, HD)
        query_r = low(apply_rope(query_pre, cosine_table, sine_table))
        key_r = low(apply_rope(key_pre, cosine_table, sine_table))
        attended = lax.map(one_sequence, (query_r, key_r, value, prefix_len))
        attended = low(low_back(attended.reshape(TOKENS, H * HD)))
        hidden_state = tokens_in + low_back(matmul_hi(attended, output_w))
        normed2 = low(rms_norm(hidden_state, gain_two))
        logits = low_back(matmul_hi(normed2, router_w))
        gate_probs = jax.nn.softmax(jnp.take_along_axis(logits, routes, axis=1), axis=-1)

        def seq_moe(packed):
            rows_all, flat_experts, flat_gates = packed

            def expert_step(mixture, inner):
                expert_id, gate_e, up_e, down_e = inner
                matches = flat_experts == expert_id
                positions_hit, = jnp.nonzero(matches, size=seq_rows, fill_value=0)
                positions_hit = positions_hit.astype(jnp.int32)
                is_live = jnp.arange(seq_rows, dtype=jnp.int32) < jnp.sum(matches.astype(jnp.int32))
                owner_row = positions_hit // TOPK
                row_block = low_back(rows_all[owner_row])
                gate_pre = low_back(matmul_hi(row_block, gate_e))
                up_pre = low_back(matmul_hi(row_block, up_e))
                active = low(jax.nn.silu(gate_pre) * up_pre)
                produced = low(low_back(matmul_hi(active, down_e)))
                row_weight = jnp.where(is_live, flat_gates[positions_hit], 0.0)
                return (mixture.at[owner_row].add(produced * row_weight[:, None]), None)
            start_mix = jnp.zeros((SEQ, D), dtype=jnp.float32)
            mixture, _ = lax.scan(jax.checkpoint(expert_step), start_mix, (jnp.arange(EXPERTS, dtype=jnp.int32), gate_w, up_w, down_w))
            return mixture
        mixture = lax.map(jax.checkpoint(seq_moe), (normed2.reshape(SEQS, SEQ, D), routes.reshape(SEQS, SEQ * TOPK), gate_probs.reshape(SEQS, SEQ * TOPK)))
        return hidden_state + mixture.reshape(TOKENS, D)
    inputs_f = (tokens.astype(jnp.float32), norm1_gain.astype(jnp.float32), w_query.astype(jnp.float32), w_key.astype(jnp.float32), w_value.astype(jnp.float32), w_output.astype(jnp.float32), norm2_gain.astype(jnp.float32), w_router.astype(jnp.float32), w_gate.astype(jnp.float32), w_up.astype(jnp.float32), w_down.astype(jnp.float32))
    block_out, pullback = jax.vjp(forward, *inputs_f)
    gradients = pullback(cotangent.astype(jnp.float32))
    return (block_out.astype(jnp.bfloat16), gradients[0].astype(jnp.bfloat16), gradients[1], gradients[2], gradients[3], gradients[4], gradients[5], gradients[6], gradients[7], gradients[8], gradients[9], gradients[10])
```

```python
import math

import jax
import jax.numpy as jnp
from jax import lax
from jax.sharding import PartitionSpec as P

H = 16
KV = 8
HD = 64


norm_eps = 1e-05
masked_score = -1e30


def rope_tables(positions, head_width):
    half_width = head_width // 2
    frequency = jnp.exp(
        jnp.arange(half_width, dtype=jnp.float32) * (-2.0 * math.log(10000.0) / head_width)
    )
    angles = positions.astype(jnp.float32)[:, None] * frequency[None, :]
    return (
        jnp.concatenate([jnp.cos(angles), jnp.cos(angles)], 1),
        jnp.concatenate([jnp.sin(angles), jnp.sin(angles)], 1),
    )


def rotate(source):
    half_width = source.shape[-1] // 2
    return jnp.concatenate([-source[..., half_width:], source[..., :half_width]], -1)


def rotate_back(source):
    half_width = source.shape[-1] // 2
    return jnp.concatenate([source[..., half_width:], -source[..., :half_width]], -1)


def apply_rope(source, cosine_table, sine_table):
    return source * cosine_table[:, None, :] + rotate(source) * sine_table[:, None, :]


def undo_rope(upstream, cosine_table, sine_table):
    return upstream * cosine_table[:, None, :] + rotate_back(upstream * sine_table[:, None, :])


def norm_forward(source, gain_vec):
    inverse = lax.rsqrt(jnp.mean(source * source, axis=-1, keepdims=True) + norm_eps)
    return (source * inverse * gain_vec, inverse)


def norm_backward(source, inverse, gain_vec, upstream):
    weighted = upstream * gain_vec
    cubed = inverse * inverse * inverse
    back = inverse * weighted - source * cubed * jnp.mean(weighted * source, axis=-1, keepdims=True)
    return (back, jnp.sum(upstream * source * inverse, axis=0))


def dot(left, right, left_dim=1, right_dim=0):
    return lax.dot_general(
        left, right, (((left_dim,), (right_dim,)), ((), ())), preferred_element_type=jnp.float32
    )


def shards(
    tokens,
    prefix_len,
    routes,
    norm1_gain,
    w_query,
    w_key,
    w_value,
    w_output,
    norm2_gain,
    w_router,
    w_gate,
    w_up,
    w_down,
    cotangent,
):
    tok_rows, model_width = tokens.shape
    groups = lax.axis_size("expert")
    copies = lax.axis_size("dp")
    me = lax.axis_index("expert")
    half = lax.axis_index("dp") % 2
    exp_dev, _, hidden_units = w_gate.shape
    half_units = hidden_units // 2
    experts = exp_dev * groups
    seq_len = tok_rows * groups
    group_size = H // KV
    score_scale = 1.0 / math.sqrt(HD)
    low = jnp.bfloat16

    def send(block, pair_flip, flip):
        return lax.ppermute(
            block,
            ("dp", "expert"),
            [
                (i * groups + j, (i ^ pair_flip) * groups + (j ^ flip))
                for i in range(copies)
                for j in range(groups)
            ],
        )

    def gather(block, pairs):
        even = [
            block if (s, r) == (0, 0) else send(block, s, r)
            for s in range(pairs)
            for r in range(0, groups, 2)
        ]
        out = []
        for b in even:
            out += [b, send(b, 0, 1)]
        return jnp.concatenate(out, axis=0)

    def scatter(blocks, pack, unpack, pairs):
        got = unpack(send(pack(blocks[:, 1]), 0, 1))
        mine = blocks[:, 0] + got
        out = mine[0]
        n = 0
        for s in range(pairs):
            for r in range(0, groups, 2):
                if n:
                    out = out + unpack(send(pack(mine[n]), s, r))
                n += 1
        return out

    def plain_pack(block):
        return block.astype(low)

    def plain_unpack(block):
        return block.astype(jnp.float32)

    tokens_f = tokens.astype(jnp.float32)
    normed_one, inverse_one = norm_forward(tokens_f, norm1_gain)
    normed1 = normed_one.astype(low)
    normed1_seq = gather(normed1, 1)

    routed = jnp.any(
        routes[:, :, None] == jnp.arange(experts, dtype=jnp.int32)[None, None, :], axis=1
    )
    lanes = 128
    cot_mask = jnp.concatenate(
        [cotangent, jnp.pad(routed.astype(low), ((0, 0), (0, lanes - experts)))], axis=1
    )
    cot_all = gather(cot_mask, 2)
    g_all = cot_all[:, :model_width]
    routed_all = cot_all[:, model_width : model_width + experts] > 0.5

    block_pos = jnp.arange(tok_rows, dtype=jnp.int32)
    positions = me * tok_rows + block_pos
    key_pos = jnp.concatenate([(me ^ r) * tok_rows + block_pos for r in range(groups)])
    key_cos, key_sin = rope_tables(key_pos, HD)
    cosine_table, sine_table = key_cos[:tok_rows], key_sin[:tok_rows]
    query_pre = dot(normed1, w_query).reshape(tok_rows, H, HD)
    key_pre = dot(normed1_seq, w_key).reshape(seq_len, KV, HD)
    values = dot(normed1_seq, w_value).astype(low)
    query_low = apply_rope(query_pre, cosine_table, sine_table).astype(low)
    keys = apply_rope(key_pre, key_cos, key_sin).astype(low).reshape(seq_len, KV * HD)
    allowed = (key_pos[None, :] <= positions[:, None]) | (key_pos[None, :] < prefix_len[0])

    def head_scores(kv_head):
        query_head = query_low[:, kv_head * group_size : (kv_head + 1) * group_size, :]
        key_head = keys[:, kv_head * HD : (kv_head + 1) * HD]
        return (
            jnp.einsum("qgd,td->gqt", query_head, key_head, preferred_element_type=jnp.float32)
            * score_scale
        )

    head_outputs = []
    log_totals = []
    for kv_head in range(KV):
        scores = head_scores(kv_head)
        row_max = jnp.max(jnp.where(allowed, scores, masked_score), axis=-1, keepdims=True)
        row_total = jnp.sum(
            jnp.where(allowed, jnp.exp(scores - row_max), 0.0), axis=-1, keepdims=True
        )
        log_total = row_max + jnp.log(row_total)
        prob_low = jnp.where(allowed, jnp.exp(scores - log_total), 0.0).astype(low)
        value_head = values[:, kv_head * HD : (kv_head + 1) * HD]
        head_outputs.append(
            jnp.einsum("gqt,td->qgd", prob_low, value_head, preferred_element_type=jnp.float32)
        )
        log_totals.append(log_total)
    attended = jnp.concatenate(head_outputs, axis=1).reshape(tok_rows, H * HD).astype(low)
    hidden_state = tokens_f + dot(attended, w_output)
    normed_two, inverse_two = norm_forward(hidden_state, norm2_gain)
    normed2 = normed_two.astype(low)

    n2_all = gather(normed2, 2)
    attended_seq = gather(attended, 1)
    logits = jnp.where(routed_all, dot(n2_all, w_router), masked_score)
    exps = jnp.where(
        routed_all, jnp.exp(logits - jnp.max(logits, axis=-1, keepdims=True)), 0.0
    )
    gate_all = exps / jnp.sum(exps, axis=-1, keepdims=True)
    gate_mine = lax.dynamic_slice_in_dim(gate_all, me * exp_dev, exp_dev, 1)
    wg = lax.dynamic_slice_in_dim(w_gate, half * half_units, half_units, 2)
    wu = lax.dynamic_slice_in_dim(w_up, half * half_units, half_units, 2)
    wd = lax.dynamic_slice_in_dim(w_down, half * half_units, half_units, 1)
    mixture = grad_rows = None
    gate_grads = []
    reduced = []
    chunk = exp_dev // 2
    outer = copies // 2
    outer_groups = [[2 * o + p for o in range(outer)] for p in range(2)]
    grads = []
    for e in range(exp_dev):
        gate_pre = dot(n2_all, wg[e])
        up_pre = dot(n2_all, wu[e])
        back = dot(g_all, wd[e], 1, 1)
        sig = jax.nn.sigmoid(gate_pre)
        silu = gate_pre * sig
        act = silu * up_pre
        weight = gate_mine[:, e : e + 1]
        gate_grads.append(jnp.sum(act * back, axis=1, keepdims=True))
        grad_active = weight * back
        scaled = (weight * act).astype(low)
        grad_gate = (grad_active * up_pre * sig * (1.0 + gate_pre * (1.0 - sig))).astype(low)
        grad_up = (grad_active * silu).astype(low)
        mix = dot(scaled, wd[e])
        rows = dot(grad_gate, wg[e], 1, 1) + dot(grad_up, wu[e], 1, 1)
        mixture = mix if mixture is None else mixture + mix
        grad_rows = rows if grad_rows is None else grad_rows + rows
        grads += [
            dot(n2_all, grad_gate, 0, 0).astype(low),
            dot(n2_all, grad_up, 0, 0).astype(low),
            dot(g_all, scaled, 0, 0).astype(low),
        ]
        if (e + 1) % chunk == 0:
            reduced.append(
                lax.psum_scatter(
                    jnp.concatenate(grads, axis=1),
                    "dp",
                    scatter_dimension=0,
                    axis_index_groups=outer_groups,
                    tiled=True,
                )
            )
            grads = []

    gg = lax.dynamic_update_slice(
        jnp.zeros((2 * seq_len, experts), jnp.float32),
        jnp.concatenate(gate_grads, axis=1),
        (0, me * exp_dev),
    )

    def split_pack(block):
        rows, extra = block[..., :model_width], block[..., model_width:]
        high = lax.reduce_precision(extra, 8, 7)
        fill = jnp.zeros(extra.shape[:-1] + (lanes - 2 * experts,), low)
        return jnp.concatenate(
            [rows.astype(low), high.astype(low), (extra - high).astype(low), fill], axis=-1
        )

    def split_unpack(block):
        block = block.astype(jnp.float32)
        a, b = model_width, model_width + experts
        return jnp.concatenate(
            [block[..., :a], block[..., a:b] + block[..., b : b + experts]], axis=-1
        )

    summed = scatter(
        jnp.concatenate([grad_rows, gg], axis=1).reshape(
            groups, 2, tok_rows, model_width + experts
        ),
        split_pack,
        split_unpack,
        2,
    )
    grad_gate_probs = summed[:, model_width:]
    mix_own = scatter(
        mixture.reshape(groups, 2, tok_rows, model_width), plain_pack, plain_unpack, 2
    )
    block_out = (hidden_state + mix_own).astype(low)

    gate_probs = gate_all[:tok_rows]
    g_out = cotangent.astype(jnp.float32)
    grad_logits = (
        gate_probs
        * (grad_gate_probs - jnp.sum(gate_probs * grad_gate_probs, axis=-1, keepdims=True))
    ).astype(low)
    grad_router = dot(grad_logits, normed2, 0, 0)
    grad_normed2 = summed[:, :model_width] + dot(grad_logits, w_router, 1, 1)
    norm_back_two, grad_norm2 = norm_backward(hidden_state, inverse_two, norm2_gain, grad_normed2)
    grad_hidden = g_out + norm_back_two
    grad_branch = grad_hidden.astype(low)
    branch_seq = gather(grad_branch, 1)
    grad_attended = dot(grad_branch, w_output, 1, 1).astype(low)

    query_parts = []
    key_parts = []
    value_parts = []
    for kv_head in range(KV):
        scores = head_scores(kv_head)
        prob_full = jnp.where(allowed, jnp.exp(scores - log_totals[kv_head]), 0.0)
        prob_low = prob_full.astype(low)
        grad_head = grad_attended[
            :, kv_head * group_size * HD : (kv_head + 1) * group_size * HD
        ].reshape(tok_rows, group_size, HD)
        value_head = values[:, kv_head * HD : (kv_head + 1) * HD]
        key_head = keys[:, kv_head * HD : (kv_head + 1) * HD]
        query_head = query_low[:, kv_head * group_size : (kv_head + 1) * group_size, :]
        grad_prob = jnp.einsum(
            "qgd,td->gqt", grad_head, value_head, preferred_element_type=jnp.float32
        )
        delta = jnp.sum(prob_full * grad_prob, axis=-1, keepdims=True)
        grad_scores = (prob_full * (grad_prob - delta)).astype(low)
        query_parts.append(
            jnp.einsum("gqt,td->qgd", grad_scores, key_head, preferred_element_type=jnp.float32)
            * score_scale
        )
        key_parts.append(
            jnp.einsum("gqt,qgd->td", grad_scores, query_head, preferred_element_type=jnp.float32)
            * score_scale
        )
        value_parts.append(
            jnp.einsum("gqt,qgd->td", prob_low, grad_head, preferred_element_type=jnp.float32)
        )
    grad_query_r = jnp.concatenate(query_parts, axis=1)
    terms = jnp.concatenate(key_parts + value_parts, axis=1)
    own_terms = scatter(
        terms.reshape(groups // 2, 2, tok_rows, 2 * KV * HD), plain_pack, plain_unpack, 1
    )
    grad_key_r, grad_value = own_terms[:, : KV * HD], own_terms[:, KV * HD :]
    grad_query = (
        undo_rope(grad_query_r, cosine_table, sine_table).reshape(tok_rows, H * HD).astype(low)
    )
    grad_key = (
        undo_rope(grad_key_r.reshape(tok_rows, KV, HD), cosine_table, sine_table)
        .reshape(tok_rows, KV * HD)
        .astype(low)
    )
    grad_value_low = grad_value.astype(low)
    query_seq = gather(grad_query, 1)
    kv_seq = gather(jnp.concatenate([grad_key, grad_value_low], axis=1), 1)
    grad_normed1 = (
        dot(grad_query, w_query, 1, 1)
        + dot(grad_key, w_key, 1, 1)
        + dot(grad_value_low, w_value, 1, 1)
    )
    norm_back_one, grad_norm1 = norm_backward(tokens_f, inverse_one, norm1_gain, grad_normed1)
    grad_tokens = (grad_hidden + norm_back_one).astype(low)

    own_rows = model_width // (copies * groups)
    picked = jnp.arange(copies * own_rows, dtype=jnp.int32)
    picked = (picked // own_rows) * (own_rows * groups) + me * own_rows + picked % own_rows
    select = (picked[:, None] == jnp.arange(model_width, dtype=jnp.int32)[None, :]).astype(low)
    normed1_t = dot(select, normed1_seq, 1, 1).astype(low)
    attended_t = dot(select, attended_seq, 1, 1).astype(low)
    small = jnp.concatenate([grad_router, grad_norm1[None], grad_norm2[None]], axis=0)
    flip = 1
    while flip < groups:
        small = small + send(small, 0, flip)
        flip *= 2
    small = lax.dynamic_index_in_dim(
        small.reshape(experts + 2, copies, groups, own_rows), me, 2, keepdims=False
    )
    small = jnp.pad(
        small.reshape(experts + 2, copies * own_rows).T, ((0, 0), (0, lanes - experts - 2))
    )
    dense = jnp.concatenate(
        [
            dot(normed1_t, query_seq).astype(low),
            dot(normed1_t, kv_seq).astype(low),
            dot(attended_t, branch_seq).astype(low),
            small.astype(low),
        ],
        axis=1,
    )
    dense = lax.psum_scatter(dense, "dp", scatter_dimension=0, tiled=True).astype(jnp.float32)
    q_cols, k_cols = H * HD, KV * HD
    o_start = q_cols + 2 * k_cols
    s_start = o_start + model_width

    expert_grads = jnp.concatenate(reduced, axis=1)
    shard_rows = model_width // copies
    keep = lax.dynamic_slice_in_dim(expert_grads, half * shard_rows, shard_rows, 0)
    give = lax.dynamic_slice_in_dim(expert_grads, (1 - half) * shard_rows, shard_rows, 0)
    got = send(give, 1, 0)
    first = jnp.where(half == 0, keep, got).reshape(shard_rows, exp_dev, 3, half_units)
    second = jnp.where(half == 0, got, keep).reshape(shard_rows, exp_dev, 3, half_units)
    full = jnp.concatenate([first, second], axis=3).astype(jnp.float32)
    grad_gate_w = full[:, :, 0].transpose(1, 0, 2)
    grad_up_w = full[:, :, 1].transpose(1, 0, 2)
    grad_down_w = full[:, :, 2].transpose(1, 2, 0)
    return (
        block_out,
        grad_tokens,
        dense[:, s_start + experts],
        dense[:, :q_cols],
        dense[:, q_cols : q_cols + k_cols],
        dense[:, q_cols + k_cols : o_start],
        dense[:, o_start:s_start],
        dense[:, s_start + experts + 1],
        dense[:, s_start : s_start + experts],
        grad_gate_w,
        grad_up_w,
        grad_down_w,
    )


def solution(mesh):
    return jax.shard_map(
        shards,
        mesh=mesh,
        in_specs=(
            P(("dp", "expert"), None),
            P("dp"),
            P(("dp", "expert"), None),
            P(),
            P(),
            P(),
            P(),
            P(),
            P(),
            P(),
            P("expert", None, None),
            P("expert", None, None),
            P("expert", None, None),
            P(("dp", "expert"), None),
        ),
        out_specs=(
            P(("dp", "expert"), None),
            P(("dp", "expert"), None),
            P(("dp", "expert")),
            P(("dp", "expert"), None),
            P(("dp", "expert"), None),
            P(("dp", "expert"), None),
            P(("dp", "expert"), None),
            P(("dp", "expert")),
            P(("dp", "expert"), None),
            P("expert", "dp", None),
            P("expert", "dp", None),
            P("expert", None, "dp"),
        ),
        check_vma=False,
    )
```

```python
import math

import jax
import jax.numpy as jnp
from jax import lax
from jax.experimental import pallas as pl
from jax.experimental.pallas import tpu as pltpu
from jax.sharding import PartitionSpec as P

H = 16
KV = 8
HD = 64


norm_eps = 1e-05
masked_score = -1e30


def rope_tables(me, tok_rows, groups):
    row = lax.broadcasted_iota(jnp.int32, (groups * tok_rows, LANES), 0)
    lane = lax.broadcasted_iota(jnp.int32, (groups * tok_rows, LANES), 1)
    position = ((row // tok_rows) ^ me) * tok_rows + row % tok_rows
    frequency = jnp.exp((lane % (HD // 2)).astype(jnp.float32) * (-2.0 * math.log(10000.0) / HD))
    angles = position.astype(jnp.float32) * frequency
    sine = jnp.sin(angles)
    return jnp.cos(angles), jnp.where(lane % HD < HD // 2, -sine, sine)


LANES = 128


def norm_forward(source, gain_vec):
    inverse = lax.rsqrt(jnp.mean(source * source, axis=-1, keepdims=True) + norm_eps)
    return (source * inverse * gain_vec, inverse)


def norm_backward(source, inverse, gain_vec, upstream):
    weighted = upstream * gain_vec
    cubed = inverse * inverse * inverse
    back = inverse * weighted - source * cubed * jnp.mean(weighted * source, axis=-1, keepdims=True)
    return (back, jnp.sum(upstream * source * inverse, axis=0, keepdims=True))


def dot(left, right, left_dim=1, right_dim=0):
    return lax.dot_general(
        left, right, (((left_dim,), (right_dim,)), ((), ())), preferred_element_type=jnp.float32
    )


def lane_of(shape):
    return lax.broadcasted_iota(jnp.int32, shape, 1)


def swap_halves(source):
    lane = lane_of(source.shape)
    return jnp.where(
        lane % HD < HD // 2,
        pltpu.roll(source, LANES - HD // 2, 1),
        pltpu.roll(source, HD // 2, 1),
    )


def rope(source, cosine_table, sine_table):
    return source * cosine_table + swap_halves(source) * sine_table


def unrope(upstream, cosine_table, sine_table):
    return upstream * cosine_table - swap_halves(upstream) * sine_table


def twice(pair):
    lane = lane_of(pair.shape)
    other = pltpu.roll(pair, HD, 1)
    return (jnp.where(lane < HD, pair, other), jnp.where(lane < HD, other, pair))


def stack_heads(pair):
    lane = lane_of(pair.shape)
    zero = jnp.zeros_like(pair)
    return jnp.concatenate(
        [jnp.where(lane < HD, pair, zero), jnp.where(lane < HD, zero, pair)], axis=0
    )


def join_heads(stacked):
    rows = stacked.shape[0] // 2
    lane = lane_of((rows, LANES))
    return jnp.where(lane < HD, stacked[:rows], stacked[rows:])


def allowed_mask(info_ref, seq_len, rows):
    me, prefix = info_ref[0], info_ref[1]
    key = lax.broadcasted_iota(jnp.int32, (seq_len, 2 * rows), 0)
    query = lax.broadcasted_iota(jnp.int32, (seq_len, 2 * rows), 1) % rows + me * rows
    key_pos = ((key // rows) ^ me) * rows + key % rows
    return (key_pos <= query) | (key_pos < prefix)


def forward_kernel(
    info_ref, tokens_ref, query_ref, wk_ref, wv_ref, wo_ref, gain_ref, cos_ref, sin_ref, *rest
):
    blocks, outs = rest[:-7], rest[-7:]
    q_ref, k_ref, v_ref, lse_ref, att_ref, hid_ref, n2_ref = outs
    rows = tokens_ref.shape[0]
    seq_len = rows * len(blocks)
    normed = jnp.concatenate([b[...] for b in blocks], axis=0)
    cosine, sine = cos_ref[...], sin_ref[...]
    keys = dot(normed, wk_ref[...])
    values = dot(normed, wv_ref[...])
    for c in range(KV // 2):
        cols = slice(c * LANES, (c + 1) * LANES)
        first, second = twice(rope(keys[:, cols], cosine, sine))
        k_ref[2 * c] = first.astype(jnp.bfloat16)
        k_ref[2 * c + 1] = second.astype(jnp.bfloat16)
        first, second = twice(values[:, cols])
        v_ref[2 * c] = first.astype(jnp.bfloat16)
        v_ref[2 * c + 1] = second.astype(jnp.bfloat16)
    allowed = allowed_mask(info_ref, seq_len, rows)
    for h in range(KV):
        cols = slice(h * LANES, (h + 1) * LANES)
        query = rope(query_ref[:, cols], cosine[:rows], sine[:rows]) * (1.0 / math.sqrt(HD))
        q_ref[:, cols] = query.astype(jnp.bfloat16)
        stacked = stack_heads(query).astype(jnp.bfloat16)
        scores = jnp.where(allowed, dot(k_ref[h], stacked, 1, 1), masked_score)
        row_max = jnp.max(scores, axis=0, keepdims=True)
        exps = jnp.exp(scores - row_max)
        total = jnp.sum(exps, axis=0, keepdims=True)
        lse_ref[h : h + 1, :] = row_max + jnp.log(total)
        prob = (exps * (1.0 / total)).astype(jnp.bfloat16)
        att_ref[:, cols] = join_heads(dot(prob, v_ref[h], 0, 0)).astype(jnp.bfloat16)
    hidden = tokens_ref[...].astype(jnp.float32) + dot(att_ref[...], wo_ref[...])
    hid_ref[...] = hidden
    n2_ref[...] = norm_forward(hidden, gain_ref[...])[0].astype(jnp.bfloat16)


def start_copies(pairs, sems):
    copies = [pltpu.make_async_copy(src, dst, sems.at[n]) for n, (src, dst) in enumerate(pairs)]
    for c in copies:
        c.start()
    return copies


def wait_all(copies):
    for c in copies:
        c.wait()


def own_half(info_ref, fh):
    return pl.ds(pl.multiple_of(info_ref[2] * fh, fh), fh)


def gate_up_parts(info_ref, wg_ref, wu_ref, w_ref, first, count):
    fh = wg_ref.shape[2] // 2
    mine = own_half(info_ref, fh)
    pairs = []
    for i in range(count):
        pairs.append((wg_ref.at[first + i, :, mine], w_ref.at[:, pl.ds(2 * i * fh, fh)]))
        pairs.append((wu_ref.at[first + i, :, mine], w_ref.at[:, pl.ds((2 * i + 1) * fh, fh)]))
    return pairs


def down_parts(info_ref, wd_ref, down_ref, first, count):
    fh = wd_ref.shape[1] // 2
    mine = own_half(info_ref, fh)
    return [
        (wd_ref.at[first + i, mine, :], down_ref.at[pl.ds(i * fh, fh), :]) for i in range(count)
    ]


def row_parts(blocks, into, cols):
    rows = blocks[0].shape[0]
    return [(b.at[:, cols], into.at[pl.ds(n * rows, rows), :]) for n, b in enumerate(blocks)]


def hidden_units(
    spot, weights, down, n2_ref, g_ref, probs_ref, gu_ref, scaled_ref, extra, two, one, tiles
):
    total_rows = n2_ref.shape[0]
    step = total_rows // tiles
    fh = (two.stop - two.start) // 2
    for t in range(tiles):
        part = slice(t * step, (t + 1) * step)
        pre = dot(n2_ref[part, :], weights)
        gate_pre, up_pre = pre[:, :fh], pre[:, fh:]
        back = dot(g_ref[part, :], down, 1, 1)
        sig = 0.5 * jnp.tanh(0.5 * gate_pre) + 0.5
        silu = gate_pre * sig
        act = silu * up_pre
        here = lane_of((step, LANES)) == spot
        weight = jnp.sum(jnp.where(here, probs_ref[part, :], 0.0), axis=1, keepdims=True)
        extra(part, jnp.where(here, jnp.sum(act * back, axis=1, keepdims=True), 0.0))
        grad_active = weight * back
        scaled_ref[part, one] = (weight * act).astype(jnp.bfloat16)
        gu_ref[part, two.start : two.start + fh] = (
            grad_active * up_pre * (sig + silu * (1.0 - sig))
        ).astype(jnp.bfloat16)
        gu_ref[part, two.start + fh : two.stop] = (grad_active * silu).astype(jnp.bfloat16)


def widen(router_ref, wide_ref):
    wide_ref[...] = jnp.zeros_like(wide_ref)
    wide_ref[:, : router_ref.shape[1]] = router_ref[...]


def experts_kernel(info_ref, router_ref, wg_ref, wu_ref, wd_ref, *rest, n_blocks, tiles):
    n2_blocks, cot_blocks = rest[:n_blocks], rest[n_blocks : 2 * n_blocks]
    sums_out, gu_out, scaled_out, extra_ref, probs_ref = rest[2 * n_blocks : 2 * n_blocks + 5]
    n2_ref, g_ref, routed_ref, w_ref, down_ref, gu_ref, scaled_ref, sums_ref, router_wide = rest[
        2 * n_blocks + 5 : 2 * n_blocks + 14
    ]
    n2_sems, routed_sems, g_sems, w_sems, down_sems, out_sems = rest[2 * n_blocks + 14 :]
    exp_dev, width, units = wg_ref.shape
    fh = units // 2
    n2_copies = start_copies(row_parts(n2_blocks, n2_ref, pl.ds(0, width)), n2_sems)
    routed_copies = start_copies(row_parts(cot_blocks, routed_ref, pl.ds(width, LANES)), routed_sems)
    g_copies = start_copies(row_parts(cot_blocks, g_ref, pl.ds(0, width)), g_sems)
    w_copies = start_copies(gate_up_parts(info_ref, wg_ref, wu_ref, w_ref, 0, exp_dev), w_sems)
    down_copies = start_copies(down_parts(info_ref, wd_ref, down_ref, 0, exp_dev), down_sems)
    widen(router_ref, router_wide)
    wait_all(n2_copies)
    wait_all(routed_copies)
    routed = routed_ref[...].astype(jnp.float32) > 0.5
    logits = jnp.where(routed, dot(n2_ref[...], router_wide[...]), masked_score)
    exps = jnp.where(routed, jnp.exp(logits - jnp.max(logits, axis=-1, keepdims=True)), 0.0)
    probs_ref[...] = exps / jnp.sum(exps, axis=-1, keepdims=True)
    wait_all(g_copies)
    for e in range(exp_dev):

        def extra(part, found, e=e):
            extra_ref[part, :] = found if e == 0 else extra_ref[part, :] + found

        two, one = slice(2 * e * fh, 2 * (e + 1) * fh), slice(e * fh, (e + 1) * fh)
        wait_all(w_copies[2 * e : 2 * e + 2])
        wait_all(down_copies[e : e + 1])
        hidden_units(
            info_ref[0] * exp_dev + e, w_ref[:, two], down_ref[one, :], n2_ref, g_ref, probs_ref,
            gu_ref, scaled_ref, extra, two, one, tiles,
        )
    out_copies = start_copies([(gu_ref, gu_out), (scaled_ref, scaled_out)], out_sems)
    pieces = [(n2_ref, gu_ref, t * exp_dev * fh, t * exp_dev * fh) for t in range(2)]
    pieces.append((g_ref, scaled_ref, 0, 2 * exp_dev * fh))
    for n, (left, right, start, at) in enumerate(pieces):
        cols = pl.ds(at, exp_dev * fh)
        sums_ref[:, cols] = dot(
            left[...], right[:, start : start + exp_dev * fh], 0, 0
        ).astype(jnp.bfloat16)
        out_copies += start_copies(
            [(sums_ref.at[:, cols], sums_out.at[:, cols])], out_sems.at[pl.ds(2 + n, 1)]
        )
    wait_all(out_copies)


def rows_kernel(
    info_ref, extra_ref, wg_ref, wu_ref, gu_in, odd_ref, even_ref, w_ref, gu_ref, w_sems, gu_sems,
    *, experts
):
    rows, width = odd_ref.shape[1], w_ref.shape[0]
    tiles = gu_sems.shape[0]
    step = gu_ref.shape[0] // tiles
    w_copies = start_copies(
        gate_up_parts(info_ref, wg_ref, wu_ref, w_ref, 0, wg_ref.shape[0]), w_sems
    )
    gu_copies = start_copies(
        [
            (gu_in.at[pl.ds(t * step, step), :], gu_ref.at[pl.ds(t * step, step), :])
            for t in range(tiles)
        ],
        gu_sems,
    )
    wait_all(w_copies)
    for t in range(tiles):
        gu_copies[t].wait()
        back_rows = dot(gu_ref[t * step : (t + 1) * step, :], w_ref[...], 1, 1)
        for n in range(t * step // rows, (t + 1) * step // rows):
            found = extra_ref[n * rows : (n + 1) * rows, :]
            high = found.astype(jnp.bfloat16).astype(jnp.float32)
            lower = (found - high).astype(jnp.bfloat16).astype(jnp.float32)
            out = odd_ref if n % 2 else even_ref
            at = n * rows - t * step
            out[n // 2, :, :width] = back_rows[at : at + rows].astype(out.dtype)
            out[n // 2, :, width:] = (high + pltpu.roll(lower, experts, 1)).astype(out.dtype)


def mixture_kernel(info_ref, wd_ref, scaled_ref, odd_ref, even_ref, down_ref, sems):
    rows = odd_ref.shape[1]
    wait_all(start_copies(down_parts(info_ref, wd_ref, down_ref, 0, wd_ref.shape[0]), sems))
    per = odd_ref.shape[0]
    for t in range(2):
        mix = dot(scaled_ref[t * per * rows : (t + 1) * per * rows, :], down_ref[...])
        for n in range(t * per, (t + 1) * per):
            out = odd_ref if n % 2 else even_ref
            at = (n - t * per) * rows
            out[n // 2] = mix[at : at + rows].astype(out.dtype)


def place_kernel(info_ref, sums_ref, arrived_ref, gate_ref, up_ref, down_ref):
    exp_dev, rows, units = gate_ref.shape
    fh = units // 2
    half = info_ref[2]
    kept = sums_ref[pl.ds(pl.multiple_of(half * rows, rows), rows), :]
    got = arrived_ref[...]
    first = jnp.where(half == 0, kept, got).astype(jnp.float32)
    second = jnp.where(half == 0, got, kept).astype(jnp.float32)
    for e in range(exp_dev):
        at = 2 * e * fh
        gate_ref[e, :, :fh] = first[:, at : at + fh]
        gate_ref[e, :, fh:] = second[:, at : at + fh]
        up_ref[e, :, :fh] = first[:, at + fh : at + 2 * fh]
        up_ref[e, :, fh:] = second[:, at + fh : at + 2 * fh]
        at = (2 * exp_dev + e) * fh
        down_ref[e, :fh, :] = first[:, at : at + fh].T
        down_ref[e, fh:, :] = second[:, at : at + fh].T


def small_rows(count):
    return -(-2 * count // 16) * 16


def put_small(ref, start, values):
    count = values.shape[0]
    high = values.astype(jnp.bfloat16).astype(jnp.float32)
    fill = jnp.zeros((small_rows(count) - 2 * count, values.shape[1]), jnp.float32)
    ref[start:] = jnp.concatenate([high, values - high, fill], axis=0).astype(jnp.bfloat16)


def backward_kernel(
    info_ref,
    own_ref,
    gate_ref,
    cot_ref,
    n2_ref,
    hid_ref,
    router_ref,
    gain_ref,
    wo_ref,
    q_ref,
    k_ref,
    v_ref,
    lse_ref,
    cos_ref,
    sin_ref,
    *rest,
    experts,
):
    arrived, outs = rest[:-6], rest[-6:]
    ghid_ref, branch_ref, dq_ref, odd_ref, even_ref, router_wide = outs
    widen(router_ref, router_wide)
    rows, width = hid_ref.shape
    seq_len = k_ref.shape[1]
    summed = own_ref[...]
    for a in arrived:
        summed = summed + a[...].astype(jnp.float32)
    extra = summed[:, width:]
    gate_grads = extra + pltpu.roll(extra, LANES - experts, 1)
    gate = gate_ref[...]
    grad_logits = (
        gate * (gate_grads - jnp.sum(gate * gate_grads, axis=-1, keepdims=True))
    ).astype(jnp.bfloat16)
    router_grad = dot(grad_logits, n2_ref[...], 0, 0)
    grad_normed = summed[:, :width] + dot(grad_logits, router_wide[...], 1, 1)
    hidden = hid_ref[...]
    inverse = lax.rsqrt(jnp.mean(hidden * hidden, axis=-1, keepdims=True) + norm_eps)
    back, norm_grad = norm_backward(hidden, inverse, gain_ref[...], grad_normed)
    grad_hidden = cot_ref[...].astype(jnp.float32) + back
    ghid_ref[...] = grad_hidden
    branch = grad_hidden.astype(jnp.bfloat16)
    branch_ref[:rows] = branch
    put_small(branch_ref, rows, jnp.concatenate([norm_grad, router_grad[:experts]], axis=0))
    grad_attended = dot(branch, wo_ref[...], 1, 1)
    allowed = allowed_mask(info_ref, seq_len, rows)
    cosine, sine = cos_ref[:rows, :], sin_ref[:rows, :]
    lane = lane_of((seq_len, LANES))
    kept = [None, None]
    for h in range(KV):
        cols = slice(h * LANES, (h + 1) * LANES)
        stacked = stack_heads(q_ref[:, cols])
        grad_stacked = stack_heads(grad_attended[:, cols]).astype(jnp.bfloat16)
        keys = k_ref[h]
        scores = jnp.where(allowed, dot(keys, stacked, 1, 1), masked_score)
        prob = jnp.exp(scores - lse_ref[h : h + 1, :])
        grad_prob = dot(v_ref[h], grad_stacked, 1, 1)
        delta = jnp.sum(prob * grad_prob, axis=0, keepdims=True)
        grad_scores = (prob * (grad_prob - delta)).astype(jnp.bfloat16)
        dq = join_heads(dot(grad_scores, keys, 0, 0)) * (1.0 / math.sqrt(HD))
        dq_ref[:, cols] = unrope(dq, cosine, sine).astype(jnp.bfloat16)
        parts = (dot(grad_scores, stacked), dot(prob.astype(jnp.bfloat16), grad_stacked))
        for n in range(2):
            both = parts[n] + pltpu.roll(parts[n], HD, 1)
            if h % 2 == 0:
                kept[n] = both
                continue
            pair = jnp.where(lane < HD, kept[n], both)
            start = (n * KV // 2 + h // 2) * LANES
            for r in range(seq_len // rows):
                block = pair[r * rows : (r + 1) * rows]
                if r % 2:
                    odd_ref[r // 2, :, start : start + LANES] = block.astype(jnp.bfloat16)
                else:
                    even_ref[r // 2, :, start : start + LANES] = block


def tokens_kernel(
    own_ref, arrived_ref, dq_ref, wq_ref, wk_ref, wv_ref, tokens_ref, gain_ref, ghid_ref,
    cos_ref, sin_ref, kv_ref, out_ref
):
    rows = tokens_ref.shape[0]
    summed = own_ref[...]
    for n in range(arrived_ref.shape[0]):
        summed = summed + arrived_ref[n].astype(jnp.float32)
    k_cols = KV * HD
    for c in range(k_cols // LANES):
        cols = slice(c * LANES, (c + 1) * LANES)
        kv_ref[:rows, cols] = unrope(summed[:, cols], cos_ref[:rows, :], sin_ref[:rows, :]).astype(
            jnp.bfloat16
        )
    kv_ref[:rows, k_cols:] = summed[:, k_cols:].astype(jnp.bfloat16)
    grad_normed = (
        dot(dq_ref[...], wq_ref[...], 1, 1)
        + dot(kv_ref[:rows, :k_cols], wk_ref[...], 1, 1)
        + dot(kv_ref[:rows, k_cols:], wv_ref[...], 1, 1)
    )
    source = tokens_ref[...].astype(jnp.float32)
    inverse = lax.rsqrt(jnp.mean(source * source, axis=-1, keepdims=True) + norm_eps)
    back, norm_grad = norm_backward(source, inverse, gain_ref[...], grad_normed)
    put_small(kv_ref, rows, norm_grad)
    out_ref[...] = (ghid_ref[...] + back).astype(jnp.bfloat16)


def call(kernel, out_shape, n_in, name, smem=True, hbm=(), hbm_out=(), scratch=()):
    specs = [pl.BlockSpec(memory_space=pltpu.VMEM)] * n_in
    if smem:
        specs[0] = pl.BlockSpec(memory_space=pltpu.SMEM)
    for n in hbm:
        specs[n] = pl.BlockSpec(memory_space=pl.ANY)
    outs = [
        pl.BlockSpec(memory_space=pl.ANY if n in hbm_out else pltpu.VMEM)
        for n in range(len(out_shape))
    ]
    return pl.pallas_call(
        kernel,
        out_shape=out_shape,
        in_specs=specs,
        out_specs=outs,
        scratch_shapes=list(scratch),
        compiler_params=pltpu.CompilerParams(vmem_limit_bytes=58 * 1024 * 1024),
        name=name,
    )


def shape(*dims, dtype=jnp.bfloat16):
    return jax.ShapeDtypeStruct(dims, dtype)


def shards(
    tokens,
    prefix_len,
    routes,
    norm1_gain,
    w_query,
    w_key,
    w_value,
    w_output,
    norm2_gain,
    w_router,
    w_gate,
    w_up,
    w_down,
    cotangent,
):
    tok_rows, model_width = tokens.shape
    groups = lax.axis_size("expert")
    copies = lax.axis_size("dp")
    me = lax.axis_index("expert")
    half = lax.axis_index("dp") % 2
    exp_dev, _, hidden_units = w_gate.shape
    half_units = hidden_units // 2
    experts = exp_dev * groups
    f32 = jnp.float32
    seq_len = tok_rows * groups
    low = jnp.bfloat16

    def send(block, pair_flip, flip):
        return lax.ppermute(
            block,
            ("dp", "expert"),
            [
                (i * groups + j, (i ^ pair_flip) * groups + (j ^ flip))
                for i in range(copies)
                for j in range(groups)
            ],
        )

    def gather_even(block, pairs):
        return [
            block if (s, r) == (0, 0) else send(block, s, r)
            for s in range(pairs)
            for r in range(0, groups, 2)
        ]

    def gather_odd(even):
        out = []
        for b in even:
            out += [b, send(b, 0, 1)]
        return out

    def gather(block, pairs):
        return gather_odd(gather_even(block, pairs))

    def core_sum(odd, even):
        return even + send(odd, 0, 1).astype(jnp.float32)

    def swap(mine, pairs):
        mine = mine.astype(low)
        spots = [(s, r) for s in range(pairs) for r in range(0, groups, 2)]
        return [send(mine[n], *spots[n]) for n in range(1, len(spots))]

    tokens_f = tokens.astype(f32)
    normed1 = norm_forward(tokens_f, norm1_gain)[0].astype(low)
    normed1_blocks = gather(normed1, 1)
    routed = jnp.any(
        routes[:, :, None] == jnp.arange(experts, dtype=jnp.int32)[None, None, :], axis=1
    )
    cot_mask = jnp.concatenate(
        [cotangent, jnp.pad(routed.astype(low), ((0, 0), (0, LANES - experts)))], axis=1
    )
    cot_even = gather_even(cot_mask, 2)
    info = jnp.stack([me, prefix_len[0], half]).astype(jnp.int32)
    gain_one, gain_two = norm1_gain[None], norm2_gain[None]

    cosine, sine = rope_tables(me, tok_rows, groups)
    query_pre = dot(normed1, w_query)
    q_low, k_two, v_two, lse, attended, hidden_state, normed2 = call(
        forward_kernel,
        (
            shape(tok_rows, H * HD),
            shape(KV, seq_len, LANES),
            shape(KV, seq_len, LANES),
            shape(KV, 2 * tok_rows, dtype=f32),
            shape(tok_rows, H * HD),
            shape(tok_rows, model_width, dtype=f32),
            shape(tok_rows, model_width),
        ),
        9 + groups,
        "attention_forward",
    )(
        info, tokens, query_pre, w_key, w_value, w_output, gain_two, cosine, sine,
        *normed1_blocks,
    )

    normed2, *cot_even = lax.optimization_barrier((normed2, *cot_even))
    cot_blocks = gather_odd(cot_even)
    n2_blocks = gather(normed2, 2)
    attended_seq = jnp.concatenate(gather(attended, 1), axis=0)
    n_blocks = 2 * groups
    all_rows = n_blocks * tok_rows
    wide = model_width + LANES

    dma = pltpu.SemaphoreType.DMA
    units = half_units * exp_dev
    sums, grad_gu, scaled, extra, probs = call(
        lambda *refs: experts_kernel(*refs, n_blocks=n_blocks, tiles=4),
        (
            shape(model_width, 3 * units),
            shape(all_rows, 2 * units),
            shape(all_rows, units),
            shape(all_rows, LANES, dtype=f32),
            shape(all_rows, LANES, dtype=f32),
        ),
        5 + 2 * n_blocks,
        "experts",
        hbm=tuple(range(2, 5 + 2 * n_blocks)),
        hbm_out=(0, 1, 2),
        scratch=(
            pltpu.VMEM((all_rows, model_width), low),
            pltpu.VMEM((all_rows, model_width), low),
            pltpu.VMEM((all_rows, LANES), low),
            pltpu.VMEM((model_width, 2 * units), low),
            pltpu.VMEM((units, model_width), low),
            pltpu.VMEM((all_rows, 2 * units), low),
            pltpu.VMEM((all_rows, units), low),
            pltpu.VMEM((model_width, 3 * units), low),
            pltpu.VMEM((model_width, LANES), low),
            dma((n_blocks,)),
            dma((n_blocks,)),
            dma((n_blocks,)),
            dma((2 * exp_dev,)),
            dma((exp_dev,)),
            dma((5,)),
        ),
    )(info, w_router, w_gate, w_up, w_down, *n2_blocks, *cot_blocks)
    gate_probs = probs[:tok_rows]
    outer = copies // 2
    shard_rows = model_width // copies
    reduced = lax.psum_scatter(
        sums,
        "dp",
        scatter_dimension=0,
        axis_index_groups=[[2 * o + p for o in range(outer)] for p in range(2)],
        tiled=True,
    )

    odd, even = call(
        lambda *refs: rows_kernel(*refs, experts=experts),
        (shape(groups, tok_rows, wide), shape(groups, tok_rows, wide, dtype=f32)),
        5,
        "experts_rows",
        hbm=(2, 3, 4),
        scratch=(
            pltpu.VMEM((model_width, 2 * units), low),
            pltpu.VMEM((all_rows, 2 * units), low),
            dma((2 * exp_dev,)),
            dma((2,)),
        ),
    )(info, extra, w_gate, w_up, grad_gu)
    mine = core_sum(odd, even)
    arrived = swap(mine, 2)
    scaled, odd = lax.optimization_barrier((scaled, odd))
    mix_odd, mix_even = call(
        mixture_kernel,
        (shape(groups, tok_rows, model_width), shape(groups, tok_rows, model_width, dtype=f32)),
        3,
        "experts_mixture",
        hbm=(1,),
        scratch=(pltpu.VMEM((units, model_width), low), dma((exp_dev,))),
    )(info, w_down, scaled)
    mix_odd, mix_even, *arrived = lax.optimization_barrier((mix_odd, mix_even, *arrived))
    mix_mine = core_sum(mix_odd, mix_even)

    grad_hidden, grad_branch, grad_query, kv_odd, kv_even = call(
        lambda *refs: backward_kernel(*refs, experts=experts),
        (
            shape(tok_rows, model_width, dtype=f32),
            shape(tok_rows + small_rows(experts + 1), model_width),
            shape(tok_rows, H * HD),
            shape(groups // 2, tok_rows, 2 * KV * HD),
            shape(groups // 2, tok_rows, 2 * KV * HD, dtype=f32),
        ),
        15 + len(arrived),
        "attention_backward",
        scratch=(pltpu.VMEM((model_width, LANES), low),),
    )(
        info, mine[0], gate_probs, cotangent, normed2, hidden_state, w_router, gain_two, w_output,
        q_low, k_two, v_two, lse, cosine, sine, *arrived,
    )
    kv_mine = core_sum(kv_odd, kv_even)
    kv_arrived = jnp.stack(swap(kv_mine, 1))
    kv_arrived, mix_mine, grad_branch, query_later = lax.optimization_barrier(
        (kv_arrived, mix_mine, grad_branch, grad_query)
    )
    mixture = mix_mine[0]
    for a in swap(mix_mine, 2):
        mixture = mixture + a.astype(f32)
    block_out = (hidden_state + mixture).astype(low)

    def without_small(blocks, count):
        rows = jnp.concatenate([b[:tok_rows] for b in blocks], axis=0)
        total = sum(b[tok_rows : tok_rows + 2 * count].astype(f32) for b in blocks)
        return rows, total[:count] + total[count:]

    branch_seq, small_two = without_small(gather(grad_branch, 1), experts + 1)
    query_seq = jnp.concatenate(gather(query_later, 1), axis=0)
    grad_kv, grad_tokens = call(
        tokens_kernel,
        (
            shape(tok_rows + small_rows(1), 2 * KV * HD),
            shape(tok_rows, model_width),
        ),
        11,
        "tokens_backward",
        smem=False,
    )(
        kv_mine[0], kv_arrived, grad_query, w_query, w_key, w_value, tokens, gain_one,
        grad_hidden, cosine, sine,
    )
    kv_seq, small_one = without_small(gather(grad_kv, 1), 1)
    normed1_seq = jnp.concatenate(normed1_blocks, axis=0)

    my_dp = lax.axis_index("dp")
    own_rows = model_width // (copies * groups)
    picked = jnp.arange(copies * own_rows, dtype=jnp.int32)
    picked = ((picked // own_rows) ^ my_dp) * (own_rows * groups) + (
        me * own_rows + picked % own_rows
    )
    select = (picked[:, None] == jnp.arange(model_width, dtype=jnp.int32)[None, :]).astype(low)
    normed1_t = dot(select, normed1_seq, 1, 1).astype(low)
    attended_t = dot(select, attended_seq, 1, 1).astype(low)

    def pick_small(small):
        small = jnp.pad(small, ((0, LANES - small.shape[0]), (0, 0)))
        high = lax.reduce_precision(small, 8, 7)
        return dot(select, high.astype(low), 1, 1) + dot(select, (small - high).astype(low), 1, 1)

    def over_pair(part):
        blocks = part.reshape(outer, 2, own_rows, part.shape[-1])
        return blocks[:, 0] + send(blocks[:, 1].astype(low), 1, 0).astype(f32)

    early = over_pair(
        jnp.concatenate(
            [dot(attended_t, branch_seq), pick_small(small_two), dot(normed1_t, query_seq)], axis=1
        )
    )
    late = over_pair(jnp.concatenate([dot(normed1_t, kv_seq), pick_small(small_one)], axis=1))
    dense_mine = jnp.concatenate([early, late], axis=2)

    reduced, dense_mine = lax.optimization_barrier((reduced, dense_mine))
    swapped = send(
        lax.dynamic_slice_in_dim(reduced, (1 - half) * shard_rows, shard_rows, 0), 1, 0
    )
    dense = dense_mine[0]
    for o in range(1, outer):
        dense = dense + send(dense_mine[o].astype(low), 2 * o, 0).astype(f32)
    grad_gate_w, grad_up_w, grad_down_w = call(
        place_kernel,
        (
            shape(exp_dev, shard_rows, hidden_units, dtype=f32),
            shape(exp_dev, shard_rows, hidden_units, dtype=f32),
            shape(exp_dev, hidden_units, shard_rows, dtype=f32),
        ),
        3,
        "place",
    )(info, reduced, swapped)
    k_cols = KV * HD
    q_at = model_width + LANES
    k_at = q_at + H * HD
    v_at = k_at + k_cols
    one_at = v_at + k_cols
    return (
        block_out,
        grad_tokens,
        dense[:, one_at],
        dense[:, q_at:k_at],
        dense[:, k_at:v_at],
        dense[:, v_at:one_at],
        dense[:, :model_width],
        dense[:, model_width],
        dense[:, model_width + 1 : model_width + 1 + experts],
        grad_gate_w,
        grad_up_w,
        grad_down_w,
    )


def solution(mesh):
    return jax.shard_map(
        shards,
        mesh=mesh,
        in_specs=(
            P(("dp", "expert"), None),
            P("dp"),
            P(("dp", "expert"), None),
            P(),
            P(),
            P(),
            P(),
            P(),
            P(),
            P(),
            P("expert", None, None),
            P("expert", None, None),
            P("expert", None, None),
            P(("dp", "expert"), None),
        ),
        out_specs=(
            P(("dp", "expert"), None),
            P(("dp", "expert"), None),
            P(("dp", "expert")),
            P(("dp", "expert"), None),
            P(("dp", "expert"), None),
            P(("dp", "expert"), None),
            P(("dp", "expert"), None),
            P(("dp", "expert")),
            P(("dp", "expert"), None),
            P("expert", "dp", None),
            P("expert", "dp", None),
            P("expert", None, "dp"),
        ),
        check_vma=False,
    )
```

```python
import math

import jax
import jax.numpy as jnp
from jax import lax
from jax.experimental import pallas as pl
from jax.experimental.pallas import tpu as pltpu
from jax.sharding import PartitionSpec as P

H = 16
KV = 8
HD = 64


norm_eps = 1e-05
masked_score = -1e30


def rope_tables(me, tok_rows, groups):
    row = lax.broadcasted_iota(jnp.int32, (groups * tok_rows, LANES), 0)
    lane = lax.broadcasted_iota(jnp.int32, (groups * tok_rows, LANES), 1)
    position = ((row // tok_rows) ^ me) * tok_rows + row % tok_rows
    frequency = jnp.exp((lane % (HD // 2)).astype(jnp.float32) * (-2.0 * math.log(10000.0) / HD))
    angles = position.astype(jnp.float32) * frequency
    sine = jnp.sin(angles)
    return jnp.cos(angles), jnp.where(lane % HD < HD // 2, -sine, sine)


LANES = 128


def norm_forward(source, gain_vec):
    inverse = lax.rsqrt(jnp.mean(source * source, axis=-1, keepdims=True) + norm_eps)
    return (source * inverse * gain_vec, inverse)


def norm_backward(source, inverse, gain_vec, upstream):
    weighted = upstream * gain_vec
    cubed = inverse * inverse * inverse
    back = inverse * weighted - source * cubed * jnp.mean(weighted * source, axis=-1, keepdims=True)
    return (back, jnp.sum(upstream * source * inverse, axis=0, keepdims=True))


def dot(left, right, left_dim=1, right_dim=0):
    return lax.dot_general(
        left, right, (((left_dim,), (right_dim,)), ((), ())), preferred_element_type=jnp.float32
    )


def lane_of(shape):
    return lax.broadcasted_iota(jnp.int32, shape, 1)


def swap_halves(source):
    lane = lane_of(source.shape)
    return jnp.where(
        lane % HD < HD // 2,
        pltpu.roll(source, LANES - HD // 2, 1),
        pltpu.roll(source, HD // 2, 1),
    )


def rope(source, cosine_table, sine_table):
    return source * cosine_table + swap_halves(source) * sine_table


def unrope(upstream, cosine_table, sine_table):
    return upstream * cosine_table - swap_halves(upstream) * sine_table


def twice(pair):
    lane = lane_of(pair.shape)
    other = pltpu.roll(pair, HD, 1)
    return (jnp.where(lane < HD, pair, other), jnp.where(lane < HD, other, pair))


def stack_heads(pair):
    lane = lane_of(pair.shape)
    zero = jnp.zeros_like(pair)
    return jnp.concatenate(
        [jnp.where(lane < HD, pair, zero), jnp.where(lane < HD, zero, pair)], axis=0
    )


def join_heads(stacked):
    rows = stacked.shape[0] // 2
    lane = lane_of((rows, LANES))
    return jnp.where(lane < HD, stacked[:rows], stacked[rows:])


def allowed_mask(info_ref, seq_len, rows):
    me, prefix = info_ref[0], info_ref[1]
    key = lax.broadcasted_iota(jnp.int32, (seq_len, 2 * rows), 0)
    query = lax.broadcasted_iota(jnp.int32, (seq_len, 2 * rows), 1) % rows + me * rows
    key_pos = ((key // rows) ^ me) * rows + key % rows
    return (key_pos <= query) | (key_pos < prefix)


def forward_kernel(
    info_ref, tokens_ref, query_ref, wk_ref, wv_ref, wo_ref, gain_ref, cos_ref, sin_ref, *rest
):
    blocks, outs = rest[:-9], rest[-9:]
    q_ref, k_ref, v_ref, lse_ref, att_ref, hid_ref, n2_ref, wo_held, sems = outs
    wo_copy = start_copies([(wo_ref, wo_held)], sems)
    rows = tokens_ref.shape[0]
    seq_len = rows * len(blocks)
    normed = jnp.concatenate([b[...] for b in blocks], axis=0)
    cosine, sine = cos_ref[...], sin_ref[...]
    keys = dot(normed, wk_ref[...])
    values = dot(normed, wv_ref[...])
    for c in range(KV // 2):
        cols = slice(c * LANES, (c + 1) * LANES)
        first, second = twice(rope(keys[:, cols], cosine, sine))
        k_ref[2 * c] = first.astype(jnp.bfloat16)
        k_ref[2 * c + 1] = second.astype(jnp.bfloat16)
        first, second = twice(values[:, cols])
        v_ref[2 * c] = first.astype(jnp.bfloat16)
        v_ref[2 * c + 1] = second.astype(jnp.bfloat16)
    allowed = allowed_mask(info_ref, seq_len, rows)
    for h in range(KV):
        cols = slice(h * LANES, (h + 1) * LANES)
        query = rope(query_ref[:, cols], cosine[:rows], sine[:rows]) * (1.0 / math.sqrt(HD))
        q_ref[:, cols] = query.astype(jnp.bfloat16)
        stacked = stack_heads(query).astype(jnp.bfloat16)
        scores = jnp.where(allowed, dot(k_ref[h], stacked, 1, 1), masked_score)
        row_max = jnp.max(scores, axis=0, keepdims=True)
        exps = jnp.exp(scores - row_max)
        total = jnp.sum(exps, axis=0, keepdims=True)
        lse_ref[h : h + 1, :] = row_max + jnp.log(total)
        prob = (exps * (1.0 / total)).astype(jnp.bfloat16)
        att_ref[:, cols] = join_heads(dot(prob, v_ref[h], 0, 0)).astype(jnp.bfloat16)
    wait_all(wo_copy)
    hidden = tokens_ref[...].astype(jnp.float32) + dot(att_ref[...], wo_held[...])
    hid_ref[...] = hidden
    n2_ref[...] = norm_forward(hidden, gain_ref[...])[0].astype(jnp.bfloat16)


def start_copies(pairs, sems):
    copies = [pltpu.make_async_copy(src, dst, sems.at[n]) for n, (src, dst) in enumerate(pairs)]
    for c in copies:
        c.start()
    return copies


def wait_all(copies):
    for c in copies:
        c.wait()


def own_half(info_ref, fh):
    return pl.ds(pl.multiple_of(info_ref[2] * fh, fh), fh)


def gate_up_parts(info_ref, wg_ref, wu_ref, w_ref, first, count):
    fh = wg_ref.shape[2] // 2
    mine = own_half(info_ref, fh)
    pairs = []
    for i in range(count):
        pairs.append((wg_ref.at[first + i, :, mine], w_ref.at[:, pl.ds(2 * i * fh, fh)]))
        pairs.append((wu_ref.at[first + i, :, mine], w_ref.at[:, pl.ds((2 * i + 1) * fh, fh)]))
    return pairs


def down_parts(info_ref, wd_ref, down_ref, first, count):
    fh = wd_ref.shape[1] // 2
    mine = own_half(info_ref, fh)
    return [
        (wd_ref.at[first + i, mine, :], down_ref.at[pl.ds(i * fh, fh), :]) for i in range(count)
    ]


def row_parts(blocks, into, cols):
    rows = blocks[0].shape[0]
    return [(b.at[:, cols], into.at[pl.ds(n * rows, rows), :]) for n, b in enumerate(blocks)]


def hidden_units(
    spot, weights, down, n2_ref, g_ref, probs_ref, gu_ref, scaled_ref, extra, two, one, tiles
):
    total_rows = n2_ref.shape[0]
    step = total_rows // tiles
    fh = (two.stop - two.start) // 2
    for t in range(tiles):
        part = slice(t * step, (t + 1) * step)
        pre = dot(n2_ref[part, :], weights)
        gate_pre, up_pre = pre[:, :fh], pre[:, fh:]
        back = dot(g_ref[part, :], down, 1, 1)
        sig = 0.5 * jnp.tanh(0.5 * gate_pre) + 0.5
        silu = gate_pre * sig
        act = silu * up_pre
        here = lane_of((step, LANES)) == spot
        weight = jnp.sum(jnp.where(here, probs_ref[part, :], 0.0), axis=1, keepdims=True)
        extra(part, jnp.where(here, jnp.sum(act * back, axis=1, keepdims=True), 0.0))
        grad_active = weight * back
        scaled_ref[part, one] = (weight * act).astype(jnp.bfloat16)
        gu_ref[part, two.start : two.start + fh] = (
            grad_active * up_pre * (sig + silu * (1.0 - sig))
        ).astype(jnp.bfloat16)
        gu_ref[part, two.start + fh : two.stop] = (grad_active * silu).astype(jnp.bfloat16)


def widen(router_ref, wide_ref):
    wide_ref[...] = jnp.zeros_like(wide_ref)
    wide_ref[:, : router_ref.shape[1]] = router_ref[...]


def routing(routed_ref, n2_ref, router_wide, probs_ref):
    routed = routed_ref[...].astype(jnp.float32) > 0.5
    logits = jnp.where(routed, dot(n2_ref[...], router_wide[...]), masked_score)
    exps = jnp.where(routed, jnp.exp(logits - jnp.max(logits, axis=-1, keepdims=True)), 0.0)
    probs_ref[...] = exps / jnp.sum(exps, axis=-1, keepdims=True)


def experts_kernel(info_ref, router_ref, wg_ref, wu_ref, wd_ref, *rest, n_blocks, tiles):
    n2_blocks, cot_blocks = rest[:n_blocks], rest[n_blocks : 2 * n_blocks]
    sums_out, gu_out, scaled_out, extra_ref, gate_ref = rest[2 * n_blocks : 2 * n_blocks + 5]
    (
        n2_ref, g_ref, routed_ref, w_ref, down_ref, gu_ref, scaled_ref, sums_ref, probs_ref,
        router_wide,
    ) = rest[2 * n_blocks + 5 : 2 * n_blocks + 15]
    n2_sems, routed_sems, g_sems, w_sems, down_sems, gu_sems, scaled_sems, sums_sems = rest[
        2 * n_blocks + 15 :
    ]
    exp_dev, width, units = wg_ref.shape
    fh = units // 2
    n2_copies = start_copies(row_parts(n2_blocks, n2_ref, pl.ds(0, width)), n2_sems)
    routed_copies = start_copies(row_parts(cot_blocks, routed_ref, pl.ds(width, LANES)), routed_sems)
    w_pairs = gate_up_parts(info_ref, wg_ref, wu_ref, w_ref, 0, exp_dev)
    down_pairs = down_parts(info_ref, wd_ref, down_ref, 0, exp_dev)

    def fetch(e):
        return start_copies(w_pairs[2 * e : 2 * e + 2], w_sems.at[pl.ds(2 * e, 2)]) + start_copies(
            down_pairs[e : e + 1], down_sems.at[pl.ds(e, 1)]
        )

    fetched = [fetch(0)]
    widen(router_ref, router_wide)
    wait_all(n2_copies)
    wait_all(routed_copies)
    g_copies = start_copies(row_parts(cot_blocks, g_ref, pl.ds(0, width)), g_sems)
    routing(routed_ref, n2_ref, router_wide, probs_ref)
    gate_ref[...] = probs_ref[: gate_ref.shape[0], :]
    wait_all(g_copies)
    out_copies = []
    for e in range(exp_dev):
        wait_all(fetched[e])
        if e + 1 < exp_dev:
            fetched.append(fetch(e + 1))

        def extra(part, found, e=e):
            extra_ref[part, :] = found if e == 0 else extra_ref[part, :] + found

        two, one = slice(2 * e * fh, 2 * (e + 1) * fh), slice(e * fh, (e + 1) * fh)
        hidden_units(
            info_ref[0] * exp_dev + e, w_ref[:, two], down_ref[one, :], n2_ref, g_ref, probs_ref,
            gu_ref, scaled_ref, extra, two, one, tiles,
        )
        part = pl.ds(2 * e * fh, 2 * fh)
        out_copies += start_copies(
            [(gu_ref.at[:, part], gu_out.at[:, part])], gu_sems.at[pl.ds(e, 1)]
        )
        part = pl.ds(e * fh, fh)
        out_copies += start_copies(
            [(scaled_ref.at[:, part], scaled_out.at[:, part])], scaled_sems.at[pl.ds(e, 1)]
        )
    cols = scaled_ref.shape[1] // 2
    pieces = [(n2_ref, gu_ref, t * cols, t * cols) for t in range(4)]
    pieces += [(g_ref, scaled_ref, t * cols, (4 + t) * cols) for t in range(2)]
    for n, (left, right, start, at) in enumerate(pieces):
        sums_ref[:, at : at + cols] = dot(
            left[...], right[:, start : start + cols], 0, 0
        ).astype(jnp.bfloat16)
        part = pl.ds(at, cols)
        out_copies += start_copies(
            [(sums_ref.at[:, part], sums_out.at[:, part])], sums_sems.at[pl.ds(n, 1)]
        )
    wait_all(out_copies)


def put_rows(values, t, odd_ref, even_ref, cols):
    rows = odd_ref.shape[1]
    count = values.shape[0] // rows
    for i in range(count):
        n = t * count + i
        out = odd_ref if n % 2 else even_ref
        out[n // 2, :, cols] = values[i * rows : (i + 1) * rows].astype(out.dtype)


def rows_kernel(
    info_ref, extra_ref, wg_ref, wu_ref, gu_in, odd_out, even_out, w_ref, gu_ref, total_ref,
    odd_ref, even_ref, w_sems, gu_sems, out_sems, *, experts
):
    exp_dev, width, _ = wg_ref.shape
    all_rows = gu_ref.shape[0]
    two = gu_ref.shape[1] // exp_dev
    w_pairs = gate_up_parts(info_ref, wg_ref, wu_ref, w_ref, 0, exp_dev)

    def fetch(e):
        part = pl.ds(e * two, two)
        return start_copies(
            w_pairs[2 * e : 2 * e + 2], w_sems.at[pl.ds(2 * e, 2)]
        ) + start_copies([(gu_in.at[:, part], gu_ref.at[:, part])], gu_sems.at[pl.ds(e, 1)])

    fetched = [fetch(0)]
    found = extra_ref[...]
    high = found.astype(jnp.bfloat16).astype(jnp.float32)
    lower = (found - high).astype(jnp.bfloat16).astype(jnp.float32)
    put_rows(
        high + pltpu.roll(lower, experts, 1), 0, odd_ref, even_ref, slice(width, width + LANES)
    )
    out_copies = []
    for e in range(exp_dev):
        wait_all(fetched[e])
        if e + 1 < exp_dev:
            fetched.append(fetch(e + 1))
        cols = slice(e * two, (e + 1) * two)
        for t in range(2):
            part = slice(t * all_rows // 2, (t + 1) * all_rows // 2)
            new = dot(gu_ref[part, cols], w_ref[:, cols], 1, 1)
            if e:
                new = total_ref[part, :] + new
            if e < exp_dev - 1:
                total_ref[part, :] = new
                continue
            put_rows(new, t, odd_ref, even_ref, slice(0, width))
            share = pl.ds(t * odd_ref.shape[0] // 2, odd_ref.shape[0] // 2)
            out_copies += start_copies(
                [(odd_ref.at[share], odd_out.at[share]), (even_ref.at[share], even_out.at[share])],
                out_sems.at[pl.ds(2 * t, 2)],
            )
    wait_all(out_copies)


def mixture_kernel(
    info_ref, wd_ref, scaled_in, odd_ref, even_ref, down_ref, scaled_ref, sems, in_sems
):
    width = wd_ref.shape[2]
    down_copies = start_copies(down_parts(info_ref, wd_ref, down_ref, 0, wd_ref.shape[0]), sems)
    wait_all(start_copies([(scaled_in, scaled_ref)], in_sems))
    wait_all(down_copies)
    step = scaled_ref.shape[0] // 2
    for t in range(2):
        mix = dot(scaled_ref[t * step : (t + 1) * step, :], down_ref[...])
        put_rows(mix, t, odd_ref, even_ref, slice(0, width))


def final_kernel(
    info_ref, sums_ref, arrived_ref, early_ref, late_ref, *rest, n_early, n_late
):
    dense = rest[:-10]
    gate_ref, up_ref, down_ref, wq_ref, wk_ref, wv_ref, wo_ref, router_ref, one_ref, two_ref = rest[-10:]
    exp_dev, rows, units = gate_ref.shape
    fh = units // 2
    half = info_ref[2]
    kept = sums_ref[pl.ds(pl.multiple_of(half * rows, rows), rows), :]
    got = arrived_ref[...]
    first = jnp.where(half == 0, kept, got).astype(jnp.float32)
    second = jnp.where(half == 0, got, kept).astype(jnp.float32)
    for e in range(exp_dev):
        at = 2 * e * fh
        gate_ref[e, :, :fh] = first[:, at : at + fh]
        gate_ref[e, :, fh:] = second[:, at : at + fh]
        up_ref[e, :, :fh] = first[:, at + fh : at + 2 * fh]
        up_ref[e, :, fh:] = second[:, at + fh : at + 2 * fh]
        at = (2 * exp_dev + e) * fh
        down_ref[e, :fh, :] = first[:, at : at + fh].T
        down_ref[e, fh:, :] = second[:, at : at + fh].T
    early, late = early_ref[0], late_ref[0]
    for d in dense:
        early = early + d[:, :n_early].astype(jnp.float32)
        late = late + d[:, n_early:].astype(jnp.float32)
    width, k_cols = wo_ref.shape[1], wk_ref.shape[1]
    wo_ref[...] = early[:, :width]
    wq_ref[...] = early[:, width + LANES :]
    wk_ref[...] = late[:, :k_cols]
    wv_ref[...] = late[:, k_cols : 2 * k_cols]
    small = early[:, width : width + LANES]
    router_ref[...] = small[:, 1 : 1 + router_ref.shape[1]]
    two_ref[...] = small.T[:1, :]
    one_ref[...] = late[:, 2 * k_cols :].T[:1, :]


def selection(info_ref, select_ref, own_rows):
    count, width = select_ref.shape
    groups = width // count
    row = lax.broadcasted_iota(jnp.int32, (count, width), 0)
    col = lax.broadcasted_iota(jnp.int32, (count, width), 1)
    want = ((row // own_rows) ^ info_ref[3]) * (own_rows * groups) + (
        info_ref[0] * own_rows + row % own_rows
    )
    select_ref[...] = jnp.where(col == want, 1.0, 0.0).astype(jnp.bfloat16)


def pick_small(blocks, rows, count, select):
    total = blocks[0][rows : rows + 2 * count].astype(jnp.float32)
    for b in blocks[1:]:
        total = total + b[rows : rows + 2 * count].astype(jnp.float32)
    total = jnp.concatenate(
        [total[:count] + total[count:], jnp.zeros((LANES - count, total.shape[1]), jnp.float32)],
        axis=0,
    )
    high = total.astype(jnp.bfloat16)
    lower = (total - high.astype(jnp.float32)).astype(jnp.bfloat16)
    return dot(select, high, 1, 1) + dot(select, lower, 1, 1)


def put_shares(values, odd_ref, even_ref, at):
    rows = odd_ref.shape[1]
    for n in range(2 * odd_ref.shape[0]):
        out = odd_ref if n % 2 else even_ref
        out[n // 2, :, at : at + values.shape[1]] = values[n * rows : (n + 1) * rows].astype(
            out.dtype
        )


def early_dense_kernel(info_ref, *rest, groups, count):
    normed, attended, branch, query = (rest[n * groups : (n + 1) * groups] for n in range(4))
    odd_ref, even_ref, normed_t_ref, select_ref = rest[4 * groups :]
    rows, width = normed[0].shape
    selection(info_ref, select_ref, odd_ref.shape[1])
    select = select_ref[...]

    def seq(blocks):
        return jnp.concatenate([b[:rows] for b in blocks], axis=0)

    normed_t = dot(select, seq(normed), 1, 1).astype(jnp.bfloat16)
    normed_t_ref[...] = normed_t
    attended_t = dot(select, seq(attended), 1, 1).astype(jnp.bfloat16)
    put_shares(dot(attended_t, seq(branch)), odd_ref, even_ref, 0)
    put_shares(pick_small(branch, rows, count, select), odd_ref, even_ref, width)
    put_shares(dot(normed_t, seq(query)), odd_ref, even_ref, width + LANES)


def late_dense_kernel(info_ref, normed_t_ref, *rest):
    blocks = rest[:-3]
    odd_ref, even_ref, select_ref = rest[-3:]
    rows = normed_t_ref.shape[1] // len(blocks)
    selection(info_ref, select_ref, odd_ref.shape[1])
    kv = jnp.concatenate([b[:rows] for b in blocks], axis=0)
    put_shares(dot(normed_t_ref[...], kv), odd_ref, even_ref, 0)
    put_shares(pick_small(blocks, rows, 1, select_ref[...]), odd_ref, even_ref, kv.shape[1])


def small_rows(count):
    return -(-2 * count // 16) * 16


def put_small(ref, start, values):
    count = values.shape[0]
    high = values.astype(jnp.bfloat16).astype(jnp.float32)
    fill = jnp.zeros((small_rows(count) - 2 * count, values.shape[1]), jnp.float32)
    ref[start:] = jnp.concatenate([high, values - high, fill], axis=0).astype(jnp.bfloat16)


def backward_kernel(
    info_ref, own_ref, gate_ref, cot_ref, n2_ref, hid_ref, router_ref, gain_ref, wo_ref, q_ref,
    lse_ref, cos_ref, sin_ref, k_hbm, v_hbm, wq_hbm, *rest, experts
):
    arrived, outs = rest[:-11], rest[-11:]
    ghid_ref, branch_ref, dq_ref, odd_ref, even_ref, gn_ref = outs[:6]
    router_wide, k_ref, v_ref, wq_ref, sems = outs[6:]
    late = start_copies([(k_hbm, k_ref), (v_hbm, v_ref), (wq_hbm, wq_ref)], sems)
    widen(router_ref, router_wide)
    rows, width = hid_ref.shape
    summed = own_ref[...]
    for a in arrived:
        summed = summed + a[...].astype(jnp.float32)
    extra = summed[:, width:]
    gate_grads = extra + pltpu.roll(extra, LANES - experts, 1)
    gate = gate_ref[...]
    grad_logits = (
        gate * (gate_grads - jnp.sum(gate * gate_grads, axis=-1, keepdims=True))
    ).astype(jnp.bfloat16)
    router_grad = dot(grad_logits, n2_ref[...], 0, 0)
    grad_normed = summed[:, :width] + dot(grad_logits, router_wide[...], 1, 1)
    hidden = hid_ref[...]
    inverse = lax.rsqrt(jnp.mean(hidden * hidden, axis=-1, keepdims=True) + norm_eps)
    back, norm_grad = norm_backward(hidden, inverse, gain_ref[...], grad_normed)
    grad_hidden = cot_ref[...].astype(jnp.float32) + back
    ghid_ref[...] = grad_hidden
    branch = grad_hidden.astype(jnp.bfloat16)
    branch_ref[:rows] = branch
    put_small(branch_ref, rows, jnp.concatenate([norm_grad, router_grad[:experts]], axis=0))
    grad_attended = dot(branch, wo_ref[...], 1, 1).astype(jnp.bfloat16)
    wait_all(late[:2])
    seq_len = k_ref.shape[1]
    allowed = allowed_mask(info_ref, seq_len, rows)
    cosine, sine = cos_ref[:rows, :], sin_ref[:rows, :]
    lane = lane_of((seq_len, LANES))
    kept = [None, None]
    for h in range(KV):
        cols = slice(h * LANES, (h + 1) * LANES)
        stacked = stack_heads(q_ref[:, cols])
        grad_stacked = stack_heads(grad_attended[:, cols])
        keys = k_ref[h]
        scores = jnp.where(allowed, dot(keys, stacked, 1, 1), masked_score)
        prob = jnp.exp(scores - lse_ref[h : h + 1, :])
        grad_prob = dot(v_ref[h], grad_stacked, 1, 1)
        delta = jnp.sum(prob * grad_prob, axis=0, keepdims=True)
        grad_scores = (prob * (grad_prob - delta)).astype(jnp.bfloat16)
        dq = join_heads(dot(grad_scores, keys, 0, 0)) * (1.0 / math.sqrt(HD))
        dq_ref[:, cols] = unrope(dq, cosine, sine).astype(jnp.bfloat16)
        parts = (dot(grad_scores, stacked), dot(prob.astype(jnp.bfloat16), grad_stacked))
        for n in range(2):
            both = parts[n] + pltpu.roll(parts[n], HD, 1)
            if h % 2 == 0:
                kept[n] = both
                continue
            pair = jnp.where(lane < HD, kept[n], both)
            start = (n * KV // 2 + h // 2) * LANES
            put_rows(pair, 0, odd_ref, even_ref, slice(start, start + LANES))
    wait_all(late[2:])
    gn_ref[...] = dot(dq_ref[...], wq_ref[...], 1, 1)


def tokens_kernel(
    own_ref, gn_ref, wk_ref, wv_ref, tokens_ref, gain_ref, ghid_ref, cos_ref, sin_ref, *rest
):
    arrived, (kv_ref, out_ref) = rest[:-2], rest[-2:]
    rows = tokens_ref.shape[0]
    summed = own_ref[...]
    for a in arrived:
        summed = summed + a[...].astype(jnp.float32)
    k_cols = KV * HD
    for c in range(k_cols // LANES):
        cols = slice(c * LANES, (c + 1) * LANES)
        kv_ref[:rows, cols] = unrope(summed[:, cols], cos_ref[:rows, :], sin_ref[:rows, :]).astype(
            jnp.bfloat16
        )
    kv_ref[:rows, k_cols:] = summed[:, k_cols:].astype(jnp.bfloat16)
    grad_normed = (
        gn_ref[...]
        + dot(kv_ref[:rows, :k_cols], wk_ref[...], 1, 1)
        + dot(kv_ref[:rows, k_cols:], wv_ref[...], 1, 1)
    )
    source = tokens_ref[...].astype(jnp.float32)
    inverse = lax.rsqrt(jnp.mean(source * source, axis=-1, keepdims=True) + norm_eps)
    back, norm_grad = norm_backward(source, inverse, gain_ref[...], grad_normed)
    put_small(kv_ref, rows, norm_grad)
    out_ref[...] = (ghid_ref[...] + back).astype(jnp.bfloat16)


def call(kernel, out_shape, name, hbm=(), hbm_out=(), scratch=(), smem=True):
    def run(*args):
        specs = [
            pl.BlockSpec(memory_space=pl.ANY if n in hbm else pltpu.VMEM)
            for n in range(len(args))
        ]
        if smem:
            specs[0] = pl.BlockSpec(memory_space=pltpu.SMEM)
        return pl.pallas_call(
            kernel,
            out_shape=out_shape,
            in_specs=specs,
            out_specs=[
                pl.BlockSpec(memory_space=pl.ANY if n in hbm_out else pltpu.VMEM)
                for n in range(len(out_shape))
            ],
            scratch_shapes=list(scratch),
            compiler_params=pltpu.CompilerParams(vmem_limit_bytes=60 * 1024 * 1024),
            name=name,
        )(*args)

    return run


def shape(*dims, dtype=jnp.bfloat16):
    return jax.ShapeDtypeStruct(dims, dtype)


def shards(
    tokens,
    prefix_len,
    routes,
    norm1_gain,
    w_query,
    w_key,
    w_value,
    w_output,
    norm2_gain,
    w_router,
    w_gate,
    w_up,
    w_down,
    cotangent,
):
    tok_rows, model_width = tokens.shape
    groups = lax.axis_size("expert")
    copies = lax.axis_size("dp")
    me = lax.axis_index("expert")
    half = lax.axis_index("dp") % 2
    exp_dev, _, hidden_units = w_gate.shape
    half_units = hidden_units // 2
    experts = exp_dev * groups
    f32 = jnp.float32
    seq_len = tok_rows * groups
    low = jnp.bfloat16

    def send(block, pair_flip, flip):
        return lax.ppermute(
            block,
            ("dp", "expert"),
            [
                (i * groups + j, (i ^ pair_flip) * groups + (j ^ flip))
                for i in range(copies)
                for j in range(groups)
            ],
        )

    def gather_even(block, pairs):
        return [
            block if (s, r) == (0, 0) else send(block, s, r)
            for s in range(pairs)
            for r in range(0, groups, 2)
        ]

    def gather_odd(even):
        out = []
        for b in even:
            out += [b, send(b, 0, 1)]
        return out

    def gather(block, pairs):
        return gather_odd(gather_even(block, pairs))

    def core_sum(odd, even):
        return even + send(odd, 0, 1).astype(jnp.float32)

    def swap(mine, pairs):
        mine = mine.astype(low)
        spots = [(s, r) for s in range(pairs) for r in range(0, groups, 2)]
        return [send(mine[n], *spots[n]) for n in range(1, len(spots))]

    tokens_f = tokens.astype(f32)
    normed1 = norm_forward(tokens_f, norm1_gain)[0].astype(low)
    normed1_even = gather_even(normed1, 1)
    cosine, sine = rope_tables(me, tok_rows, groups)
    cosine, sine, *normed1_even = lax.optimization_barrier((cosine, sine, *normed1_even))
    normed1_blocks = gather_odd(normed1_even)
    routed = jnp.any(
        routes[:, :, None] == jnp.arange(experts, dtype=jnp.int32)[None, None, :], axis=1
    )
    cot_mask = jnp.concatenate(
        [cotangent, jnp.pad(routed.astype(low), ((0, 0), (0, LANES - experts)))], axis=1
    )
    cot_mask, *normed1_even = lax.optimization_barrier((cot_mask, *normed1_even))
    cot_even = gather_even(cot_mask, 2)
    my_dp = lax.axis_index("dp")
    info = jnp.stack([me, prefix_len[0], half, my_dp]).astype(jnp.int32)
    gain_one, gain_two = norm1_gain[None], norm2_gain[None]

    query_pre = dot(normed1, w_query)
    q_low, k_two, v_two, lse, attended, hidden_state, normed2 = call(
        forward_kernel,
        (
            shape(tok_rows, H * HD),
            shape(KV, seq_len, LANES),
            shape(KV, seq_len, LANES),
            shape(KV, 2 * tok_rows, dtype=f32),
            shape(tok_rows, H * HD),
            shape(tok_rows, model_width, dtype=f32),
            shape(tok_rows, model_width),
        ),
        "attention_forward",
        hbm=(5,),
        scratch=(pltpu.VMEM((H * HD, model_width), low), pltpu.SemaphoreType.DMA((1,))),
    )(
        info, tokens, query_pre, w_key, w_value, w_output, gain_two, cosine, sine,
        *normed1_blocks,
    )

    normed2, *cot_even = lax.optimization_barrier((normed2, *cot_even))
    cot_blocks = gather_odd(cot_even)
    n2_blocks = gather(normed2, 2)
    attended_even = gather_even(attended, 1)
    n_blocks = 2 * groups
    all_rows = n_blocks * tok_rows
    wide = model_width + LANES

    dma = pltpu.SemaphoreType.DMA
    units = half_units * exp_dev
    sums, grad_gu, scaled, extra, gate_probs = call(
        lambda *refs: experts_kernel(*refs, n_blocks=n_blocks, tiles=2),
        (
            shape(model_width, 3 * units),
            shape(all_rows, 2 * units),
            shape(all_rows, units),
            shape(all_rows, LANES, dtype=f32),
            shape(tok_rows, LANES, dtype=f32),
        ),
        "experts",
        hbm=tuple(range(2, 5 + 2 * n_blocks)),
        hbm_out=(0, 1, 2),
        scratch=(
            pltpu.VMEM((all_rows, model_width), low),
            pltpu.VMEM((all_rows, model_width), low),
            pltpu.VMEM((all_rows, LANES), low),
            pltpu.VMEM((model_width, 2 * units), low),
            pltpu.VMEM((units, model_width), low),
            pltpu.VMEM((all_rows, 2 * units), low),
            pltpu.VMEM((all_rows, units), low),
            pltpu.VMEM((model_width, 3 * units), low),
            pltpu.VMEM((all_rows, LANES), f32),
            pltpu.VMEM((model_width, LANES), low),
            dma((n_blocks,)),
            dma((n_blocks,)),
            dma((n_blocks,)),
            dma((2 * exp_dev,)),
            dma((exp_dev,)),
            dma((exp_dev,)),
            dma((exp_dev,)),
            dma((6,)),
        ),
    )(info, w_router, w_gate, w_up, w_down, *n2_blocks, *cot_blocks)
    outer = copies // 2
    shard_rows = model_width // copies
    reduced = lax.psum_scatter(
        sums,
        "dp",
        scatter_dimension=0,
        axis_index_groups=[[2 * o + p for o in range(outer)] for p in range(2)],
        tiled=True,
    )

    odd, even = call(
        lambda *refs: rows_kernel(*refs, experts=experts),
        (shape(groups, tok_rows, wide), shape(groups, tok_rows, wide, dtype=f32)),
        "experts_rows",
        hbm=(2, 3, 4),
        hbm_out=(0, 1),
        scratch=(
            pltpu.VMEM((model_width, 2 * units), low),
            pltpu.VMEM((all_rows, 2 * units), low),
            pltpu.VMEM((all_rows, model_width), f32),
            pltpu.VMEM((groups, tok_rows, wide), low),
            pltpu.VMEM((groups, tok_rows, wide), f32),
            dma((2 * exp_dev,)),
            dma((exp_dev,)),
            dma((4,)),
        ),
    )(info, extra, w_gate, w_up, grad_gu)
    odd, *attended_even = lax.optimization_barrier((odd, *attended_even))
    mine = core_sum(odd, even)
    scaled, mine = lax.optimization_barrier((scaled, mine))
    arrived = swap(mine, 2)
    mix_odd, mix_even = call(
        mixture_kernel,
        (shape(groups, tok_rows, model_width), shape(groups, tok_rows, model_width, dtype=f32)),
        "experts_mixture",
        hbm=(1, 2),
        scratch=(
            pltpu.VMEM((units, model_width), low),
            pltpu.VMEM((all_rows, units), low),
            dma((exp_dev,)),
            dma((1,)),
        ),
    )(info, w_down, scaled)
    mix_odd, mix_even, *arrived = lax.optimization_barrier((mix_odd, mix_even, *arrived))
    mix_mine = core_sum(mix_odd, mix_even).reshape(2, groups // 2, tok_rows, model_width)
    attended_blocks = gather_odd(attended_even)

    grad_hidden, grad_branch, grad_query, kv_odd, kv_even, grad_normed_q = call(
        lambda *refs: backward_kernel(*refs, experts=experts),
        (
            shape(tok_rows, model_width, dtype=f32),
            shape(tok_rows + small_rows(experts + 1), model_width),
            shape(tok_rows, H * HD),
            shape(groups // 2, tok_rows, 2 * KV * HD),
            shape(groups // 2, tok_rows, 2 * KV * HD, dtype=f32),
            shape(tok_rows, model_width, dtype=f32),
        ),
        "attention_backward",
        hbm=(13, 14, 15),
        scratch=(
            pltpu.VMEM((model_width, LANES), low),
            pltpu.VMEM((KV, seq_len, LANES), low),
            pltpu.VMEM((KV, seq_len, LANES), low),
            pltpu.VMEM((model_width, H * HD), low),
            dma((3,)),
        ),
    )(
        info, mine[0], gate_probs, cotangent, normed2, hidden_state, w_router, gain_two, w_output,
        q_low, lse, cosine, sine, k_two, v_two, w_query, *arrived,
    )
    kv_mine = core_sum(kv_odd, kv_even)
    kv_arrived = swap(kv_mine, 1)
    mix_mine, kv_mine = lax.optimization_barrier((mix_mine, kv_mine))
    mix_pair = mix_mine[0] + send(mix_mine[1].astype(low), 1, 0).astype(f32)
    query_later, grad_branch, *kv_arrived = lax.optimization_barrier(
        (grad_query, grad_branch, *kv_arrived)
    )
    branch_blocks = gather(grad_branch, 1)
    query_blocks = gather(query_later, 1)
    grad_kv, grad_tokens = call(
        tokens_kernel,
        (
            shape(tok_rows + small_rows(1), 2 * KV * HD),
            shape(tok_rows, model_width),
        ),
        "tokens_backward",
        smem=False,
    )(
        kv_mine[0], grad_normed_q, w_key, w_value, tokens, gain_one, grad_hidden, cosine, sine,
        *kv_arrived,
    )
    kv_even_blocks = gather_even(grad_kv, 1)
    mix_pair, *kv_even_blocks = lax.optimization_barrier((mix_pair, *kv_even_blocks))
    kv_blocks = gather_odd(kv_even_blocks)
    mixture = mix_pair[0]
    for a in swap(mix_pair, 1):
        mixture = mixture + a.astype(f32)
    block_out = (hidden_state + mixture).astype(low)

    own_rows = model_width // (copies * groups)
    n_early, n_late = model_width + LANES + H * HD, 2 * KV * HD + LANES
    select = pltpu.VMEM((copies * own_rows, model_width), low)
    early_odd, early_even, normed1_t = call(
        lambda *refs: early_dense_kernel(*refs, groups=groups, count=experts + 1),
        (
            shape(outer, own_rows, n_early),
            shape(outer, own_rows, n_early, dtype=f32),
            shape(copies * own_rows, seq_len),
        ),
        "dense_early",
        scratch=(select,),
    )(info, *normed1_blocks, *attended_blocks, *branch_blocks, *query_blocks)
    early = early_even + send(early_odd, 1, 0).astype(f32)
    late_odd, late_even = call(
        late_dense_kernel,
        (shape(outer, own_rows, n_late), shape(outer, own_rows, n_late, dtype=f32)),
        "dense_late",
        scratch=(select,),
    )(info, normed1_t, *kv_blocks)
    late = late_even + send(late_odd, 1, 0).astype(f32)
    dense_send = jnp.concatenate([early[1:].astype(low), late[1:].astype(low)], axis=2)

    swapped = send(
        lax.dynamic_slice_in_dim(reduced, (1 - half) * shard_rows, shard_rows, 0), 1, 0
    )
    _, dense_send = lax.optimization_barrier((reduced, dense_send))
    dense_arrived = [send(dense_send[o - 1], 2 * o, 0) for o in range(1, outer)]
    k_cols = KV * HD
    (
        grad_gate_w, grad_up_w, grad_down_w, grad_query_w, grad_key_w, grad_value_w,
        grad_output_w, grad_router, grad_norm1, grad_norm2,
    ) = call(
        lambda *refs: final_kernel(*refs, n_early=n_early, n_late=n_late),
        (
            shape(exp_dev, shard_rows, hidden_units, dtype=f32),
            shape(exp_dev, shard_rows, hidden_units, dtype=f32),
            shape(exp_dev, hidden_units, shard_rows, dtype=f32),
            shape(own_rows, H * HD, dtype=f32),
            shape(own_rows, k_cols, dtype=f32),
            shape(own_rows, k_cols, dtype=f32),
            shape(own_rows, model_width, dtype=f32),
            shape(own_rows, experts, dtype=f32),
            shape(1, own_rows, dtype=f32),
            shape(1, own_rows, dtype=f32),
        ),
        "place",
    )(info, reduced, swapped, early, late, *dense_arrived)
    return (
        block_out,
        grad_tokens,
        grad_norm1[0],
        grad_query_w,
        grad_key_w,
        grad_value_w,
        grad_output_w,
        grad_norm2[0],
        grad_router,
        grad_gate_w,
        grad_up_w,
        grad_down_w,
    )


def solution(mesh):
    return jax.shard_map(
        shards,
        mesh=mesh,
        in_specs=(
            P(("dp", "expert"), None),
            P("dp"),
            P(("dp", "expert"), None),
            P(),
            P(),
            P(),
            P(),
            P(),
            P(),
            P(),
            P("expert", None, None),
            P("expert", None, None),
            P("expert", None, None),
            P(("dp", "expert"), None),
        ),
        out_specs=(
            P(("dp", "expert"), None),
            P(("dp", "expert"), None),
            P(("dp", "expert")),
            P(("dp", "expert"), None),
            P(("dp", "expert"), None),
            P(("dp", "expert"), None),
            P(("dp", "expert"), None),
            P(("dp", "expert")),
            P(("dp", "expert"), None),
            P("expert", "dp", None),
            P("expert", "dp", None),
            P("expert", None, "dp"),
        ),
        check_vma=False,
    )
```

```python
import math

import jax
import jax.numpy as jnp
from jax import lax
from jax.experimental import pallas as pl
from jax.experimental.pallas import tpu as pltpu
from jax.sharding import PartitionSpec as P

H = 16
KV = 8
HD = 64


norm_eps = 1e-05
masked_score = -1e30


def rope_tables(me, tok_rows, groups):
    row = lax.broadcasted_iota(jnp.int32, (groups * tok_rows, LANES), 0)
    lane = lax.broadcasted_iota(jnp.int32, (groups * tok_rows, LANES), 1)
    position = ((row // tok_rows) ^ me) * tok_rows + row % tok_rows
    frequency = jnp.exp((lane % (HD // 2)).astype(jnp.float32) * (-2.0 * math.log(10000.0) / HD))
    angles = position.astype(jnp.float32) * frequency
    sine = jnp.sin(angles)
    return jnp.cos(angles), jnp.where(lane % HD < HD // 2, -sine, sine)


LANES = 128
LIMIT_MIB = 63


def norm_forward(source, gain_vec):
    inverse = lax.rsqrt(jnp.mean(source * source, axis=-1, keepdims=True) + norm_eps)
    return (source * inverse * gain_vec, inverse)


def norm_backward(source, inverse, gain_vec, upstream):
    weighted = upstream * gain_vec
    cubed = inverse * inverse * inverse
    back = inverse * weighted - source * cubed * jnp.mean(weighted * source, axis=-1, keepdims=True)
    return (back, jnp.sum(upstream * source * inverse, axis=0, keepdims=True))


def dot(left, right, left_dim=1, right_dim=0):
    return lax.dot_general(
        left, right, (((left_dim,), (right_dim,)), ((), ())), preferred_element_type=jnp.float32
    )


def lane_of(shape):
    return lax.broadcasted_iota(jnp.int32, shape, 1)


def swap_halves(source):
    lane = lane_of(source.shape)
    return jnp.where(
        lane % HD < HD // 2,
        pltpu.roll(source, LANES - HD // 2, 1),
        pltpu.roll(source, HD // 2, 1),
    )


def rope(source, cosine_table, sine_table):
    return source * cosine_table + swap_halves(source) * sine_table


def unrope(upstream, cosine_table, sine_table):
    return upstream * cosine_table - swap_halves(upstream) * sine_table


def twice(pair):
    lane = lane_of(pair.shape)
    other = pltpu.roll(pair, HD, 1)
    return (jnp.where(lane < HD, pair, other), jnp.where(lane < HD, other, pair))


def stack_heads(pair):
    lane = lane_of(pair.shape)
    zero = jnp.zeros_like(pair)
    return jnp.concatenate(
        [jnp.where(lane < HD, pair, zero), jnp.where(lane < HD, zero, pair)], axis=0
    )


def join_heads(stacked):
    rows = stacked.shape[0] // 2
    lane = lane_of((rows, LANES))
    return jnp.where(lane < HD, stacked[:rows], stacked[rows:])


def allowed_mask(info_ref, seq_len, rows):
    me, prefix = info_ref[0], info_ref[1]
    key = lax.broadcasted_iota(jnp.int32, (seq_len, 2 * rows), 0)
    query = lax.broadcasted_iota(jnp.int32, (seq_len, 2 * rows), 1) % rows + me * rows
    key_pos = ((key // rows) ^ me) * rows + key % rows
    return (key_pos <= query) | (key_pos < prefix)


def forward_kernel(
    info_ref, tokens_ref, query_ref, wk_ref, wv_ref, wo_ref, gain_ref, cos_ref, sin_ref, *rest
):
    blocks, outs = rest[:-9], rest[-9:]
    q_ref, k_ref, v_ref, lse_ref, att_ref, hid_ref, n2_ref, wo_held, sems = outs
    wo_copy = start_copies([(wo_ref, wo_held)], sems)
    rows = tokens_ref.shape[0]
    seq_len = rows * len(blocks)
    normed = jnp.concatenate([b[...] for b in blocks], axis=0)
    cosine, sine = cos_ref[...], sin_ref[...]
    keys = dot(normed, wk_ref[...])
    values = dot(normed, wv_ref[...])
    for c in range(KV // 2):
        cols = slice(c * LANES, (c + 1) * LANES)
        first, second = twice(rope(keys[:, cols], cosine, sine))
        k_ref[2 * c] = first.astype(jnp.bfloat16)
        k_ref[2 * c + 1] = second.astype(jnp.bfloat16)
        first, second = twice(values[:, cols])
        v_ref[2 * c] = first.astype(jnp.bfloat16)
        v_ref[2 * c + 1] = second.astype(jnp.bfloat16)
    allowed = allowed_mask(info_ref, seq_len, rows)
    for h in range(KV):
        cols = slice(h * LANES, (h + 1) * LANES)
        query = rope(query_ref[:, cols], cosine[:rows], sine[:rows]) * (1.0 / math.sqrt(HD))
        q_ref[:, cols] = query.astype(jnp.bfloat16)
        stacked = stack_heads(query).astype(jnp.bfloat16)
        scores = jnp.where(allowed, dot(k_ref[h], stacked, 1, 1), masked_score)
        row_max = jnp.max(scores, axis=0, keepdims=True)
        exps = jnp.exp(scores - row_max)
        total = jnp.sum(exps, axis=0, keepdims=True)
        lse_ref[h : h + 1, :] = row_max + jnp.log(total)
        prob = (exps * (1.0 / total)).astype(jnp.bfloat16)
        att_ref[:, cols] = join_heads(dot(prob, v_ref[h], 0, 0)).astype(jnp.bfloat16)
    wait_all(wo_copy)
    hidden = tokens_ref[...].astype(jnp.float32) + dot(att_ref[...], wo_held[...])
    hid_ref[...] = hidden
    n2_ref[...] = norm_forward(hidden, gain_ref[...])[0].astype(jnp.bfloat16)


def start_copies(pairs, sems):
    copies = describe(pairs, sems)
    for c in copies:
        c.start()
    return copies


def wait_all(copies):
    for c in copies:
        c.wait()


def own_half(info_ref, fh):
    return pl.ds(pl.multiple_of(info_ref[2] * fh, fh), fh)


def expert_parts(info_ref, wg_ref, wu_ref, w_ref, e):
    fh = wg_ref.shape[2] // 2
    mine = own_half(info_ref, fh)
    return [
        (wg_ref.at[e, :, mine], w_ref.at[e, :, pl.ds(0, fh)]),
        (wu_ref.at[e, :, mine], w_ref.at[e, :, pl.ds(fh, fh)]),
    ]


def down_part(info_ref, wd_ref, down_ref, e):
    mine = own_half(info_ref, wd_ref.shape[1] // 2)
    return [(wd_ref.at[e, mine, :], down_ref.at[e])]


def describe(pairs, sems):
    return [pltpu.make_async_copy(src, dst, sems.at[n]) for n, (src, dst) in enumerate(pairs)]


def row_parts(blocks, into, cols):
    rows = blocks[0].shape[0]
    return [(b.at[:, cols], into.at[pl.ds(n * rows, rows), :]) for n, b in enumerate(blocks)]


def widen(router_ref, wide_ref):
    wide_ref[...] = jnp.zeros_like(wide_ref)
    wide_ref[:, : router_ref.shape[1]] = router_ref[...]


def routing(routed_ref, n2_ref, router_wide, probs_ref):
    routed = routed_ref[...].astype(jnp.float32) > 0.5
    logits = jnp.where(routed, dot(n2_ref[...], router_wide[...]), masked_score)
    exps = jnp.where(routed, jnp.exp(logits - jnp.max(logits, axis=-1, keepdims=True)), 0.0)
    probs_ref[...] = exps / jnp.sum(exps, axis=-1, keepdims=True)


def experts_kernel(info_ref, router_ref, wg_ref, wu_ref, wd_ref, *rest, n_blocks, tiles):
    n2_blocks, cot_blocks = rest[:n_blocks], rest[n_blocks : 2 * n_blocks]
    sums_out, gu_out, scaled_out, extra_ref, gate_ref = rest[2 * n_blocks : 2 * n_blocks + 5]
    (
        n2_ref, g_ref, routed_ref, w_ref, down_ref, gu_ref, scaled_ref, sums_ref, probs_ref,
        router_wide,
    ) = rest[2 * n_blocks + 5 : 2 * n_blocks + 15]
    n2_sems, routed_sems, g_sems, w_sems, out_sems = rest[2 * n_blocks + 15 :]
    exp_dev, width, units = wg_ref.shape
    fh = units // 2
    n2_copies = start_copies(row_parts(n2_blocks, n2_ref, pl.ds(0, width)), n2_sems)
    routed_copies = start_copies(row_parts(cot_blocks, routed_ref, pl.ds(width, LANES)), routed_sems)

    def weights(e):
        pairs = expert_parts(info_ref, wg_ref, wu_ref, w_ref, e)
        return describe(pairs + down_part(info_ref, wd_ref, down_ref, e), w_sems.at[e])

    def results(e):
        cols = pl.ds(pl.multiple_of(e * 3 * fh, 3 * fh), 3 * fh)
        return describe(
            [
                (gu_ref.at[e], gu_out.at[e]),
                (scaled_ref.at[e], scaled_out.at[e]),
                (sums_ref.at[e], sums_out.at[:, cols]),
            ],
            out_sems.at[e],
        )

    for c in weights(0):
        c.start()
    widen(router_ref, router_wide)
    extra_ref[...] = jnp.zeros_like(extra_ref)
    wait_all(n2_copies)
    wait_all(routed_copies)
    g_copies = start_copies(row_parts(cot_blocks, g_ref, pl.ds(0, width)), g_sems)
    routing(routed_ref, n2_ref, router_wide, probs_ref)
    gate_ref[...] = probs_ref[: gate_ref.shape[0], :]
    wait_all(g_copies)
    step = n2_ref.shape[0] // tiles

    def one_expert(e, carry):
        wait_all(weights(e))

        @pl.when(e + 1 < exp_dev)
        def _():
            for c in weights(e + 1):
                c.start()

        spot = info_ref[0] * exp_dev + e
        for t in range(tiles):
            part = slice(t * step, (t + 1) * step)
            pre = dot(n2_ref[part, :], w_ref[e])
            gate_pre, up_pre = pre[:, :fh], pre[:, fh:]
            back = dot(g_ref[part, :], down_ref[e], 1, 1)
            sig = 0.5 * jnp.tanh(0.5 * gate_pre) + 0.5
            silu = gate_pre * sig
            act = silu * up_pre
            here = lane_of((step, LANES)) == spot
            weight = jnp.sum(jnp.where(here, probs_ref[part, :], 0.0), axis=1, keepdims=True)
            extra_ref[part, :] += jnp.where(here, jnp.sum(act * back, axis=1, keepdims=True), 0.0)
            grad_active = weight * back
            scaled_ref[e, part, :] = (weight * act).astype(jnp.bfloat16)
            gu_ref[e, part, :fh] = (
                grad_active * up_pre * (sig + silu * (1.0 - sig))
            ).astype(jnp.bfloat16)
            gu_ref[e, part, fh:] = (grad_active * silu).astype(jnp.bfloat16)
        sums_ref[e, :, : 2 * fh] = dot(n2_ref[...], gu_ref[e], 0, 0).astype(jnp.bfloat16)
        sums_ref[e, :, 2 * fh :] = dot(g_ref[...], scaled_ref[e], 0, 0).astype(jnp.bfloat16)
        for c in results(e):
            c.start()
        return carry

    lax.fori_loop(0, exp_dev, one_expert, 0)
    for e in range(exp_dev):
        wait_all(results(e))


def put_rows(values, t, odd_ref, even_ref, cols):
    rows = odd_ref.shape[1]
    count = values.shape[0] // rows
    for i in range(count):
        n = t * count + i
        out = odd_ref if n % 2 else even_ref
        out[n // 2, :, cols] = values[i * rows : (i + 1) * rows].astype(out.dtype)


def rows_kernel(
    info_ref, extra_ref, wg_ref, wu_ref, gu_in, odd_out, even_out, w_ref, gu_ref, total_ref,
    odd_ref, even_ref, w_sems, out_sems, *, experts
):
    exp_dev, width, _ = wg_ref.shape
    all_rows = gu_ref.shape[1]

    def operands(e):
        pairs = expert_parts(info_ref, wg_ref, wu_ref, w_ref, e)
        return describe(pairs + [(gu_in.at[e], gu_ref.at[e])], w_sems.at[e])

    for c in operands(0):
        c.start()
    found = extra_ref[...]
    high = found.astype(jnp.bfloat16).astype(jnp.float32)
    lower = (found - high).astype(jnp.bfloat16).astype(jnp.float32)
    put_rows(
        high + pltpu.roll(lower, experts, 1), 0, odd_ref, even_ref, slice(width, width + LANES)
    )
    total_ref[...] = jnp.zeros_like(total_ref)

    def one_expert(e, carry):
        wait_all(operands(e))
        for c in operands(e + 1):
            c.start()
        total_ref[...] += dot(gu_ref[e], w_ref[e], 1, 1)
        return carry

    lax.fori_loop(0, exp_dev - 1, one_expert, 0)
    wait_all(operands(exp_dev - 1))
    out_copies = []
    for t in range(2):
        part = slice(t * all_rows // 2, (t + 1) * all_rows // 2)
        new = total_ref[part, :] + dot(gu_ref[exp_dev - 1, part, :], w_ref[exp_dev - 1], 1, 1)
        put_rows(new, t, odd_ref, even_ref, slice(0, width))
        share = pl.ds(t * odd_ref.shape[0] // 2, odd_ref.shape[0] // 2)
        out_copies += start_copies(
            [(odd_ref.at[share], odd_out.at[share]), (even_ref.at[share], even_out.at[share])],
            out_sems.at[pl.ds(2 * t, 2)],
        )
    wait_all(out_copies)


def final_kernel(
    info_ref, sums_ref, arrived_ref, early_ref, late_ref, *rest, n_early, n_late
):
    dense = rest[:-10]
    gate_ref, up_ref, down_ref, wq_ref, wk_ref, wv_ref, wo_ref, router_ref, one_ref, two_ref = rest[-10:]
    exp_dev, rows, units = gate_ref.shape
    fh = units // 2
    half = info_ref[2]
    kept = sums_ref[pl.ds(pl.multiple_of(half * rows, rows), rows), :]
    got = arrived_ref[...]
    first = jnp.where(half == 0, kept, got).astype(jnp.float32)
    second = jnp.where(half == 0, got, kept).astype(jnp.float32)
    for e in range(exp_dev):
        at = 3 * e * fh
        gate_ref[e, :, :fh] = first[:, at : at + fh]
        gate_ref[e, :, fh:] = second[:, at : at + fh]
        up_ref[e, :, :fh] = first[:, at + fh : at + 2 * fh]
        up_ref[e, :, fh:] = second[:, at + fh : at + 2 * fh]
        at = (3 * e + 2) * fh
        down_ref[e, :fh, :] = first[:, at : at + fh].T
        down_ref[e, fh:, :] = second[:, at : at + fh].T
    early, late = early_ref[0], late_ref[0]
    for d in dense:
        early = early + d[:, :n_early].astype(jnp.float32)
        late = late + d[:, n_early:].astype(jnp.float32)
    width, k_cols = wo_ref.shape[1], wk_ref.shape[1]
    wo_ref[...] = early[:, :width]
    wq_ref[...] = early[:, width + LANES :]
    wk_ref[...] = late[:, :k_cols]
    wv_ref[...] = late[:, k_cols : 2 * k_cols]
    small = early[:, width : width + LANES]
    small = small.T
    router_ref[...] = small[1 : 1 + router_ref.shape[0], :]
    two_ref[...] = small[:1, :]
    one_ref[...] = late[:, 2 * k_cols :].T[:1, :]


def selection(info_ref, select_ref, own_rows):
    count, width = select_ref.shape
    groups = width // count
    row = lax.broadcasted_iota(jnp.int32, (count, width), 0)
    col = lax.broadcasted_iota(jnp.int32, (count, width), 1)
    want = ((row // own_rows) ^ info_ref[3]) * (own_rows * groups) + (
        info_ref[0] * own_rows + row % own_rows
    )
    select_ref[...] = jnp.where(col == want, 1.0, 0.0).astype(jnp.bfloat16)


def pick_small(blocks, rows, count, select):
    total = blocks[0][rows : rows + 2 * count].astype(jnp.float32)
    for b in blocks[1:]:
        total = total + b[rows : rows + 2 * count].astype(jnp.float32)
    total = jnp.concatenate(
        [total[:count] + total[count:], jnp.zeros((LANES - count, total.shape[1]), jnp.float32)],
        axis=0,
    )
    high = total.astype(jnp.bfloat16)
    lower = (total - high.astype(jnp.float32)).astype(jnp.bfloat16)
    return dot(select, high, 1, 1) + dot(select, lower, 1, 1)


def put_shares(values, odd_ref, even_ref, at):
    rows = odd_ref.shape[1]
    for n in range(2 * odd_ref.shape[0]):
        out = odd_ref if n % 2 else even_ref
        out[n // 2, :, at : at + values.shape[1]] = values[n * rows : (n + 1) * rows].astype(
            out.dtype
        )


def early_dense_kernel(info_ref, *rest, groups, count):
    normed, attended, branch, query = (rest[n * groups : (n + 1) * groups] for n in range(4))
    odd_ref, even_ref, normed_t_ref, select_ref = rest[4 * groups :]
    rows, width = normed[0].shape
    selection(info_ref, select_ref, odd_ref.shape[1])
    select = select_ref[...]

    def seq(blocks):
        return jnp.concatenate([b[:rows] for b in blocks], axis=0)

    normed_t = dot(select, seq(normed), 1, 1).astype(jnp.bfloat16)
    normed_t_ref[...] = normed_t
    attended_t = dot(select, seq(attended), 1, 1).astype(jnp.bfloat16)
    put_shares(dot(attended_t, seq(branch)), odd_ref, even_ref, 0)
    put_shares(pick_small(branch, rows, count, select), odd_ref, even_ref, width)
    put_shares(dot(normed_t, seq(query)), odd_ref, even_ref, width + LANES)


def late_dense_kernel(info_ref, normed_t_ref, *rest):
    blocks = rest[:-3]
    odd_ref, even_ref, select_ref = rest[-3:]
    rows = normed_t_ref.shape[1] // len(blocks)
    selection(info_ref, select_ref, odd_ref.shape[1])
    kv = jnp.concatenate([b[:rows] for b in blocks], axis=0)
    put_shares(dot(normed_t_ref[...], kv), odd_ref, even_ref, 0)
    put_shares(pick_small(blocks, rows, 1, select_ref[...]), odd_ref, even_ref, kv.shape[1])


def small_rows(count):
    return -(-2 * count // 16) * 16


def put_small(ref, start, values):
    count = values.shape[0]
    high = values.astype(jnp.bfloat16).astype(jnp.float32)
    fill = jnp.zeros((small_rows(count) - 2 * count, values.shape[1]), jnp.float32)
    ref[start:] = jnp.concatenate([high, values - high, fill], axis=0).astype(jnp.bfloat16)


def backward_kernel(
    info_ref, own_ref, gate_ref, cot_ref, n2_ref, hid_ref, router_ref, gain_ref, wo_ref, q_ref,
    lse_ref, cos_ref, sin_ref, k_hbm, v_hbm, wq_hbm, scaled_hbm, wd_hbm, *rest, experts
):
    arrived, outs = rest[:-18], rest[-18:]
    ghid_ref, branch_ref, dq_ref, odd_ref, even_ref, gn_ref, mix_odd_out, mix_even_out = outs[:8]
    (
        router_wide, k_ref, v_ref, wq_ref, scaled_ref, down_ref, mix_odd_ref, mix_even_ref, sems,
        mix_sems,
    ) = outs[8:]
    late = start_copies([(k_hbm, k_ref), (v_hbm, v_ref), (wq_hbm, wq_ref)], sems)
    exp_dev, units, _ = wd_hbm.shape
    fh = units // 2
    pairs = []
    for e in range(exp_dev):
        part = pl.ds(e * fh, fh)
        pairs += [(wd_hbm.at[e, own_half(info_ref, fh), :], down_ref.at[part, :])]
        pairs += [(scaled_hbm.at[e], scaled_ref.at[:, part])]
    mix_copies = start_copies(pairs, mix_sems)
    widen(router_ref, router_wide)
    rows, width = hid_ref.shape
    summed = own_ref[...]
    for a in arrived:
        summed = summed + a[...].astype(jnp.float32)
    extra = summed[:, width:]
    gate_grads = extra + pltpu.roll(extra, LANES - experts, 1)
    gate = gate_ref[...]
    grad_logits = (
        gate * (gate_grads - jnp.sum(gate * gate_grads, axis=-1, keepdims=True))
    ).astype(jnp.bfloat16)
    router_grad = dot(grad_logits, n2_ref[...], 0, 0)
    grad_normed = summed[:, :width] + dot(grad_logits, router_wide[...], 1, 1)
    hidden = hid_ref[...]
    inverse = lax.rsqrt(jnp.mean(hidden * hidden, axis=-1, keepdims=True) + norm_eps)
    back, norm_grad = norm_backward(hidden, inverse, gain_ref[...], grad_normed)
    grad_hidden = cot_ref[...].astype(jnp.float32) + back
    ghid_ref[...] = grad_hidden
    branch = grad_hidden.astype(jnp.bfloat16)
    branch_ref[:rows] = branch
    put_small(branch_ref, rows, jnp.concatenate([norm_grad, router_grad[:experts]], axis=0))
    grad_attended = dot(branch, wo_ref[...], 1, 1).astype(jnp.bfloat16)
    wait_all(late[:2])
    seq_len = k_ref.shape[1]
    allowed = allowed_mask(info_ref, seq_len, rows)
    cosine, sine = cos_ref[:rows, :], sin_ref[:rows, :]
    lane = lane_of((seq_len, LANES))
    kept = [None, None]
    for h in range(KV):
        cols = slice(h * LANES, (h + 1) * LANES)
        stacked = stack_heads(q_ref[:, cols])
        grad_stacked = stack_heads(grad_attended[:, cols])
        keys = k_ref[h]
        scores = jnp.where(allowed, dot(keys, stacked, 1, 1), masked_score)
        prob = jnp.exp(scores - lse_ref[h : h + 1, :])
        grad_prob = dot(v_ref[h], grad_stacked, 1, 1)
        delta = jnp.sum(prob * grad_prob, axis=0, keepdims=True)
        grad_scores = (prob * (grad_prob - delta)).astype(jnp.bfloat16)
        dq = join_heads(dot(grad_scores, keys, 0, 0)) * (1.0 / math.sqrt(HD))
        dq_ref[:, cols] = unrope(dq, cosine, sine).astype(jnp.bfloat16)
        parts = (dot(grad_scores, stacked), dot(prob.astype(jnp.bfloat16), grad_stacked))
        for n in range(2):
            both = parts[n] + pltpu.roll(parts[n], HD, 1)
            if h % 2 == 0:
                kept[n] = both
                continue
            pair = jnp.where(lane < HD, kept[n], both)
            start = (n * KV // 2 + h // 2) * LANES
            put_rows(pair, 0, odd_ref, even_ref, slice(start, start + LANES))
    wait_all(mix_copies)
    tokens = scaled_ref.shape[0] // 2
    out_copies = []
    for t in range(2):
        mix = dot(scaled_ref[t * tokens : (t + 1) * tokens, :], down_ref[...])
        put_rows(mix, t, mix_odd_ref, mix_even_ref, slice(0, width))
        share = pl.ds(t * mix_odd_ref.shape[0] // 2, mix_odd_ref.shape[0] // 2)
        out_copies += start_copies(
            [
                (mix_odd_ref.at[share], mix_odd_out.at[share]),
                (mix_even_ref.at[share], mix_even_out.at[share]),
            ],
            mix_sems.at[pl.ds(2 * t, 2)],
        )
    wait_all(late[2:])
    gn_ref[...] = dot(dq_ref[...], wq_ref[...], 1, 1)
    wait_all(out_copies)


def tokens_kernel(
    own_ref, gn_ref, wk_ref, wv_ref, tokens_ref, gain_ref, ghid_ref, cos_ref, sin_ref, *rest
):
    arrived, (kv_ref, out_ref) = rest[:-2], rest[-2:]
    rows = tokens_ref.shape[0]
    summed = own_ref[...]
    for a in arrived:
        summed = summed + a[...].astype(jnp.float32)
    k_cols = KV * HD
    for c in range(k_cols // LANES):
        cols = slice(c * LANES, (c + 1) * LANES)
        kv_ref[:rows, cols] = unrope(summed[:, cols], cos_ref[:rows, :], sin_ref[:rows, :]).astype(
            jnp.bfloat16
        )
    kv_ref[:rows, k_cols:] = summed[:, k_cols:].astype(jnp.bfloat16)
    grad_normed = (
        gn_ref[...]
        + dot(kv_ref[:rows, :k_cols], wk_ref[...], 1, 1)
        + dot(kv_ref[:rows, k_cols:], wv_ref[...], 1, 1)
    )
    source = tokens_ref[...].astype(jnp.float32)
    inverse = lax.rsqrt(jnp.mean(source * source, axis=-1, keepdims=True) + norm_eps)
    back, norm_grad = norm_backward(source, inverse, gain_ref[...], grad_normed)
    put_small(kv_ref, rows, norm_grad)
    out_ref[...] = (ghid_ref[...] + back).astype(jnp.bfloat16)


def call(kernel, out_shape, name, hbm=(), hbm_out=(), scratch=(), smem=True):
    def run(*args):
        specs = [
            pl.BlockSpec(memory_space=pl.ANY if n in hbm else pltpu.VMEM)
            for n in range(len(args))
        ]
        if smem:
            specs[0] = pl.BlockSpec(memory_space=pltpu.SMEM)
        return pl.pallas_call(
            kernel,
            out_shape=out_shape,
            in_specs=specs,
            out_specs=[
                pl.BlockSpec(memory_space=pl.ANY if n in hbm_out else pltpu.VMEM)
                for n in range(len(out_shape))
            ],
            scratch_shapes=list(scratch),
            compiler_params=pltpu.CompilerParams(vmem_limit_bytes=LIMIT_MIB * 1024 * 1024),
            name=name,
        )(*args)

    return run


def shape(*dims, dtype=jnp.bfloat16):
    return jax.ShapeDtypeStruct(dims, dtype)


def shards(
    tokens,
    prefix_len,
    routes,
    norm1_gain,
    w_query,
    w_key,
    w_value,
    w_output,
    norm2_gain,
    w_router,
    w_gate,
    w_up,
    w_down,
    cotangent,
):
    tok_rows, model_width = tokens.shape
    groups = lax.axis_size("expert")
    copies = lax.axis_size("dp")
    me = lax.axis_index("expert")
    half = lax.axis_index("dp") % 2
    exp_dev, _, hidden_units = w_gate.shape
    half_units = hidden_units // 2
    experts = exp_dev * groups
    f32 = jnp.float32
    seq_len = tok_rows * groups
    low = jnp.bfloat16

    def send(block, pair_flip, flip):
        return lax.ppermute(
            block,
            ("dp", "expert"),
            [
                (i * groups + j, (i ^ pair_flip) * groups + (j ^ flip))
                for i in range(copies)
                for j in range(groups)
            ],
        )

    def gather_even(block, pairs):
        return [
            block if (s, r) == (0, 0) else send(block, s, r)
            for s in range(pairs)
            for r in range(0, groups, 2)
        ]

    def gather_odd(even):
        out = []
        for b in even:
            out += [b, send(b, 0, 1)]
        return out

    def gather(block, pairs):
        return gather_odd(gather_even(block, pairs))

    def core_sum(odd, even):
        return even + send(odd, 0, 1).astype(jnp.float32)

    def swap(mine, pairs):
        mine = mine.astype(low)
        spots = [(s, r) for s in range(pairs) for r in range(0, groups, 2)]
        return [send(mine[n], *spots[n]) for n in range(1, len(spots))]

    tokens_f = tokens.astype(f32)
    normed1 = norm_forward(tokens_f, norm1_gain)[0].astype(low)
    normed1_even = gather_even(normed1, 1)
    cosine, sine = rope_tables(me, tok_rows, groups)
    cosine, sine, *normed1_even = lax.optimization_barrier((cosine, sine, *normed1_even))
    normed1_blocks = gather_odd(normed1_even)
    routed = jnp.any(
        routes[:, :, None] == jnp.arange(experts, dtype=jnp.int32)[None, None, :], axis=1
    )
    cot_mask = jnp.concatenate(
        [cotangent, jnp.pad(routed.astype(low), ((0, 0), (0, LANES - experts)))], axis=1
    )
    cot_mask, *normed1_even = lax.optimization_barrier((cot_mask, *normed1_even))
    cot_even = gather_even(cot_mask, 2)
    my_dp = lax.axis_index("dp")
    info = jnp.stack([me, prefix_len[0], half, my_dp]).astype(jnp.int32)
    gain_one, gain_two = norm1_gain[None], norm2_gain[None]

    query_pre = dot(normed1, w_query)
    q_low, k_two, v_two, lse, attended, hidden_state, normed2 = call(
        forward_kernel,
        (
            shape(tok_rows, H * HD),
            shape(KV, seq_len, LANES),
            shape(KV, seq_len, LANES),
            shape(KV, 2 * tok_rows, dtype=f32),
            shape(tok_rows, H * HD),
            shape(tok_rows, model_width, dtype=f32),
            shape(tok_rows, model_width),
        ),
        "attention_forward",
        hbm=(5,),
        scratch=(pltpu.VMEM((H * HD, model_width), low), pltpu.SemaphoreType.DMA((1,))),
    )(
        info, tokens, query_pre, w_key, w_value, w_output, gain_two, cosine, sine,
        *normed1_blocks,
    )

    normed2, *cot_even = lax.optimization_barrier((normed2, *cot_even))
    cot_blocks = gather_odd(cot_even)
    n2_blocks = gather(normed2, 2)
    attended_even = gather_even(attended, 1)
    n_blocks = 2 * groups
    all_rows = n_blocks * tok_rows
    wide = model_width + LANES

    dma = pltpu.SemaphoreType.DMA
    units = half_units * exp_dev
    sums, grad_gu, scaled, extra, gate_probs = call(
        lambda *refs: experts_kernel(*refs, n_blocks=n_blocks, tiles=2),
        (
            shape(model_width, 3 * units),
            shape(exp_dev, all_rows, 2 * half_units),
            shape(exp_dev, all_rows, half_units),
            shape(all_rows, LANES, dtype=f32),
            shape(tok_rows, LANES, dtype=f32),
        ),
        "experts",
        hbm=tuple(range(2, 5 + 2 * n_blocks)),
        hbm_out=(0, 1, 2),
        scratch=(
            pltpu.VMEM((all_rows, model_width), low),
            pltpu.VMEM((all_rows, model_width), low),
            pltpu.VMEM((all_rows, LANES), low),
            pltpu.VMEM((exp_dev, model_width, 2 * half_units), low),
            pltpu.VMEM((exp_dev, half_units, model_width), low),
            pltpu.VMEM((exp_dev, all_rows, 2 * half_units), low),
            pltpu.VMEM((exp_dev, all_rows, half_units), low),
            pltpu.VMEM((exp_dev, model_width, 3 * half_units), low),
            pltpu.VMEM((all_rows, LANES), f32),
            pltpu.VMEM((model_width, LANES), low),
            dma((n_blocks,)),
            dma((n_blocks,)),
            dma((n_blocks,)),
            dma((exp_dev, 3)),
            dma((exp_dev, 3)),
        ),
    )(info, w_router, w_gate, w_up, w_down, *n2_blocks, *cot_blocks)
    outer = copies // 2
    shard_rows = model_width // copies
    reduced = lax.psum_scatter(
        sums,
        "dp",
        scatter_dimension=0,
        axis_index_groups=[[2 * o + p for o in range(outer)] for p in range(2)],
        tiled=True,
    )

    odd, even = call(
        lambda *refs: rows_kernel(*refs, experts=experts),
        (shape(groups, tok_rows, wide), shape(groups, tok_rows, wide, dtype=f32)),
        "experts_rows",
        hbm=(2, 3, 4),
        hbm_out=(0, 1),
        scratch=(
            pltpu.VMEM((exp_dev, model_width, 2 * half_units), low),
            pltpu.VMEM((exp_dev, all_rows, 2 * half_units), low),
            pltpu.VMEM((all_rows, model_width), f32),
            pltpu.VMEM((groups, tok_rows, wide), low),
            pltpu.VMEM((groups, tok_rows, wide), f32),
            dma((exp_dev, 3)),
            dma((4,)),
        ),
    )(info, extra, w_gate, w_up, grad_gu)
    odd, *attended_even = lax.optimization_barrier((odd, *attended_even))
    mine = core_sum(odd, even)
    arrived = swap(mine, 2)
    attended_blocks = gather_odd(attended_even)

    (
        grad_hidden, grad_branch, grad_query, kv_odd, kv_even, grad_normed_q, mix_odd, mix_even
    ) = call(
        lambda *refs: backward_kernel(*refs, experts=experts),
        (
            shape(tok_rows, model_width, dtype=f32),
            shape(tok_rows + small_rows(experts + 1), model_width),
            shape(tok_rows, H * HD),
            shape(groups // 2, tok_rows, 2 * KV * HD),
            shape(groups // 2, tok_rows, 2 * KV * HD, dtype=f32),
            shape(tok_rows, model_width, dtype=f32),
            shape(groups, tok_rows, model_width),
            shape(groups, tok_rows, model_width, dtype=f32),
        ),
        "attention_backward",
        hbm=(13, 14, 15, 16, 17),
        hbm_out=(6, 7),
        scratch=(
            pltpu.VMEM((model_width, LANES), low),
            pltpu.VMEM((KV, seq_len, LANES), low),
            pltpu.VMEM((KV, seq_len, LANES), low),
            pltpu.VMEM((model_width, H * HD), low),
            pltpu.VMEM((all_rows, units), low),
            pltpu.VMEM((units, model_width), low),
            pltpu.VMEM((groups, tok_rows, model_width), low),
            pltpu.VMEM((groups, tok_rows, model_width), f32),
            dma((3,)),
            dma((2 * exp_dev,)),
        ),
    )(
        info, mine[0], gate_probs, cotangent, normed2, hidden_state, w_router, gain_two, w_output,
        q_low, lse, cosine, sine, k_two, v_two, w_query, scaled, w_down, *arrived,
    )
    kv_mine = core_sum(kv_odd, kv_even)
    kv_arrived = swap(kv_mine, 1)
    mix_odd, kv_mine = lax.optimization_barrier((mix_odd, kv_mine))
    mix_mine = core_sum(mix_odd, mix_even).reshape(2, groups // 2, tok_rows, model_width)
    mix_pair = mix_mine[0] + send(mix_mine[1].astype(low), 1, 0).astype(f32)
    query_later, grad_branch, *kv_arrived = lax.optimization_barrier(
        (grad_query, grad_branch, *kv_arrived)
    )
    branch_even = gather_even(grad_branch, 1)
    query_even = gather_even(query_later, 1)
    grad_kv, grad_tokens = call(
        tokens_kernel,
        (
            shape(tok_rows + small_rows(1), 2 * KV * HD),
            shape(tok_rows, model_width),
        ),
        "tokens_backward",
        smem=False,
    )(
        kv_mine[0], grad_normed_q, w_key, w_value, tokens, gain_one, grad_hidden, cosine, sine,
        *kv_arrived,
    )
    grad_kv, *later = lax.optimization_barrier((grad_kv, *branch_even, *query_even))
    kv_even_blocks = gather_even(grad_kv, 1)
    branch_blocks = gather_odd(later[: len(branch_even)])
    query_blocks = gather_odd(later[len(branch_even) :])
    mix_pair, *kv_even_blocks = lax.optimization_barrier((mix_pair, *kv_even_blocks))
    kv_blocks = gather_odd(kv_even_blocks)
    mixture = mix_pair[0]
    for a in swap(mix_pair, 1):
        mixture = mixture + a.astype(f32)
    block_out = (hidden_state + mixture).astype(low)

    own_rows = model_width // (copies * groups)
    n_early, n_late = model_width + LANES + H * HD, 2 * KV * HD + LANES
    select = pltpu.VMEM((copies * own_rows, model_width), low)
    early_odd, early_even, normed1_t = call(
        lambda *refs: early_dense_kernel(*refs, groups=groups, count=experts + 1),
        (
            shape(outer, own_rows, n_early),
            shape(outer, own_rows, n_early, dtype=f32),
            shape(copies * own_rows, seq_len),
        ),
        "dense_early",
        scratch=(select,),
    )(info, *normed1_blocks, *attended_blocks, *branch_blocks, *query_blocks)
    early = early_even + send(early_odd, 1, 0).astype(f32)
    late_odd, late_even = call(
        late_dense_kernel,
        (shape(outer, own_rows, n_late), shape(outer, own_rows, n_late, dtype=f32)),
        "dense_late",
        scratch=(select,),
    )(info, normed1_t, *kv_blocks)
    late = late_even + send(late_odd, 1, 0).astype(f32)
    dense_send = jnp.concatenate([early[1:].astype(low), late[1:].astype(low)], axis=2)

    swapped = send(
        lax.dynamic_slice_in_dim(reduced, (1 - half) * shard_rows, shard_rows, 0), 1, 0
    )
    _, dense_send = lax.optimization_barrier((reduced, dense_send))
    dense_arrived = [send(dense_send[o - 1], 2 * o, 0) for o in range(1, outer)]
    k_cols = KV * HD
    (
        grad_gate_w, grad_up_w, grad_down_w, grad_query_w, grad_key_w, grad_value_w,
        grad_output_w, grad_router, grad_norm1, grad_norm2,
    ) = call(
        lambda *refs: final_kernel(*refs, n_early=n_early, n_late=n_late),
        (
            shape(exp_dev, shard_rows, hidden_units, dtype=f32),
            shape(exp_dev, shard_rows, hidden_units, dtype=f32),
            shape(exp_dev, hidden_units, shard_rows, dtype=f32),
            shape(own_rows, H * HD, dtype=f32),
            shape(own_rows, k_cols, dtype=f32),
            shape(own_rows, k_cols, dtype=f32),
            shape(own_rows, model_width, dtype=f32),
            shape(experts, own_rows, dtype=f32),
            shape(1, own_rows, dtype=f32),
            shape(1, own_rows, dtype=f32),
        ),
        "place",
    )(info, reduced, swapped, early, late, *dense_arrived)
    return (
        block_out,
        grad_tokens,
        grad_norm1[0],
        grad_query_w,
        grad_key_w,
        grad_value_w,
        grad_output_w,
        grad_norm2[0],
        grad_router.T,
        grad_gate_w,
        grad_up_w,
        grad_down_w,
    )


def solution(mesh):
    return jax.shard_map(
        shards,
        mesh=mesh,
        in_specs=(
            P(("dp", "expert"), None),
            P("dp"),
            P(("dp", "expert"), None),
            P(),
            P(),
            P(),
            P(),
            P(),
            P(),
            P(),
            P("expert", None, None),
            P("expert", None, None),
            P("expert", None, None),
            P(("dp", "expert"), None),
        ),
        out_specs=(
            P(("dp", "expert"), None),
            P(("dp", "expert"), None),
            P(("dp", "expert")),
            P(("dp", "expert"), None),
            P(("dp", "expert"), None),
            P(("dp", "expert"), None),
            P(("dp", "expert"), None),
            P(("dp", "expert")),
            P(("dp", "expert"), None),
            P("expert", "dp", None),
            P("expert", "dp", None),
            P("expert", None, "dp"),
        ),
        check_vma=False,
    )
```

```python
import math

import jax
import jax.numpy as jnp
from jax import lax
from jax.experimental import pallas as pl
from jax.experimental.pallas import tpu as pltpu
from jax.sharding import PartitionSpec as P

H = 16
KV = 8
HD = 64


norm_eps = 1e-05
masked_score = -1e30


def rope_tables(me, tok_rows, groups):
    row = lax.broadcasted_iota(jnp.int32, (groups * tok_rows, LANES), 0)
    lane = lax.broadcasted_iota(jnp.int32, (groups * tok_rows, LANES), 1)
    position = ((row // tok_rows) ^ me) * tok_rows + row % tok_rows
    frequency = jnp.exp((lane % (HD // 2)).astype(jnp.float32) * (-2.0 * math.log(10000.0) / HD))
    angles = position.astype(jnp.float32) * frequency
    sine = jnp.sin(angles)
    return jnp.cos(angles), jnp.where(lane % HD < HD // 2, -sine, sine)


LANES = 128
LIMIT_MIB = 63


def norm_forward(source, gain_vec):
    inverse = lax.rsqrt(jnp.mean(source * source, axis=-1, keepdims=True) + norm_eps)
    return (source * inverse * gain_vec, inverse)


def norm_backward(source, inverse, gain_vec, upstream):
    weighted = upstream * gain_vec
    cubed = inverse * inverse * inverse
    back = inverse * weighted - source * cubed * jnp.mean(weighted * source, axis=-1, keepdims=True)
    return (back, jnp.sum(upstream * source * inverse, axis=0, keepdims=True))


def dot(left, right, left_dim=1, right_dim=0):
    return lax.dot_general(
        left, right, (((left_dim,), (right_dim,)), ((), ())), preferred_element_type=jnp.float32
    )


def lane_of(shape):
    return lax.broadcasted_iota(jnp.int32, shape, 1)


def swap_halves(source):
    lane = lane_of(source.shape)
    return jnp.where(
        lane % HD < HD // 2,
        pltpu.roll(source, LANES - HD // 2, 1),
        pltpu.roll(source, HD // 2, 1),
    )


def rope(source, cosine_table, sine_table):
    return source * cosine_table + swap_halves(source) * sine_table


def unrope(upstream, cosine_table, sine_table):
    return upstream * cosine_table - swap_halves(upstream) * sine_table


def twice(pair):
    lane = lane_of(pair.shape)
    other = pltpu.roll(pair, HD, 1)
    return (jnp.where(lane < HD, pair, other), jnp.where(lane < HD, other, pair))


def stack_heads(pair):
    lane = lane_of(pair.shape)
    zero = jnp.zeros_like(pair)
    return jnp.concatenate(
        [jnp.where(lane < HD, pair, zero), jnp.where(lane < HD, zero, pair)], axis=0
    )


def join_heads(stacked):
    rows = stacked.shape[0] // 2
    lane = lane_of((rows, LANES))
    return jnp.where(lane < HD, stacked[:rows], stacked[rows:])


def allowed_mask(info_ref, seq_len, rows):
    me, prefix = info_ref[0], info_ref[1]
    key = lax.broadcasted_iota(jnp.int32, (seq_len, 2 * rows), 0)
    query = lax.broadcasted_iota(jnp.int32, (seq_len, 2 * rows), 1) % rows + me * rows
    key_pos = ((key // rows) ^ me) * rows + key % rows
    return (key_pos <= query) | (key_pos < prefix)


def forward_kernel(
    info_ref, wq_ref, wk_ref, wv_ref, wo_ref, gain_one_ref, gain_two_ref, cos_ref, sin_ref, *rest
):
    blocks, outs = rest[:-11], rest[-11:]
    q_ref, k_ref, v_ref, lse_ref, att_ref, hid_ref, n2_ref, n1_ref, wq_held, wo_held, sems = outs
    copies = start_copies([(wq_ref, wq_held), (wo_ref, wo_held)], sems)
    tokens_ref = blocks[0]
    rows = tokens_ref.shape[0]
    seq_len = rows * len(blocks)
    for n, b in enumerate(blocks):
        n1_ref[n * rows : (n + 1) * rows, :] = norm_forward(
            b[...].astype(jnp.float32), gain_one_ref[...]
        )[0].astype(jnp.bfloat16)
    normed = n1_ref[...]
    cosine, sine = cos_ref[...], sin_ref[...]
    keys = dot(normed, wk_ref[...])
    values = dot(normed, wv_ref[...])
    for c in range(KV // 2):
        cols = slice(c * LANES, (c + 1) * LANES)
        first, second = twice(rope(keys[:, cols], cosine, sine))
        k_ref[2 * c] = first.astype(jnp.bfloat16)
        k_ref[2 * c + 1] = second.astype(jnp.bfloat16)
        first, second = twice(values[:, cols])
        v_ref[2 * c] = first.astype(jnp.bfloat16)
        v_ref[2 * c + 1] = second.astype(jnp.bfloat16)
    allowed = allowed_mask(info_ref, seq_len, rows)
    wait_all(copies[:1])
    query_pre = dot(n1_ref[:rows, :], wq_held[...])
    for h in range(KV):
        cols = slice(h * LANES, (h + 1) * LANES)
        query = rope(query_pre[:, cols], cosine[:rows], sine[:rows]) * (1.0 / math.sqrt(HD))
        q_ref[:, cols] = query.astype(jnp.bfloat16)
        stacked = stack_heads(query).astype(jnp.bfloat16)
        scores = jnp.where(allowed, dot(k_ref[h], stacked, 1, 1), masked_score)
        row_max = jnp.max(scores, axis=0, keepdims=True)
        exps = jnp.exp(scores - row_max)
        total = jnp.sum(exps, axis=0, keepdims=True)
        lse_ref[h : h + 1, :] = row_max + jnp.log(total)
        prob = (exps * (1.0 / total)).astype(jnp.bfloat16)
        att_ref[:, cols] = join_heads(dot(prob, v_ref[h], 0, 0)).astype(jnp.bfloat16)
    wait_all(copies[1:])
    hidden = tokens_ref[...].astype(jnp.float32) + dot(att_ref[...], wo_held[...])
    hid_ref[...] = hidden
    n2_ref[...] = norm_forward(hidden, gain_two_ref[...])[0].astype(jnp.bfloat16)


def start_copies(pairs, sems):
    copies = describe(pairs, sems)
    for c in copies:
        c.start()
    return copies


def wait_all(copies):
    for c in copies:
        c.wait()


def own_half(info_ref, fh):
    return pl.ds(pl.multiple_of(info_ref[2] * fh, fh), fh)


def expert_parts(info_ref, wg_ref, wu_ref, w_ref, e):
    fh = wg_ref.shape[2] // 2
    mine = own_half(info_ref, fh)
    return [
        (wg_ref.at[e, :, mine], w_ref.at[e, :, pl.ds(0, fh)]),
        (wu_ref.at[e, :, mine], w_ref.at[e, :, pl.ds(fh, fh)]),
    ]


def down_part(info_ref, wd_ref, down_ref, e):
    mine = own_half(info_ref, wd_ref.shape[1] // 2)
    return [(wd_ref.at[e, mine, :], down_ref.at[e])]


def describe(pairs, sems):
    return [pltpu.make_async_copy(src, dst, sems.at[n]) for n, (src, dst) in enumerate(pairs)]


def row_parts(blocks, into, cols):
    rows = blocks[0].shape[0]
    return [(b.at[:, cols], into.at[pl.ds(n * rows, rows), :]) for n, b in enumerate(blocks)]


def widen(router_ref, wide_ref):
    wide_ref[...] = jnp.zeros_like(wide_ref)
    wide_ref[:, : router_ref.shape[1]] = router_ref[...]


def routing(routed, logits):
    logits = jnp.where(routed, logits, masked_score)
    exps = jnp.where(routed, jnp.exp(logits - jnp.max(logits, axis=-1, keepdims=True)), 0.0)
    return exps / jnp.sum(exps, axis=-1, keepdims=True)


def experts_kernel(
    info_ref, router_ref, wg_ref, wu_ref, wd_ref, *rest, n_blocks, experts, tiles
):
    cot_blocks, n2_blocks = rest[:n_blocks], rest[n_blocks : 2 * n_blocks]
    sums_out, acts_out = rest[2 * n_blocks : 2 * n_blocks + 2]
    (
        n2_ref, g_ref, routed_ref, w_ref, down_ref, acts_ref, sums_ref, probs_ref, router_wide,
        extra_ref,
    ) = rest[2 * n_blocks + 2 : 2 * n_blocks + 12]
    n2_sems, routed_sems, g_sems, w_sems, out_sems = rest[2 * n_blocks + 12 :]
    exp_dev, width, units = wg_ref.shape
    rows = n2_blocks[0].shape[0]
    fh = units // 2
    n2_copies = start_copies(row_parts(n2_blocks, n2_ref, pl.ds(0, width)), n2_sems)
    routed_copies = start_copies(row_parts(cot_blocks, routed_ref, pl.ds(width, LANES)), routed_sems)

    def weights(e):
        pairs = expert_parts(info_ref, wg_ref, wu_ref, w_ref, e)
        return describe(pairs + down_part(info_ref, wd_ref, down_ref, e), w_sems.at[e])

    def results(e):
        two = pl.ds(pl.multiple_of(e * 3 * fh, fh), 2 * fh)
        one = pl.ds(pl.multiple_of((3 * e + 2) * fh, fh), fh)
        return describe(
            [
                (acts_ref.at[e], acts_out.at[e]),
                (sums_ref.at[e, :, pl.ds(0, 2 * fh)], sums_out.at[:, two]),
                (sums_ref.at[e, :, pl.ds(2 * fh, fh)], sums_out.at[:, one]),
            ],
            out_sems.at[e],
        )

    for c in weights(0):
        c.start()
    widen(router_ref, router_wide)
    extra_ref[...] = jnp.zeros_like(extra_ref)
    wait_all(n2_copies)
    wait_all(routed_copies)
    g_copies = start_copies(row_parts(cot_blocks, g_ref, pl.ds(0, width)), g_sems)
    probs_ref[...] = routing(
        routed_ref[...].astype(jnp.float32) > 0.5, dot(n2_ref[...], router_wide[...])
    )
    wait_all(g_copies)
    step = n2_ref.shape[0] // tiles

    def one_expert(e, carry):
        wait_all(weights(e))

        @pl.when(e + 1 < exp_dev)
        def _():
            for c in weights(e + 1):
                c.start()

        spot = info_ref[0] * exp_dev + e
        for t in range(tiles):
            part = slice(t * step, (t + 1) * step)
            pre = dot(n2_ref[part, :], w_ref[e])
            gate_pre, up_pre = pre[:, :fh], pre[:, fh:]
            back = dot(g_ref[part, :], down_ref[e], 1, 1)
            sig = 0.5 * jnp.tanh(0.5 * gate_pre) + 0.5
            silu = gate_pre * sig
            act = silu * up_pre
            here = lane_of((step, LANES)) == spot
            weight = jnp.sum(jnp.where(here, probs_ref[part, :], 0.0), axis=1, keepdims=True)
            extra_ref[part, :] += jnp.where(here, jnp.sum(act * back, axis=1, keepdims=True), 0.0)
            grad_active = weight * back
            acts_ref[e, part, :fh] = (
                grad_active * up_pre * (sig + silu * (1.0 - sig))
            ).astype(jnp.bfloat16)
            acts_ref[e, part, fh : 2 * fh] = (grad_active * silu).astype(jnp.bfloat16)
            acts_ref[e, part, 2 * fh : 3 * fh] = (weight * act).astype(jnp.bfloat16)
            found = extra_ref[part, :]
            high = found.astype(jnp.bfloat16).astype(jnp.float32)
            lower = (found - high).astype(jnp.bfloat16).astype(jnp.float32)
            acts_ref[e, part, 3 * fh :] = (high + pltpu.roll(lower, experts, 1)).astype(
                jnp.bfloat16
            )
        leaving = results(e)
        leaving[0].start()
        sums_ref[e, :, : 2 * fh] = dot(n2_ref[...], acts_ref[e, :, : 2 * fh], 0, 0).astype(
            jnp.bfloat16
        )
        leaving[1].start()
        sums_ref[e, :, 2 * fh :] = dot(g_ref[...], acts_ref[e, :, 2 * fh : 3 * fh], 0, 0).astype(
            jnp.bfloat16
        )
        leaving[2].start()
        return carry

    lax.fori_loop(0, exp_dev, one_expert, 0)
    for e in range(exp_dev):
        wait_all(results(e))


def put_rows(values, t, odd_ref, even_ref, cols):
    rows = odd_ref.shape[1]
    count = values.shape[0] // rows
    for i in range(count):
        n = t * count + i
        out = odd_ref if n % 2 else even_ref
        out[n // 2, :, cols] = values[i * rows : (i + 1) * rows].astype(out.dtype)


def rows_kernel(
    info_ref, wg_ref, wu_ref, acts_in, odd_out, even_out, w_ref, gu_ref, total_ref, extra_ref,
    odd_ref, even_ref, w_sems, out_sems, extra_sems
):
    exp_dev, width, _ = wg_ref.shape
    all_rows, two = gu_ref.shape[1:]
    extra_part = pl.ds(3 * two // 2, LANES)
    extra_copy = start_copies([(acts_in.at[exp_dev - 1, :, extra_part], extra_ref)], extra_sems)

    def operands(e):
        pairs = expert_parts(info_ref, wg_ref, wu_ref, w_ref, e)
        acts = acts_in.at[e, :, pl.ds(0, two)]
        return describe(pairs + [(acts, gu_ref.at[e])], w_sems.at[e])

    for c in operands(0):
        c.start()
    wait_all(extra_copy)
    put_rows(
        extra_ref[...].astype(jnp.float32), 0, odd_ref, even_ref, slice(width, width + LANES)
    )
    total_ref[...] = jnp.zeros_like(total_ref)

    def one_expert(e, carry):
        wait_all(operands(e))
        for c in operands(e + 1):
            c.start()
        total_ref[...] += dot(gu_ref[e], w_ref[e], 1, 1)
        return carry

    lax.fori_loop(0, exp_dev - 1, one_expert, 0)
    wait_all(operands(exp_dev - 1))
    out_copies = []
    for t in range(2):
        part = slice(t * all_rows // 2, (t + 1) * all_rows // 2)
        new = total_ref[part, :] + dot(gu_ref[exp_dev - 1, part, :], w_ref[exp_dev - 1], 1, 1)
        put_rows(new, t, odd_ref, even_ref, slice(0, width))
        share = pl.ds(t * odd_ref.shape[0] // 2, odd_ref.shape[0] // 2)
        out_copies += start_copies(
            [(odd_ref.at[share], odd_out.at[share]), (even_ref.at[share], even_out.at[share])],
            out_sems.at[pl.ds(2 * t, 2)],
        )
    wait_all(out_copies)


def final_kernel(
    info_ref, sums_ref, arrived_ref, early_ref, late_ref, *rest, n_early, n_late
):
    dense = rest[:-10]
    gate_ref, up_ref, down_ref, wq_ref, wk_ref, wv_ref, wo_ref, router_ref, one_ref, two_ref = rest[-10:]
    exp_dev, rows, units = gate_ref.shape
    fh = units // 2
    half = info_ref[2]
    kept = sums_ref[pl.ds(pl.multiple_of(half * rows, rows), rows), :]
    got = arrived_ref[...]
    first = jnp.where(half == 0, kept, got).astype(jnp.float32)
    second = jnp.where(half == 0, got, kept).astype(jnp.float32)
    for e in range(exp_dev):
        at = 3 * e * fh
        gate_ref[e, :, :fh] = first[:, at : at + fh]
        gate_ref[e, :, fh:] = second[:, at : at + fh]
        up_ref[e, :, :fh] = first[:, at + fh : at + 2 * fh]
        up_ref[e, :, fh:] = second[:, at + fh : at + 2 * fh]
        at = (3 * e + 2) * fh
        down_ref[e, :fh, :] = first[:, at : at + fh].T
        down_ref[e, fh:, :] = second[:, at : at + fh].T
    early, late = early_ref[0], late_ref[0]
    for d in dense:
        early = early + d[:, :n_early].astype(jnp.float32)
        late = late + d[:, n_early:].astype(jnp.float32)
    width, k_cols = wo_ref.shape[1], wk_ref.shape[1]
    wo_ref[...] = early[:, :width]
    wq_ref[...] = early[:, width + LANES :]
    wk_ref[...] = late[:, :k_cols]
    wv_ref[...] = late[:, k_cols : 2 * k_cols]
    small = early[:, width : width + LANES]
    small = small.T
    router_ref[...] = small[1 : 1 + router_ref.shape[0], :]
    two_ref[...] = small[:1, :]
    one_ref[...] = late[:, 2 * k_cols :].T[:1, :]


def selection(info_ref, select_ref, own_rows):
    count, width = select_ref.shape
    groups = width // count
    row = lax.broadcasted_iota(jnp.int32, (count, width), 0)
    col = lax.broadcasted_iota(jnp.int32, (count, width), 1)
    want = ((row // own_rows) ^ info_ref[3]) * (own_rows * groups) + (
        info_ref[0] * own_rows + row % own_rows
    )
    select_ref[...] = jnp.where(col == want, 1.0, 0.0).astype(jnp.bfloat16)


def pick_small(blocks, rows, count, select):
    total = blocks[0][rows : rows + 2 * count].astype(jnp.float32)
    for b in blocks[1:]:
        total = total + b[rows : rows + 2 * count].astype(jnp.float32)
    total = jnp.concatenate(
        [total[:count] + total[count:], jnp.zeros((LANES - count, total.shape[1]), jnp.float32)],
        axis=0,
    )
    high = total.astype(jnp.bfloat16)
    lower = (total - high.astype(jnp.float32)).astype(jnp.bfloat16)
    return dot(select, high, 1, 1) + dot(select, lower, 1, 1)


def put_shares(values, odd_ref, even_ref, at):
    rows = odd_ref.shape[1]
    for n in range(2 * odd_ref.shape[0]):
        out = odd_ref if n % 2 else even_ref
        out[n // 2, :, at : at + values.shape[1]] = values[n * rows : (n + 1) * rows].astype(
            out.dtype
        )


def early_dense_kernel(info_ref, *rest, groups, count):
    attended, branch, query = (rest[1 + n * groups : 1 + (n + 1) * groups] for n in range(3))
    odd_ref, even_ref, normed_t_ref, select_ref = rest[1 + 3 * groups :]
    rows, width = attended[0].shape
    selection(info_ref, select_ref, odd_ref.shape[1])
    select = select_ref[...]

    def seq(blocks):
        return jnp.concatenate([b[:rows] for b in blocks], axis=0)

    normed_t = dot(select, rest[0][...], 1, 1).astype(jnp.bfloat16)
    normed_t_ref[...] = normed_t
    attended_t = dot(select, seq(attended), 1, 1).astype(jnp.bfloat16)
    put_shares(dot(attended_t, seq(branch)), odd_ref, even_ref, 0)
    put_shares(pick_small(branch, rows, count, select), odd_ref, even_ref, width)
    put_shares(dot(normed_t, seq(query)), odd_ref, even_ref, width + LANES)


def late_dense_kernel(info_ref, normed_t_ref, *rest):
    blocks = rest[:-3]
    odd_ref, even_ref, select_ref = rest[-3:]
    rows = normed_t_ref.shape[1] // len(blocks)
    selection(info_ref, select_ref, odd_ref.shape[1])
    kv = jnp.concatenate([b[:rows] for b in blocks], axis=0)
    put_shares(dot(normed_t_ref[...], kv), odd_ref, even_ref, 0)
    put_shares(pick_small(blocks, rows, 1, select_ref[...]), odd_ref, even_ref, kv.shape[1])


def small_rows(count):
    return -(-2 * count // 16) * 16


def put_small(ref, start, values):
    count = values.shape[0]
    high = values.astype(jnp.bfloat16).astype(jnp.float32)
    fill = jnp.zeros((small_rows(count) - 2 * count, values.shape[1]), jnp.float32)
    ref[start:] = jnp.concatenate([high, values - high, fill], axis=0).astype(jnp.bfloat16)


def backward_kernel(
    info_ref, own_ref, cot_ref, n2_ref, hid_ref, router_ref, gain_ref, wo_ref, q_ref,
    lse_ref, cos_ref, sin_ref, k_hbm, v_hbm, wq_hbm, acts_hbm, wd_hbm, *rest, experts
):
    arrived, outs = rest[:-18], rest[-18:]
    ghid_ref, branch_ref, dq_ref, odd_ref, even_ref, gn_ref, mix_odd_out, mix_even_out = outs[:8]
    (
        router_wide, k_ref, v_ref, wq_ref, scaled_ref, down_ref, mix_odd_ref, mix_even_ref, sems,
        mix_sems,
    ) = outs[8:]
    late = start_copies([(k_hbm, k_ref), (v_hbm, v_ref), (wq_hbm, wq_ref)], sems)
    exp_dev, units, _ = wd_hbm.shape
    fh = units // 2
    pairs = []
    for e in range(exp_dev):
        part = pl.ds(e * fh, fh)
        pairs += [(wd_hbm.at[e, own_half(info_ref, fh), :], down_ref.at[part, :])]
        pairs += [(acts_hbm.at[e, :, pl.ds(2 * fh, fh)], scaled_ref.at[:, part])]
    mix_copies = start_copies(pairs, mix_sems)
    widen(router_ref, router_wide)
    rows, width = hid_ref.shape
    summed = own_ref[...]
    for a in arrived:
        summed = summed + a[...].astype(jnp.float32)
    extra = summed[:, width:]
    gate_grads = extra + pltpu.roll(extra, LANES - experts, 1)
    routed = cot_ref[:, width:].astype(jnp.float32) > 0.5
    gate = routing(routed, dot(n2_ref[...], router_wide[...]))
    grad_logits = (
        gate * (gate_grads - jnp.sum(gate * gate_grads, axis=-1, keepdims=True))
    ).astype(jnp.bfloat16)
    router_grad = dot(grad_logits, n2_ref[...], 0, 0)
    grad_normed = summed[:, :width] + dot(grad_logits, router_wide[...], 1, 1)
    hidden = hid_ref[...]
    inverse = lax.rsqrt(jnp.mean(hidden * hidden, axis=-1, keepdims=True) + norm_eps)
    back, norm_grad = norm_backward(hidden, inverse, gain_ref[...], grad_normed)
    grad_hidden = cot_ref[:, :width].astype(jnp.float32) + back
    ghid_ref[...] = grad_hidden
    branch = grad_hidden.astype(jnp.bfloat16)
    branch_ref[:rows] = branch
    put_small(branch_ref, rows, jnp.concatenate([norm_grad, router_grad[:experts]], axis=0))
    grad_attended = dot(branch, wo_ref[...], 1, 1).astype(jnp.bfloat16)
    wait_all(late[:2])
    seq_len = k_ref.shape[1]
    allowed = allowed_mask(info_ref, seq_len, rows)
    cosine, sine = cos_ref[:rows, :], sin_ref[:rows, :]
    lane = lane_of((seq_len, LANES))
    kept = [None, None]
    for h in range(KV):
        cols = slice(h * LANES, (h + 1) * LANES)
        stacked = stack_heads(q_ref[:, cols])
        grad_stacked = stack_heads(grad_attended[:, cols])
        keys = k_ref[h]
        scores = jnp.where(allowed, dot(keys, stacked, 1, 1), masked_score)
        prob = jnp.exp(scores - lse_ref[h : h + 1, :])
        grad_prob = dot(v_ref[h], grad_stacked, 1, 1)
        delta = jnp.sum(prob * grad_prob, axis=0, keepdims=True)
        grad_scores = (prob * (grad_prob - delta)).astype(jnp.bfloat16)
        dq = join_heads(dot(grad_scores, keys, 0, 0)) * (1.0 / math.sqrt(HD))
        dq_ref[:, cols] = unrope(dq, cosine, sine).astype(jnp.bfloat16)
        parts = (dot(grad_scores, stacked), dot(prob.astype(jnp.bfloat16), grad_stacked))
        for n in range(2):
            both = parts[n] + pltpu.roll(parts[n], HD, 1)
            if h % 2 == 0:
                kept[n] = both
                continue
            pair = jnp.where(lane < HD, kept[n], both)
            start = (n * KV // 2 + h // 2) * LANES
            put_rows(pair, 0, odd_ref, even_ref, slice(start, start + LANES))
    wait_all(mix_copies)
    tokens = scaled_ref.shape[0] // 2
    out_copies = []
    for t in range(2):
        mix = dot(scaled_ref[t * tokens : (t + 1) * tokens, :], down_ref[...])
        put_rows(mix, t, mix_odd_ref, mix_even_ref, slice(0, width))
        share = pl.ds(t * mix_odd_ref.shape[0] // 2, mix_odd_ref.shape[0] // 2)
        out_copies += start_copies(
            [
                (mix_odd_ref.at[share], mix_odd_out.at[share]),
                (mix_even_ref.at[share], mix_even_out.at[share]),
            ],
            mix_sems.at[pl.ds(2 * t, 2)],
        )
    wait_all(late[2:])
    gn_ref[...] = dot(dq_ref[...], wq_ref[...], 1, 1)
    wait_all(out_copies)


def tokens_kernel(
    own_ref, gn_ref, wk_ref, wv_ref, tokens_ref, gain_ref, ghid_ref, cos_ref, sin_ref, *rest
):
    arrived, (kv_ref, out_ref) = rest[:-2], rest[-2:]
    rows = tokens_ref.shape[0]
    summed = own_ref[...]
    for a in arrived:
        summed = summed + a[...].astype(jnp.float32)
    k_cols = KV * HD
    for c in range(k_cols // LANES):
        cols = slice(c * LANES, (c + 1) * LANES)
        kv_ref[:rows, cols] = unrope(summed[:, cols], cos_ref[:rows, :], sin_ref[:rows, :]).astype(
            jnp.bfloat16
        )
    kv_ref[:rows, k_cols:] = summed[:, k_cols:].astype(jnp.bfloat16)
    grad_normed = (
        gn_ref[...]
        + dot(kv_ref[:rows, :k_cols], wk_ref[...], 1, 1)
        + dot(kv_ref[:rows, k_cols:], wv_ref[...], 1, 1)
    )
    source = tokens_ref[...].astype(jnp.float32)
    inverse = lax.rsqrt(jnp.mean(source * source, axis=-1, keepdims=True) + norm_eps)
    back, norm_grad = norm_backward(source, inverse, gain_ref[...], grad_normed)
    put_small(kv_ref, rows, norm_grad)
    out_ref[...] = (ghid_ref[...] + back).astype(jnp.bfloat16)


def call(kernel, out_shape, name, hbm=(), hbm_out=(), scratch=(), smem=True, limit=LIMIT_MIB):
    def run(*args):
        specs = [
            pl.BlockSpec(memory_space=pl.ANY if n in hbm else pltpu.VMEM)
            for n in range(len(args))
        ]
        if smem:
            specs[0] = pl.BlockSpec(memory_space=pltpu.SMEM)
        return pl.pallas_call(
            kernel,
            out_shape=out_shape,
            in_specs=specs,
            out_specs=[
                pl.BlockSpec(memory_space=pl.ANY if n in hbm_out else pltpu.VMEM)
                for n in range(len(out_shape))
            ],
            scratch_shapes=list(scratch),
            compiler_params=pltpu.CompilerParams(vmem_limit_bytes=limit * 1024 * 1024),
            name=name,
        )(*args)

    return run


def shape(*dims, dtype=jnp.bfloat16):
    return jax.ShapeDtypeStruct(dims, dtype)


def shards(
    tokens,
    prefix_len,
    routes,
    norm1_gain,
    w_query,
    w_key,
    w_value,
    w_output,
    norm2_gain,
    w_router,
    w_gate,
    w_up,
    w_down,
    cotangent,
):
    tok_rows, model_width = tokens.shape
    groups = lax.axis_size("expert")
    copies = lax.axis_size("dp")
    me = lax.axis_index("expert")
    half = lax.axis_index("dp") % 2
    exp_dev, _, hidden_units = w_gate.shape
    half_units = hidden_units // 2
    experts = exp_dev * groups
    f32 = jnp.float32
    seq_len = tok_rows * groups
    low = jnp.bfloat16

    def send(block, pair_flip, flip):
        return lax.ppermute(
            block,
            ("dp", "expert"),
            [
                (i * groups + j, (i ^ pair_flip) * groups + (j ^ flip))
                for i in range(copies)
                for j in range(groups)
            ],
        )

    def gather_even(block, pairs):
        return [
            block if (s, r) == (0, 0) else send(block, s, r)
            for s in range(pairs)
            for r in range(0, groups, 2)
        ]

    def gather_odd(even):
        out = []
        for b in even:
            out += [b, send(b, 0, 1)]
        return out

    def gather(block, pairs):
        return gather_odd(gather_even(block, pairs))

    def core_sum(odd, even):
        return even + send(odd, 0, 1).astype(jnp.float32)

    def swap(mine, pairs):
        mine = mine.astype(low)
        spots = [(s, r) for s in range(pairs) for r in range(0, groups, 2)]
        return [send(mine[n], *spots[n]) for n in range(1, len(spots))]

    tokens_even = gather_even(tokens, 1)
    cosine, sine = rope_tables(me, tok_rows, groups)
    cosine, sine, *tokens_even = lax.optimization_barrier((cosine, sine, *tokens_even))
    tokens_blocks = gather_odd(tokens_even)
    routed = jnp.any(
        routes[:, :, None] == jnp.arange(experts, dtype=jnp.int32)[None, None, :], axis=1
    )
    cot_mask = jnp.concatenate(
        [cotangent, jnp.pad(routed.astype(low), ((0, 0), (0, LANES - experts)))], axis=1
    )
    cot_mask, *tokens_even = lax.optimization_barrier((cot_mask, *tokens_even))
    cot_even = gather_even(cot_mask, 2)
    my_dp = lax.axis_index("dp")
    info = jnp.stack([me, prefix_len[0], half, my_dp]).astype(jnp.int32)
    gain_one, gain_two = norm1_gain[None], norm2_gain[None]

    q_low, k_two, v_two, lse, attended, hidden_state, normed2, normed1_all = call(
        forward_kernel,
        (
            shape(tok_rows, H * HD),
            shape(KV, seq_len, LANES),
            shape(KV, seq_len, LANES),
            shape(KV, 2 * tok_rows, dtype=f32),
            shape(tok_rows, H * HD),
            shape(tok_rows, model_width, dtype=f32),
            shape(tok_rows, model_width),
            shape(seq_len, model_width),
        ),
        "attention_forward",
        hbm=(1, 4),
        scratch=(
            pltpu.VMEM((model_width, H * HD), low),
            pltpu.VMEM((H * HD, model_width), low),
            pltpu.SemaphoreType.DMA((2,)),
        ),
    )(
        info, w_query, w_key, w_value, w_output, gain_one, gain_two, cosine, sine, *tokens_blocks,
    )

    normed2, *cot_even = lax.optimization_barrier((normed2, *cot_even))
    cot_blocks = gather_odd(cot_even)
    n2_blocks = gather(normed2, 2)
    attended_even = gather_even(attended, 1)
    n_blocks = 2 * groups
    all_rows = n_blocks * tok_rows
    wide = model_width + LANES

    dma = pltpu.SemaphoreType.DMA
    units = half_units * exp_dev
    wide_acts = 3 * half_units + LANES
    sums, acts = call(
        lambda *refs: experts_kernel(*refs, n_blocks=n_blocks, experts=experts, tiles=2),
        (
            shape(model_width, 3 * units),
            shape(exp_dev, all_rows, wide_acts),
        ),
        "experts",
        limit=48 if all_rows <= 1024 else LIMIT_MIB,
        hbm=tuple(range(2, 5 + 2 * n_blocks)),
        hbm_out=(0, 1),
        scratch=(
            pltpu.VMEM((all_rows, model_width), low),
            pltpu.VMEM((all_rows, model_width), low),
            pltpu.VMEM((all_rows, LANES), low),
            pltpu.VMEM((exp_dev, model_width, 2 * half_units), low),
            pltpu.VMEM((exp_dev, half_units, model_width), low),
            pltpu.VMEM((exp_dev, all_rows, wide_acts), low),
            pltpu.VMEM((exp_dev, model_width, 3 * half_units), low),
            pltpu.VMEM((all_rows, LANES), f32),
            pltpu.VMEM((model_width, LANES), low),
            pltpu.VMEM((all_rows, LANES), f32),
            dma((n_blocks,)),
            dma((n_blocks,)),
            dma((n_blocks,)),
            dma((exp_dev, 3)),
            dma((exp_dev, 3)),
        ),
    )(info, w_router, w_gate, w_up, w_down, *cot_blocks, *n2_blocks)
    outer = copies // 2
    shard_rows = model_width // copies
    reduced = lax.psum_scatter(
        sums,
        "dp",
        scatter_dimension=0,
        axis_index_groups=[[2 * o + p for o in range(outer)] for p in range(2)],
        tiled=True,
    )

    odd, even = call(
        rows_kernel,
        (shape(groups, tok_rows, wide), shape(groups, tok_rows, wide, dtype=f32)),
        "experts_rows",
        hbm=(1, 2, 3),
        hbm_out=(0, 1),
        scratch=(
            pltpu.VMEM((exp_dev, model_width, 2 * half_units), low),
            pltpu.VMEM((exp_dev, all_rows, 2 * half_units), low),
            pltpu.VMEM((all_rows, model_width), f32),
            pltpu.VMEM((all_rows, LANES), low),
            pltpu.VMEM((groups, tok_rows, wide), low),
            pltpu.VMEM((groups, tok_rows, wide), f32),
            dma((exp_dev, 3)),
            dma((4,)),
            dma((1,)),
        ),
    )(info, w_gate, w_up, acts)
    odd, *attended_even = lax.optimization_barrier((odd, *attended_even))
    mine = core_sum(odd, even)
    arrived = swap(mine, 2)
    attended_blocks = gather_odd(attended_even)

    (
        grad_hidden, grad_branch, grad_query, kv_odd, kv_even, grad_normed_q, mix_odd, mix_even
    ) = call(
        lambda *refs: backward_kernel(*refs, experts=experts),
        (
            shape(tok_rows, model_width, dtype=f32),
            shape(tok_rows + small_rows(experts + 1), model_width),
            shape(tok_rows, H * HD),
            shape(groups // 2, tok_rows, 2 * KV * HD),
            shape(groups // 2, tok_rows, 2 * KV * HD, dtype=f32),
            shape(tok_rows, model_width, dtype=f32),
            shape(groups, tok_rows, model_width),
            shape(groups, tok_rows, model_width, dtype=f32),
        ),
        "attention_backward",
        hbm=(12, 13, 14, 15, 16),
        hbm_out=(6, 7),
        scratch=(
            pltpu.VMEM((model_width, LANES), low),
            pltpu.VMEM((KV, seq_len, LANES), low),
            pltpu.VMEM((KV, seq_len, LANES), low),
            pltpu.VMEM((model_width, H * HD), low),
            pltpu.VMEM((all_rows, units), low),
            pltpu.VMEM((units, model_width), low),
            pltpu.VMEM((groups, tok_rows, model_width), low),
            pltpu.VMEM((groups, tok_rows, model_width), f32),
            dma((3,)),
            dma((2 * exp_dev,)),
        ),
    )(
        info, mine[0], cot_mask, normed2, hidden_state, w_router, gain_two, w_output,
        q_low, lse, cosine, sine, k_two, v_two, w_query, acts, w_down, *arrived,
    )
    kv_mine = core_sum(kv_odd, kv_even)
    kv_arrived = swap(kv_mine, 1)
    mix_odd, kv_mine = lax.optimization_barrier((mix_odd, kv_mine))
    mix_mine = core_sum(mix_odd, mix_even).reshape(2, groups // 2, tok_rows, model_width)
    mix_pair = mix_mine[0] + send(mix_mine[1].astype(low), 1, 0).astype(f32)
    query_later, grad_branch, *kv_arrived = lax.optimization_barrier(
        (grad_query, grad_branch, *kv_arrived)
    )
    branch_even = gather_even(grad_branch, 1)
    query_even = gather_even(query_later, 1)
    grad_kv, grad_tokens = call(
        tokens_kernel,
        (
            shape(tok_rows + small_rows(1), 2 * KV * HD),
            shape(tok_rows, model_width),
        ),
        "tokens_backward",
        smem=False,
    )(
        kv_mine[0], grad_normed_q, w_key, w_value, tokens, gain_one, grad_hidden, cosine, sine,
        *kv_arrived,
    )
    grad_kv, *later = lax.optimization_barrier((grad_kv, *branch_even, *query_even))
    kv_even_blocks = gather_even(grad_kv, 1)
    branch_blocks = gather_odd(later[: len(branch_even)])
    query_blocks = gather_odd(later[len(branch_even) :])
    mix_pair, *kv_even_blocks = lax.optimization_barrier((mix_pair, *kv_even_blocks))
    kv_blocks = gather_odd(kv_even_blocks)
    mixture = mix_pair[0]
    for a in swap(mix_pair, 1):
        mixture = mixture + a.astype(f32)
    block_out = (hidden_state + mixture).astype(low)

    own_rows = model_width // (copies * groups)
    n_early, n_late = model_width + LANES + H * HD, 2 * KV * HD + LANES
    select = pltpu.VMEM((copies * own_rows, model_width), low)
    early_odd, early_even, normed1_t = call(
        lambda *refs: early_dense_kernel(*refs, groups=groups, count=experts + 1),
        (
            shape(outer, own_rows, n_early),
            shape(outer, own_rows, n_early, dtype=f32),
            shape(copies * own_rows, seq_len),
        ),
        "dense_early",
        scratch=(select,),
    )(info, normed1_all, *attended_blocks, *branch_blocks, *query_blocks)
    early = early_even + send(early_odd, 1, 0).astype(f32)
    late_odd, late_even = call(
        late_dense_kernel,
        (shape(outer, own_rows, n_late), shape(outer, own_rows, n_late, dtype=f32)),
        "dense_late",
        scratch=(select,),
    )(info, normed1_t, *kv_blocks)
    late = late_even + send(late_odd, 1, 0).astype(f32)
    dense_send = jnp.concatenate([early[1:].astype(low), late[1:].astype(low)], axis=2)

    swapped = send(
        lax.dynamic_slice_in_dim(reduced, (1 - half) * shard_rows, shard_rows, 0), 1, 0
    )
    _, dense_send = lax.optimization_barrier((reduced, dense_send))
    dense_arrived = [send(dense_send[o - 1], 2 * o, 0) for o in range(1, outer)]
    k_cols = KV * HD
    (
        grad_gate_w, grad_up_w, grad_down_w, grad_query_w, grad_key_w, grad_value_w,
        grad_output_w, grad_router, grad_norm1, grad_norm2,
    ) = call(
        lambda *refs: final_kernel(*refs, n_early=n_early, n_late=n_late),
        (
            shape(exp_dev, shard_rows, hidden_units, dtype=f32),
            shape(exp_dev, shard_rows, hidden_units, dtype=f32),
            shape(exp_dev, hidden_units, shard_rows, dtype=f32),
            shape(own_rows, H * HD, dtype=f32),
            shape(own_rows, k_cols, dtype=f32),
            shape(own_rows, k_cols, dtype=f32),
            shape(own_rows, model_width, dtype=f32),
            shape(experts, own_rows, dtype=f32),
            shape(1, own_rows, dtype=f32),
            shape(1, own_rows, dtype=f32),
        ),
        "place",
    )(info, reduced, swapped, early, late, *dense_arrived)
    return (
        block_out,
        grad_tokens,
        grad_norm1[0],
        grad_query_w,
        grad_key_w,
        grad_value_w,
        grad_output_w,
        grad_norm2[0],
        grad_router.T,
        grad_gate_w,
        grad_up_w,
        grad_down_w,
    )


def solution(mesh):
    return jax.shard_map(
        shards,
        mesh=mesh,
        in_specs=(
            P(("dp", "expert"), None),
            P("dp"),
            P(("dp", "expert"), None),
            P(),
            P(),
            P(),
            P(),
            P(),
            P(),
            P(),
            P("expert", None, None),
            P("expert", None, None),
            P("expert", None, None),
            P(("dp", "expert"), None),
        ),
        out_specs=(
            P(("dp", "expert"), None),
            P(("dp", "expert"), None),
            P(("dp", "expert")),
            P(("dp", "expert"), None),
            P(("dp", "expert"), None),
            P(("dp", "expert"), None),
            P(("dp", "expert"), None),
            P(("dp", "expert")),
            P(("dp", "expert"), None),
            P("expert", "dp", None),
            P("expert", "dp", None),
            P("expert", None, "dp"),
        ),
        check_vma=False,
    )
```

```python
import math

import jax
import jax.numpy as jnp
from jax import lax
from jax.experimental import pallas as pl
from jax.experimental.pallas import tpu as pltpu
from jax.sharding import PartitionSpec as P

H = 16
KV = 8
HD = 64


norm_eps = 1e-05
masked_score = -1e30


def rope_tables(me, tok_rows, groups):
    row = lax.broadcasted_iota(jnp.int32, (groups * tok_rows, LANES), 0)
    lane = lax.broadcasted_iota(jnp.int32, (groups * tok_rows, LANES), 1)
    position = ((row // tok_rows) ^ me) * tok_rows + row % tok_rows
    frequency = jnp.exp((lane % (HD // 2)).astype(jnp.float32) * (-2.0 * math.log(10000.0) / HD))
    angles = position.astype(jnp.float32) * frequency
    sine = jnp.sin(angles)
    return jnp.cos(angles), jnp.where(lane % HD < HD // 2, -sine, sine)


LANES = 128
LIMIT_MIB = 63


def norm_forward(source, gain_vec):
    inverse = lax.rsqrt(jnp.mean(source * source, axis=-1, keepdims=True) + norm_eps)
    return (source * inverse * gain_vec, inverse)


def norm_backward(source, inverse, gain_vec, upstream):
    weighted = upstream * gain_vec
    cubed = inverse * inverse * inverse
    back = inverse * weighted - source * cubed * jnp.mean(weighted * source, axis=-1, keepdims=True)
    return (back, jnp.sum(upstream * source * inverse, axis=0, keepdims=True))


def dot(left, right, left_dim=1, right_dim=0):
    return lax.dot_general(
        left, right, (((left_dim,), (right_dim,)), ((), ())), preferred_element_type=jnp.float32
    )


def lane_of(shape):
    return lax.broadcasted_iota(jnp.int32, shape, 1)


def swap_halves(source):
    lane = lane_of(source.shape)
    return jnp.where(
        lane % HD < HD // 2,
        pltpu.roll(source, LANES - HD // 2, 1),
        pltpu.roll(source, HD // 2, 1),
    )


def rope(source, cosine_table, sine_table):
    return source * cosine_table + swap_halves(source) * sine_table


def unrope(upstream, cosine_table, sine_table):
    return upstream * cosine_table - swap_halves(upstream) * sine_table


def twice(pair):
    lane = lane_of(pair.shape)
    other = pltpu.roll(pair, HD, 1)
    return (jnp.where(lane < HD, pair, other), jnp.where(lane < HD, other, pair))


def stack_heads(pair):
    lane = lane_of(pair.shape)
    zero = jnp.zeros_like(pair)
    return jnp.concatenate(
        [jnp.where(lane < HD, pair, zero), jnp.where(lane < HD, zero, pair)], axis=0
    )


def join_heads(stacked):
    rows = stacked.shape[0] // 2
    lane = lane_of((rows, LANES))
    return jnp.where(lane < HD, stacked[:rows], stacked[rows:])


def allowed_mask(info_ref, seq_len, rows):
    me, prefix = info_ref[0], info_ref[1]
    key = lax.broadcasted_iota(jnp.int32, (seq_len, 2 * rows), 0)
    query = lax.broadcasted_iota(jnp.int32, (seq_len, 2 * rows), 1) % rows + me * rows
    key_pos = ((key // rows) ^ me) * rows + key % rows
    return (key_pos <= query) | (key_pos < prefix)


def forward_kernel(
    info_ref, wq_ref, wk_ref, wv_ref, wo_ref, gain_one_ref, gain_two_ref, cos_ref, sin_ref, *rest
):
    blocks, outs = rest[:-16], rest[-16:]
    q_out, k_out, v_out, lse_ref, att_ref, hid_ref, n2_ref, n1_out = outs[:8]
    wq_held, wo_held, q_ref, k_ref, v_ref, n1_ref, sems, out_sems = outs[8:]
    copies = start_copies([(wq_ref, wq_held), (wo_ref, wo_held)], sems)
    tokens_ref = blocks[0]
    rows = tokens_ref.shape[0]
    seq_len = rows * len(blocks)
    for n, b in enumerate(blocks):
        n1_ref[n * rows : (n + 1) * rows, :] = norm_forward(
            b[...].astype(jnp.float32), gain_one_ref[...]
        )[0].astype(jnp.bfloat16)
    normed = n1_ref[...]
    out_copies = start_copies([(n1_ref, n1_out)], out_sems)
    cosine, sine = cos_ref[...], sin_ref[...]
    keys = dot(normed, wk_ref[...])
    values = dot(normed, wv_ref[...])
    for c in range(KV // 2):
        cols = slice(c * LANES, (c + 1) * LANES)
        first, second = twice(rope(keys[:, cols], cosine, sine))
        k_ref[2 * c] = first.astype(jnp.bfloat16)
        k_ref[2 * c + 1] = second.astype(jnp.bfloat16)
        first, second = twice(values[:, cols])
        v_ref[2 * c] = first.astype(jnp.bfloat16)
        v_ref[2 * c + 1] = second.astype(jnp.bfloat16)
    out_copies += start_copies([(k_ref, k_out), (v_ref, v_out)], out_sems.at[pl.ds(1, 2)])
    allowed = allowed_mask(info_ref, seq_len, rows)
    wait_all(copies[:1])
    query_pre = dot(n1_ref[:rows, :], wq_held[...])
    for h in range(KV):
        cols = slice(h * LANES, (h + 1) * LANES)
        query = rope(query_pre[:, cols], cosine[:rows], sine[:rows]) * (1.0 / math.sqrt(HD))
        q_ref[:, cols] = query.astype(jnp.bfloat16)
        stacked = stack_heads(query).astype(jnp.bfloat16)
        scores = jnp.where(allowed, dot(k_ref[h], stacked, 1, 1), masked_score)
        row_max = jnp.max(scores, axis=0, keepdims=True)
        exps = jnp.exp(scores - row_max)
        total = jnp.sum(exps, axis=0, keepdims=True)
        lse_ref[h : h + 1, :] = row_max + jnp.log(total)
        prob = (exps * (1.0 / total)).astype(jnp.bfloat16)
        att_ref[:, cols] = join_heads(dot(prob, v_ref[h], 0, 0)).astype(jnp.bfloat16)
    out_copies += start_copies([(q_ref, q_out)], out_sems.at[pl.ds(3, 1)])
    wait_all(copies[1:])
    hidden = tokens_ref[...].astype(jnp.float32) + dot(att_ref[...], wo_held[...])
    hid_ref[...] = hidden
    n2_ref[...] = norm_forward(hidden, gain_two_ref[...])[0].astype(jnp.bfloat16)
    wait_all(out_copies)


def start_copies(pairs, sems):
    copies = describe(pairs, sems)
    for c in copies:
        c.start()
    return copies


def wait_all(copies):
    for c in copies:
        c.wait()


def own_half(info_ref, fh):
    return pl.ds(pl.multiple_of(info_ref[2] * fh, fh), fh)


def expert_parts(info_ref, wg_ref, wu_ref, w_ref, e):
    fh = wg_ref.shape[2] // 2
    mine = own_half(info_ref, fh)
    return [
        (wg_ref.at[e, :, mine], w_ref.at[e, :, pl.ds(0, fh)]),
        (wu_ref.at[e, :, mine], w_ref.at[e, :, pl.ds(fh, fh)]),
    ]


def down_part(info_ref, wd_ref, down_ref, e):
    mine = own_half(info_ref, wd_ref.shape[1] // 2)
    return [(wd_ref.at[e, mine, :], down_ref.at[e])]


def describe(pairs, sems):
    return [pltpu.make_async_copy(src, dst, sems.at[n]) for n, (src, dst) in enumerate(pairs)]


def row_parts(blocks, into, cols):
    rows = blocks[0].shape[0]
    return [(b.at[:, cols], into.at[pl.ds(n * rows, rows), :]) for n, b in enumerate(blocks)]


def widen(router_ref, wide_ref):
    wide_ref[...] = jnp.zeros_like(wide_ref)
    wide_ref[:, : router_ref.shape[1]] = router_ref[...]


def routing(routed, logits):
    logits = jnp.where(routed, logits, masked_score)
    exps = jnp.where(routed, jnp.exp(logits - jnp.max(logits, axis=-1, keepdims=True)), 0.0)
    return exps / jnp.sum(exps, axis=-1, keepdims=True)


def experts_kernel(
    info_ref, router_ref, wg_ref, wu_ref, wd_ref, *rest, n_blocks, experts, tiles
):
    cot_blocks, n2_blocks = rest[:n_blocks], rest[n_blocks : 2 * n_blocks]
    sums_out, acts_out = rest[2 * n_blocks : 2 * n_blocks + 2]
    (
        n2_ref, g_ref, routed_ref, w_ref, down_ref, acts_ref, sums_ref, probs_ref, router_wide,
        extra_ref,
    ) = rest[2 * n_blocks + 2 : 2 * n_blocks + 12]
    n2_sems, routed_sems, g_sems, w_sems, out_sems = rest[2 * n_blocks + 12 :]
    exp_dev, width, units = wg_ref.shape
    rows = n2_blocks[0].shape[0]
    fh = units // 2
    n2_copies = start_copies(row_parts(n2_blocks, n2_ref, pl.ds(0, width)), n2_sems)
    routed_copies = start_copies(row_parts(cot_blocks, routed_ref, pl.ds(width, LANES)), routed_sems)

    def weights(e):
        pairs = expert_parts(info_ref, wg_ref, wu_ref, w_ref, e)
        return describe(pairs + down_part(info_ref, wd_ref, down_ref, e), w_sems.at[e])

    def results(e):
        two = pl.ds(pl.multiple_of(e * 3 * fh, fh), 2 * fh)
        one = pl.ds(pl.multiple_of((3 * e + 2) * fh, fh), fh)
        return describe(
            [
                (acts_ref.at[e], acts_out.at[e]),
                (sums_ref.at[e, :, pl.ds(0, 2 * fh)], sums_out.at[:, two]),
                (sums_ref.at[e, :, pl.ds(2 * fh, fh)], sums_out.at[:, one]),
            ],
            out_sems.at[e],
        )

    for c in weights(0):
        c.start()
    widen(router_ref, router_wide)
    extra_ref[...] = jnp.zeros_like(extra_ref)
    wait_all(n2_copies)
    wait_all(routed_copies)
    g_copies = start_copies(row_parts(cot_blocks, g_ref, pl.ds(0, width)), g_sems)
    probs_ref[...] = routing(
        routed_ref[...].astype(jnp.float32) > 0.5, dot(n2_ref[...], router_wide[...])
    )
    wait_all(g_copies)
    step = n2_ref.shape[0] // tiles

    def one_expert(e, carry):
        wait_all(weights(e))

        @pl.when(e + 1 < exp_dev)
        def _():
            for c in weights(e + 1):
                c.start()

        spot = info_ref[0] * exp_dev + e
        for t in range(tiles):
            part = slice(t * step, (t + 1) * step)
            pre = dot(n2_ref[part, :], w_ref[e])
            gate_pre, up_pre = pre[:, :fh], pre[:, fh:]
            back = dot(g_ref[part, :], down_ref[e], 1, 1)
            sig = 0.5 * jnp.tanh(0.5 * gate_pre) + 0.5
            silu = gate_pre * sig
            act = silu * up_pre
            here = lane_of((step, LANES)) == spot
            weight = jnp.sum(jnp.where(here, probs_ref[part, :], 0.0), axis=1, keepdims=True)
            extra_ref[part, :] += jnp.where(here, jnp.sum(act * back, axis=1, keepdims=True), 0.0)
            grad_active = weight * back
            acts_ref[e, part, :fh] = (
                grad_active * up_pre * (sig + silu * (1.0 - sig))
            ).astype(jnp.bfloat16)
            acts_ref[e, part, fh : 2 * fh] = (grad_active * silu).astype(jnp.bfloat16)
            acts_ref[e, part, 2 * fh : 3 * fh] = (weight * act).astype(jnp.bfloat16)
            found = extra_ref[part, :]
            high = found.astype(jnp.bfloat16).astype(jnp.float32)
            lower = (found - high).astype(jnp.bfloat16).astype(jnp.float32)
            acts_ref[e, part, 3 * fh :] = (high + pltpu.roll(lower, experts, 1)).astype(
                jnp.bfloat16
            )
        leaving = results(e)
        leaving[0].start()
        sums_ref[e, :, : 2 * fh] = dot(n2_ref[...], acts_ref[e, :, : 2 * fh], 0, 0).astype(
            jnp.bfloat16
        )
        leaving[1].start()
        sums_ref[e, :, 2 * fh :] = dot(g_ref[...], acts_ref[e, :, 2 * fh : 3 * fh], 0, 0).astype(
            jnp.bfloat16
        )
        leaving[2].start()
        return carry

    lax.fori_loop(0, exp_dev, one_expert, 0)
    for e in range(exp_dev):
        wait_all(results(e))


def put_rows(values, t, odd_ref, even_ref, cols):
    rows = odd_ref.shape[1]
    count = values.shape[0] // rows
    for i in range(count):
        n = t * count + i
        out = odd_ref if n % 2 else even_ref
        out[n // 2, :, cols] = values[i * rows : (i + 1) * rows].astype(out.dtype)


def rows_kernel(
    info_ref, wg_ref, wu_ref, acts_in, odd_out, even_out, w_ref, gu_ref, total_ref, extra_ref,
    odd_ref, even_ref, w_sems, out_sems, extra_sems
):
    exp_dev, width, _ = wg_ref.shape
    all_rows, two = gu_ref.shape[1:]
    extra_part = pl.ds(3 * two // 2, LANES)
    extra_copy = start_copies([(acts_in.at[exp_dev - 1, :, extra_part], extra_ref)], extra_sems)

    def operands(e):
        pairs = expert_parts(info_ref, wg_ref, wu_ref, w_ref, e)
        acts = acts_in.at[e, :, pl.ds(0, two)]
        return describe(pairs + [(acts, gu_ref.at[e])], w_sems.at[e])

    for c in operands(0):
        c.start()
    wait_all(extra_copy)
    put_rows(
        extra_ref[...].astype(jnp.float32), 0, odd_ref, even_ref, slice(width, width + LANES)
    )
    total_ref[...] = jnp.zeros_like(total_ref)

    def one_expert(e, carry):
        wait_all(operands(e))
        for c in operands(e + 1):
            c.start()
        total_ref[...] += dot(gu_ref[e], w_ref[e], 1, 1)
        return carry

    lax.fori_loop(0, exp_dev - 1, one_expert, 0)
    wait_all(operands(exp_dev - 1))
    out_copies = []
    for t in range(2):
        part = slice(t * all_rows // 2, (t + 1) * all_rows // 2)
        new = total_ref[part, :] + dot(gu_ref[exp_dev - 1, part, :], w_ref[exp_dev - 1], 1, 1)
        put_rows(new, t, odd_ref, even_ref, slice(0, width))
        share = pl.ds(t * odd_ref.shape[0] // 2, odd_ref.shape[0] // 2)
        out_copies += start_copies(
            [(odd_ref.at[share], odd_out.at[share]), (even_ref.at[share], even_out.at[share])],
            out_sems.at[pl.ds(2 * t, 2)],
        )
    wait_all(out_copies)


def final_kernel(
    info_ref, sums_ref, arrived_ref, early_ref, late_ref, *rest, n_early, n_late
):
    dense = rest[:-10]
    gate_ref, up_ref, down_ref, wq_ref, wk_ref, wv_ref, wo_ref, router_ref, one_ref, two_ref = rest[-10:]
    exp_dev, rows, units = gate_ref.shape
    fh = units // 2
    half = info_ref[2]
    kept = sums_ref[pl.ds(pl.multiple_of(half * rows, rows), rows), :]
    got = arrived_ref[...]
    first = jnp.where(half == 0, kept, got).astype(jnp.float32)
    second = jnp.where(half == 0, got, kept).astype(jnp.float32)
    for e in range(exp_dev):
        at = 3 * e * fh
        gate_ref[e, :, :fh] = first[:, at : at + fh]
        gate_ref[e, :, fh:] = second[:, at : at + fh]
        up_ref[e, :, :fh] = first[:, at + fh : at + 2 * fh]
        up_ref[e, :, fh:] = second[:, at + fh : at + 2 * fh]
        at = (3 * e + 2) * fh
        down_ref[e, :fh, :] = first[:, at : at + fh].T
        down_ref[e, fh:, :] = second[:, at : at + fh].T
    early, late = early_ref[0], late_ref[0]
    for d in dense:
        early = early + d[:, :n_early].astype(jnp.float32)
        late = late + d[:, n_early:].astype(jnp.float32)
    width, k_cols = wo_ref.shape[1], wk_ref.shape[1]
    wo_ref[...] = early[:, :width]
    wq_ref[...] = early[:, width + LANES :]
    wk_ref[...] = late[:, :k_cols]
    wv_ref[...] = late[:, k_cols : 2 * k_cols]
    small = early[:, width : width + LANES]
    small = small.T
    router_ref[...] = small[1 : 1 + router_ref.shape[0], :]
    two_ref[...] = small[:1, :]
    one_ref[...] = late[:, 2 * k_cols :].T[:1, :]


def selection(info_ref, select_ref, own_rows):
    count, width = select_ref.shape
    groups = width // count
    row = lax.broadcasted_iota(jnp.int32, (count, width), 0)
    col = lax.broadcasted_iota(jnp.int32, (count, width), 1)
    want = ((row // own_rows) ^ info_ref[3]) * (own_rows * groups) + (
        info_ref[0] * own_rows + row % own_rows
    )
    select_ref[...] = jnp.where(col == want, 1.0, 0.0).astype(jnp.bfloat16)


def pick_small(blocks, rows, count, select):
    total = blocks[0][rows : rows + 2 * count].astype(jnp.float32)
    for b in blocks[1:]:
        total = total + b[rows : rows + 2 * count].astype(jnp.float32)
    total = jnp.concatenate(
        [total[:count] + total[count:], jnp.zeros((LANES - count, total.shape[1]), jnp.float32)],
        axis=0,
    )
    high = total.astype(jnp.bfloat16)
    lower = (total - high.astype(jnp.float32)).astype(jnp.bfloat16)
    return dot(select, high, 1, 1) + dot(select, lower, 1, 1)


def put_shares(values, odd_ref, even_ref, at):
    rows = odd_ref.shape[1]
    for n in range(2 * odd_ref.shape[0]):
        out = odd_ref if n % 2 else even_ref
        out[n // 2, :, at : at + values.shape[1]] = values[n * rows : (n + 1) * rows].astype(
            out.dtype
        )


def early_dense_kernel(info_ref, *rest, groups, count):
    attended, branch, query = (rest[1 + n * groups : 1 + (n + 1) * groups] for n in range(3))
    odd_ref, even_ref, normed_t_ref, select_ref = rest[1 + 3 * groups :]
    rows, width = attended[0].shape
    selection(info_ref, select_ref, odd_ref.shape[1])
    select = select_ref[...]

    def seq(blocks):
        return jnp.concatenate([b[:rows] for b in blocks], axis=0)

    normed_t = dot(select, rest[0][...], 1, 1).astype(jnp.bfloat16)
    normed_t_ref[...] = normed_t
    attended_t = dot(select, seq(attended), 1, 1).astype(jnp.bfloat16)
    put_shares(dot(attended_t, seq(branch)), odd_ref, even_ref, 0)
    put_shares(pick_small(branch, rows, count, select), odd_ref, even_ref, width)
    put_shares(dot(normed_t, seq(query)), odd_ref, even_ref, width + LANES)


def late_dense_kernel(info_ref, normed_t_ref, *rest):
    blocks = rest[:-3]
    odd_ref, even_ref, select_ref = rest[-3:]
    rows = normed_t_ref.shape[1] // len(blocks)
    selection(info_ref, select_ref, odd_ref.shape[1])
    kv = jnp.concatenate([b[:rows] for b in blocks], axis=0)
    put_shares(dot(normed_t_ref[...], kv), odd_ref, even_ref, 0)
    put_shares(pick_small(blocks, rows, 1, select_ref[...]), odd_ref, even_ref, kv.shape[1])


def small_rows(count):
    return -(-2 * count // 16) * 16


def put_small(ref, start, values):
    count = values.shape[0]
    high = values.astype(jnp.bfloat16).astype(jnp.float32)
    fill = jnp.zeros((small_rows(count) - 2 * count, values.shape[1]), jnp.float32)
    ref[start:] = jnp.concatenate([high, values - high, fill], axis=0).astype(jnp.bfloat16)


def backward_kernel(
    info_ref, own_ref, cot_ref, n2_ref, hid_ref, router_ref, gain_ref, wo_ref, q_ref,
    lse_ref, cos_ref, sin_ref, k_hbm, v_hbm, wq_hbm, acts_hbm, wd_hbm, *rest, experts
):
    arrived, outs = rest[:-18], rest[-18:]
    ghid_ref, branch_ref, dq_ref, odd_ref, even_ref, gn_ref, mix_odd_out, mix_even_out = outs[:8]
    (
        router_wide, k_ref, v_ref, wq_ref, scaled_ref, down_ref, mix_odd_ref, mix_even_ref, sems,
        mix_sems,
    ) = outs[8:]
    late = start_copies([(k_hbm, k_ref), (v_hbm, v_ref), (wq_hbm, wq_ref)], sems)
    exp_dev, units, _ = wd_hbm.shape
    fh = units // 2
    pairs = []
    for e in range(exp_dev):
        part = pl.ds(e * fh, fh)
        pairs += [(wd_hbm.at[e, own_half(info_ref, fh), :], down_ref.at[part, :])]
        pairs += [(acts_hbm.at[e, :, pl.ds(2 * fh, fh)], scaled_ref.at[:, part])]
    mix_copies = start_copies(pairs, mix_sems)
    widen(router_ref, router_wide)
    rows, width = hid_ref.shape
    summed = own_ref[...]
    for a in arrived:
        summed = summed + a[...].astype(jnp.float32)
    extra = summed[:, width:]
    gate_grads = extra + pltpu.roll(extra, LANES - experts, 1)
    routed = cot_ref[:, width:].astype(jnp.float32) > 0.5
    gate = routing(routed, dot(n2_ref[...], router_wide[...]))
    grad_logits = (
        gate * (gate_grads - jnp.sum(gate * gate_grads, axis=-1, keepdims=True))
    ).astype(jnp.bfloat16)
    router_grad = dot(grad_logits, n2_ref[...], 0, 0)
    grad_normed = summed[:, :width] + dot(grad_logits, router_wide[...], 1, 1)
    hidden = hid_ref[...]
    inverse = lax.rsqrt(jnp.mean(hidden * hidden, axis=-1, keepdims=True) + norm_eps)
    back, norm_grad = norm_backward(hidden, inverse, gain_ref[...], grad_normed)
    grad_hidden = cot_ref[:, :width].astype(jnp.float32) + back
    ghid_ref[...] = grad_hidden
    branch = grad_hidden.astype(jnp.bfloat16)
    branch_ref[:rows] = branch
    put_small(branch_ref, rows, jnp.concatenate([norm_grad, router_grad[:experts]], axis=0))
    grad_attended = dot(branch, wo_ref[...], 1, 1).astype(jnp.bfloat16)
    wait_all(late[:2])
    seq_len = k_ref.shape[1]
    allowed = allowed_mask(info_ref, seq_len, rows)
    cosine, sine = cos_ref[:rows, :], sin_ref[:rows, :]
    lane = lane_of((seq_len, LANES))
    kept = [None, None]
    for h in range(KV):
        cols = slice(h * LANES, (h + 1) * LANES)
        stacked = stack_heads(q_ref[:, cols])
        grad_stacked = stack_heads(grad_attended[:, cols])
        keys = k_ref[h]
        scores = jnp.where(allowed, dot(keys, stacked, 1, 1), masked_score)
        prob = jnp.exp(scores - lse_ref[h : h + 1, :])
        grad_prob = dot(v_ref[h], grad_stacked, 1, 1)
        delta = jnp.sum(prob * grad_prob, axis=0, keepdims=True)
        grad_scores = (prob * (grad_prob - delta)).astype(jnp.bfloat16)
        dq = join_heads(dot(grad_scores, keys, 0, 0)) * (1.0 / math.sqrt(HD))
        dq_ref[:, cols] = unrope(dq, cosine, sine).astype(jnp.bfloat16)
        parts = (dot(grad_scores, stacked), dot(prob.astype(jnp.bfloat16), grad_stacked))
        for n in range(2):
            both = parts[n] + pltpu.roll(parts[n], HD, 1)
            if h % 2 == 0:
                kept[n] = both
                continue
            pair = jnp.where(lane < HD, kept[n], both)
            start = (n * KV // 2 + h // 2) * LANES
            put_rows(pair, 0, odd_ref, even_ref, slice(start, start + LANES))
    wait_all(mix_copies)
    tokens = scaled_ref.shape[0] // 2
    out_copies = []
    for t in range(2):
        mix = dot(scaled_ref[t * tokens : (t + 1) * tokens, :], down_ref[...])
        put_rows(mix, t, mix_odd_ref, mix_even_ref, slice(0, width))
        share = pl.ds(t * mix_odd_ref.shape[0] // 2, mix_odd_ref.shape[0] // 2)
        out_copies += start_copies(
            [
                (mix_odd_ref.at[share], mix_odd_out.at[share]),
                (mix_even_ref.at[share], mix_even_out.at[share]),
            ],
            mix_sems.at[pl.ds(2 * t, 2)],
        )
    wait_all(late[2:])
    gn_ref[...] = dot(dq_ref[...], wq_ref[...], 1, 1)
    wait_all(out_copies)


def tokens_kernel(
    own_ref, gn_ref, wk_ref, wv_ref, tokens_ref, gain_ref, ghid_ref, cos_ref, sin_ref, *rest
):
    arrived, (kv_ref, out_ref) = rest[:-2], rest[-2:]
    rows = tokens_ref.shape[0]
    summed = own_ref[...]
    for a in arrived:
        summed = summed + a[...].astype(jnp.float32)
    k_cols = KV * HD
    for c in range(k_cols // LANES):
        cols = slice(c * LANES, (c + 1) * LANES)
        kv_ref[:rows, cols] = unrope(summed[:, cols], cos_ref[:rows, :], sin_ref[:rows, :]).astype(
            jnp.bfloat16
        )
    kv_ref[:rows, k_cols:] = summed[:, k_cols:].astype(jnp.bfloat16)
    grad_normed = (
        gn_ref[...]
        + dot(kv_ref[:rows, :k_cols], wk_ref[...], 1, 1)
        + dot(kv_ref[:rows, k_cols:], wv_ref[...], 1, 1)
    )
    source = tokens_ref[...].astype(jnp.float32)
    inverse = lax.rsqrt(jnp.mean(source * source, axis=-1, keepdims=True) + norm_eps)
    back, norm_grad = norm_backward(source, inverse, gain_ref[...], grad_normed)
    put_small(kv_ref, rows, norm_grad)
    out_ref[...] = (ghid_ref[...] + back).astype(jnp.bfloat16)


def call(kernel, out_shape, name, hbm=(), hbm_out=(), scratch=(), smem=True, limit=LIMIT_MIB):
    def run(*args):
        specs = [
            pl.BlockSpec(memory_space=pl.ANY if n in hbm else pltpu.VMEM)
            for n in range(len(args))
        ]
        if smem:
            specs[0] = pl.BlockSpec(memory_space=pltpu.SMEM)
        return pl.pallas_call(
            kernel,
            out_shape=out_shape,
            in_specs=specs,
            out_specs=[
                pl.BlockSpec(memory_space=pl.ANY if n in hbm_out else pltpu.VMEM)
                for n in range(len(out_shape))
            ],
            scratch_shapes=list(scratch),
            compiler_params=pltpu.CompilerParams(vmem_limit_bytes=limit * 1024 * 1024),
            name=name,
        )(*args)

    return run


def shape(*dims, dtype=jnp.bfloat16):
    return jax.ShapeDtypeStruct(dims, dtype)


def shards(
    tokens,
    prefix_len,
    routes,
    norm1_gain,
    w_query,
    w_key,
    w_value,
    w_output,
    norm2_gain,
    w_router,
    w_gate,
    w_up,
    w_down,
    cotangent,
):
    tok_rows, model_width = tokens.shape
    groups = lax.axis_size("expert")
    copies = lax.axis_size("dp")
    me = lax.axis_index("expert")
    half = lax.axis_index("dp") % 2
    exp_dev, _, hidden_units = w_gate.shape
    half_units = hidden_units // 2
    experts = exp_dev * groups
    f32 = jnp.float32
    seq_len = tok_rows * groups
    low = jnp.bfloat16

    def send(block, pair_flip, flip):
        return lax.ppermute(
            block,
            ("dp", "expert"),
            [
                (i * groups + j, (i ^ pair_flip) * groups + (j ^ flip))
                for i in range(copies)
                for j in range(groups)
            ],
        )

    def gather_even(block, pairs):
        return [
            block if (s, r) == (0, 0) else send(block, s, r)
            for s in range(pairs)
            for r in range(0, groups, 2)
        ]

    def gather_odd(even):
        out = []
        for b in even:
            out += [b, send(b, 0, 1)]
        return out

    def gather(block, pairs):
        return gather_odd(gather_even(block, pairs))

    def core_sum(odd, even):
        return even + send(odd, 0, 1).astype(jnp.float32)

    def swap(mine, pairs):
        mine = mine.astype(low)
        spots = [(s, r) for s in range(pairs) for r in range(0, groups, 2)]
        return [send(mine[n], *spots[n]) for n in range(1, len(spots))]

    tokens_even = gather_even(tokens, 1)
    cosine, sine = rope_tables(me, tok_rows, groups)
    cosine, sine, *tokens_even = lax.optimization_barrier((cosine, sine, *tokens_even))
    tokens_blocks = gather_odd(tokens_even)
    routed = jnp.any(
        routes[:, :, None] == jnp.arange(experts, dtype=jnp.int32)[None, None, :], axis=1
    )
    cot_mask = jnp.concatenate(
        [cotangent, jnp.pad(routed.astype(low), ((0, 0), (0, LANES - experts)))], axis=1
    )
    first_cot = cot_mask
    cot_mask, *tokens_even = lax.optimization_barrier((cot_mask, *tokens_even))
    cot_even = [
        cot_mask if q == (0, 0) else send(first_cot if q == (1, 0) else cot_mask, *q)
        for q in [(s, r) for s in range(2) for r in range(0, groups, 2)]
    ]
    my_dp = lax.axis_index("dp")
    info = jnp.stack([me, prefix_len[0], half, my_dp]).astype(jnp.int32)
    gain_one, gain_two = norm1_gain[None], norm2_gain[None]

    q_low, k_two, v_two, lse, attended, hidden_state, normed2, normed1_all = call(
        forward_kernel,
        (
            shape(tok_rows, H * HD),
            shape(KV, seq_len, LANES),
            shape(KV, seq_len, LANES),
            shape(KV, 2 * tok_rows, dtype=f32),
            shape(tok_rows, H * HD),
            shape(tok_rows, model_width, dtype=f32),
            shape(tok_rows, model_width),
            shape(seq_len, model_width),
        ),
        "attention_forward",
        hbm=(1, 4),
        hbm_out=(0, 1, 2, 7),
        scratch=(
            pltpu.VMEM((model_width, H * HD), low),
            pltpu.VMEM((H * HD, model_width), low),
            pltpu.VMEM((tok_rows, H * HD), low),
            pltpu.VMEM((KV, seq_len, LANES), low),
            pltpu.VMEM((KV, seq_len, LANES), low),
            pltpu.VMEM((seq_len, model_width), low),
            pltpu.SemaphoreType.DMA((2,)),
            pltpu.SemaphoreType.DMA((4,)),
        ),
    )(
        info, w_query, w_key, w_value, w_output, gain_one, gain_two, cosine, sine, *tokens_blocks,
    )

    normed2, *cot_even = lax.optimization_barrier((normed2, *cot_even))
    cot_blocks = gather_odd(cot_even)
    n2_blocks = gather(normed2, 2)
    attended_even = gather_even(attended, 1)
    n_blocks = 2 * groups
    all_rows = n_blocks * tok_rows
    wide = model_width + LANES

    dma = pltpu.SemaphoreType.DMA
    units = half_units * exp_dev
    wide_acts = 3 * half_units + LANES
    sums, acts = call(
        lambda *refs: experts_kernel(*refs, n_blocks=n_blocks, experts=experts, tiles=2),
        (
            shape(model_width, 3 * units),
            shape(exp_dev, all_rows, wide_acts),
        ),
        "experts",
        limit=48 if all_rows <= 1024 else LIMIT_MIB,
        hbm=tuple(range(2, 5 + 2 * n_blocks)),
        hbm_out=(0, 1),
        scratch=(
            pltpu.VMEM((all_rows, model_width), low),
            pltpu.VMEM((all_rows, model_width), low),
            pltpu.VMEM((all_rows, LANES), low),
            pltpu.VMEM((exp_dev, model_width, 2 * half_units), low),
            pltpu.VMEM((exp_dev, half_units, model_width), low),
            pltpu.VMEM((exp_dev, all_rows, wide_acts), low),
            pltpu.VMEM((exp_dev, model_width, 3 * half_units), low),
            pltpu.VMEM((all_rows, LANES), f32),
            pltpu.VMEM((model_width, LANES), low),
            pltpu.VMEM((all_rows, LANES), f32),
            dma((n_blocks,)),
            dma((n_blocks,)),
            dma((n_blocks,)),
            dma((exp_dev, 3)),
            dma((exp_dev, 3)),
        ),
    )(info, w_router, w_gate, w_up, w_down, *cot_blocks, *n2_blocks)
    outer = copies // 2
    shard_rows = model_width // copies
    reduced = lax.psum_scatter(
        sums,
        "dp",
        scatter_dimension=0,
        axis_index_groups=[[2 * o + p for o in range(outer)] for p in range(2)],
        tiled=True,
    )

    odd, even = call(
        rows_kernel,
        (shape(groups, tok_rows, wide), shape(groups, tok_rows, wide, dtype=f32)),
        "experts_rows",
        hbm=(1, 2, 3),
        hbm_out=(0, 1),
        scratch=(
            pltpu.VMEM((exp_dev, model_width, 2 * half_units), low),
            pltpu.VMEM((exp_dev, all_rows, 2 * half_units), low),
            pltpu.VMEM((all_rows, model_width), f32),
            pltpu.VMEM((all_rows, LANES), low),
            pltpu.VMEM((groups, tok_rows, wide), low),
            pltpu.VMEM((groups, tok_rows, wide), f32),
            dma((exp_dev, 3)),
            dma((4,)),
            dma((1,)),
        ),
    )(info, w_gate, w_up, acts)
    odd, *attended_even = lax.optimization_barrier((odd, *attended_even))
    mine = core_sum(odd, even)
    arrived = swap(mine, 2)
    attended_blocks = gather_odd(attended_even)

    (
        grad_hidden, grad_branch, grad_query, kv_odd, kv_even, grad_normed_q, mix_odd, mix_even
    ) = call(
        lambda *refs: backward_kernel(*refs, experts=experts),
        (
            shape(tok_rows, model_width, dtype=f32),
            shape(tok_rows + small_rows(experts + 1), model_width),
            shape(tok_rows, H * HD),
            shape(groups // 2, tok_rows, 2 * KV * HD),
            shape(groups // 2, tok_rows, 2 * KV * HD, dtype=f32),
            shape(tok_rows, model_width, dtype=f32),
            shape(groups, tok_rows, model_width),
            shape(groups, tok_rows, model_width, dtype=f32),
        ),
        "attention_backward",
        hbm=(12, 13, 14, 15, 16),
        hbm_out=(6, 7),
        scratch=(
            pltpu.VMEM((model_width, LANES), low),
            pltpu.VMEM((KV, seq_len, LANES), low),
            pltpu.VMEM((KV, seq_len, LANES), low),
            pltpu.VMEM((model_width, H * HD), low),
            pltpu.VMEM((all_rows, units), low),
            pltpu.VMEM((units, model_width), low),
            pltpu.VMEM((groups, tok_rows, model_width), low),
            pltpu.VMEM((groups, tok_rows, model_width), f32),
            dma((3,)),
            dma((2 * exp_dev,)),
        ),
    )(
        info, mine[0], cot_mask, normed2, hidden_state, w_router, gain_two, w_output,
        q_low, lse, cosine, sine, k_two, v_two, w_query, acts, w_down, *arrived,
    )
    kv_mine = core_sum(kv_odd, kv_even)
    kv_arrived = swap(kv_mine, 1)
    mix_odd, kv_mine = lax.optimization_barrier((mix_odd, kv_mine))
    mix_got = send(mix_odd, 0, 1)
    n_own = groups // 2
    mix_got_pair = send(
        (mix_even[n_own:] + mix_got[n_own:].astype(f32)).astype(low), 1, 0
    )
    query_later, grad_branch, *kv_arrived = lax.optimization_barrier(
        (grad_query, grad_branch, *kv_arrived)
    )
    branch_even = gather_even(grad_branch, 1)
    query_even = gather_even(query_later, 1)
    grad_kv, grad_tokens = call(
        tokens_kernel,
        (
            shape(tok_rows + small_rows(1), 2 * KV * HD),
            shape(tok_rows, model_width),
        ),
        "tokens_backward",
        smem=False,
    )(
        kv_mine[0], grad_normed_q, w_key, w_value, tokens, gain_one, grad_hidden, cosine, sine,
        *kv_arrived,
    )
    grad_kv, mix_got_pair, *later = lax.optimization_barrier(
        (grad_kv, mix_got_pair, *branch_even, *query_even)
    )
    kv_even_blocks = gather_even(grad_kv, 1)
    branch_blocks = gather_odd(later[: len(branch_even)])
    query_blocks = gather_odd(later[len(branch_even) :])
    own_rows = model_width // (copies * groups)
    n_early, n_late = model_width + LANES + H * HD, 2 * KV * HD + LANES
    select = pltpu.VMEM((copies * own_rows, model_width), low)
    early_odd, early_even, normed1_t = call(
        lambda *refs: early_dense_kernel(*refs, groups=groups, count=experts + 1),
        (
            shape(outer, own_rows, n_early),
            shape(outer, own_rows, n_early, dtype=f32),
            shape(copies * own_rows, seq_len),
        ),
        "dense_early",
        scratch=(select,),
    )(info, normed1_all, *attended_blocks, *branch_blocks, *query_blocks)
    early = early_even + send(early_odd, 1, 0).astype(f32)
    _, *kv_even_blocks = lax.optimization_barrier((early_odd, *kv_even_blocks))
    kv_blocks = gather_odd(kv_even_blocks)
    late_odd, late_even = call(
        late_dense_kernel,
        (shape(outer, own_rows, n_late), shape(outer, own_rows, n_late, dtype=f32)),
        "dense_late",
        scratch=(select,),
    )(info, normed1_t, *kv_blocks)
    mix_got_pair, late_odd = lax.optimization_barrier((mix_got_pair, late_odd))
    mix_pair = mix_even[:n_own] + mix_got[:n_own].astype(f32) + mix_got_pair.astype(f32)
    mixture = mix_pair[0]
    for a in swap(mix_pair, 1):
        mixture = mixture + a.astype(f32)
    block_out = (hidden_state + mixture).astype(low)
    late = late_even + send(late_odd, 1, 0).astype(f32)
    dense_send = jnp.concatenate([early[1:].astype(low), late[1:].astype(low)], axis=2)

    swapped = send(
        lax.dynamic_slice_in_dim(reduced, (1 - half) * shard_rows, shard_rows, 0), 1, 0
    )
    _, dense_send = lax.optimization_barrier((reduced, dense_send))
    dense_arrived = [send(dense_send[o - 1], 2 * o, 0) for o in range(1, outer)]
    k_cols = KV * HD
    (
        grad_gate_w, grad_up_w, grad_down_w, grad_query_w, grad_key_w, grad_value_w,
        grad_output_w, grad_router, grad_norm1, grad_norm2,
    ) = call(
        lambda *refs: final_kernel(*refs, n_early=n_early, n_late=n_late),
        (
            shape(exp_dev, shard_rows, hidden_units, dtype=f32),
            shape(exp_dev, shard_rows, hidden_units, dtype=f32),
            shape(exp_dev, hidden_units, shard_rows, dtype=f32),
            shape(own_rows, H * HD, dtype=f32),
            shape(own_rows, k_cols, dtype=f32),
            shape(own_rows, k_cols, dtype=f32),
            shape(own_rows, model_width, dtype=f32),
            shape(experts, own_rows, dtype=f32),
            shape(1, own_rows, dtype=f32),
            shape(1, own_rows, dtype=f32),
        ),
        "place",
        limit=48,
    )(info, reduced, swapped, early, late, *dense_arrived)
    return (
        block_out,
        grad_tokens,
        grad_norm1[0],
        grad_query_w,
        grad_key_w,
        grad_value_w,
        grad_output_w,
        grad_norm2[0],
        grad_router.T,
        grad_gate_w,
        grad_up_w,
        grad_down_w,
    )


def solution(mesh):
    return jax.shard_map(
        shards,
        mesh=mesh,
        in_specs=(
            P(("dp", "expert"), None),
            P("dp"),
            P(("dp", "expert"), None),
            P(),
            P(),
            P(),
            P(),
            P(),
            P(),
            P(),
            P("expert", None, None),
            P("expert", None, None),
            P("expert", None, None),
            P(("dp", "expert"), None),
        ),
        out_specs=(
            P(("dp", "expert"), None),
            P(("dp", "expert"), None),
            P(("dp", "expert")),
            P(("dp", "expert"), None),
            P(("dp", "expert"), None),
            P(("dp", "expert"), None),
            P(("dp", "expert"), None),
            P(("dp", "expert")),
            P(("dp", "expert"), None),
            P("expert", "dp", None),
            P("expert", "dp", None),
            P("expert", None, "dp"),
        ),
        check_vma=False,
    )
```

```python
import math

import jax
import jax.numpy as jnp
from jax import lax
from jax.experimental import pallas as pl
from jax.experimental.pallas import tpu as pltpu
from jax.sharding import PartitionSpec as P

H = 16
KV = 8
HD = 64


norm_eps = 1e-05
masked_score = -1e30


def rope_tables(me, tok_rows, groups):
    row = lax.broadcasted_iota(jnp.int32, (groups * tok_rows, LANES), 0)
    lane = lax.broadcasted_iota(jnp.int32, (groups * tok_rows, LANES), 1)
    position = ((row // tok_rows) ^ me) * tok_rows + row % tok_rows
    frequency = jnp.exp((lane % (HD // 2)).astype(jnp.float32) * (-2.0 * math.log(10000.0) / HD))
    angles = position.astype(jnp.float32) * frequency
    sine = jnp.sin(angles)
    return jnp.cos(angles), jnp.where(lane % HD < HD // 2, -sine, sine)


LANES = 128
LIMIT_MIB = 63


def norm_forward(source, gain_vec):
    inverse = lax.rsqrt(jnp.mean(source * source, axis=-1, keepdims=True) + norm_eps)
    return (source * inverse * gain_vec, inverse)


def norm_backward(source, inverse, gain_vec, upstream):
    weighted = upstream * gain_vec
    cubed = inverse * inverse * inverse
    back = inverse * weighted - source * cubed * jnp.mean(weighted * source, axis=-1, keepdims=True)
    return (back, jnp.sum(upstream * source * inverse, axis=0, keepdims=True))


def dot(left, right, left_dim=1, right_dim=0):
    return lax.dot_general(
        left, right, (((left_dim,), (right_dim,)), ((), ())), preferred_element_type=jnp.float32
    )


def lane_of(shape):
    return lax.broadcasted_iota(jnp.int32, shape, 1)


def swap_halves(source):
    lane = lane_of(source.shape)
    return jnp.where(
        lane % HD < HD // 2,
        pltpu.roll(source, LANES - HD // 2, 1),
        pltpu.roll(source, HD // 2, 1),
    )


def rope(source, cosine_table, sine_table):
    return source * cosine_table + swap_halves(source) * sine_table


def unrope(upstream, cosine_table, sine_table):
    return upstream * cosine_table - swap_halves(upstream) * sine_table


def twice(pair):
    lane = lane_of(pair.shape)
    other = pltpu.roll(pair, HD, 1)
    return (jnp.where(lane < HD, pair, other), jnp.where(lane < HD, other, pair))


def stack_heads(pair):
    lane = lane_of(pair.shape)
    zero = jnp.zeros_like(pair)
    return jnp.concatenate(
        [jnp.where(lane < HD, pair, zero), jnp.where(lane < HD, zero, pair)], axis=0
    )


def join_heads(stacked):
    rows = stacked.shape[0] // 2
    lane = lane_of((rows, LANES))
    return jnp.where(lane < HD, stacked[:rows], stacked[rows:])


def allowed_mask(info_ref, seq_len, rows):
    me, prefix = info_ref[0], info_ref[1]
    key = lax.broadcasted_iota(jnp.int32, (seq_len, 2 * rows), 0)
    query = lax.broadcasted_iota(jnp.int32, (seq_len, 2 * rows), 1) % rows + me * rows
    key_pos = ((key // rows) ^ me) * rows + key % rows
    return (key_pos <= query) | (key_pos < prefix)


def forward_kernel(
    info_ref, wq_ref, wk_ref, wv_ref, wo_ref, gain_one_ref, gain_two_ref, cos_ref, sin_ref, *rest
):
    blocks, outs = rest[:-16], rest[-16:]
    q_out, k_out, v_out, lse_ref, att_ref, hid_ref, n2_ref, n1_out = outs[:8]
    wq_held, wo_held, q_ref, k_ref, v_ref, n1_ref, sems, out_sems = outs[8:]
    copies = start_copies([(wq_ref, wq_held), (wo_ref, wo_held)], sems)
    tokens_ref = blocks[0]
    rows = tokens_ref.shape[0]
    seq_len = rows * len(blocks)
    for n, b in enumerate(blocks):
        n1_ref[n * rows : (n + 1) * rows, :] = norm_forward(
            b[...].astype(jnp.float32), gain_one_ref[...]
        )[0].astype(jnp.bfloat16)
    normed = n1_ref[...]
    out_copies = start_copies([(n1_ref, n1_out)], out_sems)
    cosine, sine = cos_ref[...], sin_ref[...]
    keys = dot(normed, wk_ref[...])
    values = dot(normed, wv_ref[...])
    for c in range(KV // 2):
        cols = slice(c * LANES, (c + 1) * LANES)
        first, second = twice(rope(keys[:, cols], cosine, sine))
        k_ref[2 * c] = first.astype(jnp.bfloat16)
        k_ref[2 * c + 1] = second.astype(jnp.bfloat16)
        first, second = twice(values[:, cols])
        v_ref[2 * c] = first.astype(jnp.bfloat16)
        v_ref[2 * c + 1] = second.astype(jnp.bfloat16)
    out_copies += start_copies([(k_ref, k_out), (v_ref, v_out)], out_sems.at[pl.ds(1, 2)])
    allowed = allowed_mask(info_ref, seq_len, rows)
    wait_all(copies[:1])
    query_pre = dot(n1_ref[:rows, :], wq_held[...])
    for h in range(KV):
        cols = slice(h * LANES, (h + 1) * LANES)
        query = rope(query_pre[:, cols], cosine[:rows], sine[:rows]) * (1.0 / math.sqrt(HD))
        q_ref[:, cols] = query.astype(jnp.bfloat16)
        stacked = stack_heads(query).astype(jnp.bfloat16)
        scores = jnp.where(allowed, dot(k_ref[h], stacked, 1, 1), masked_score)
        row_max = jnp.max(scores, axis=0, keepdims=True)
        exps = jnp.exp(scores - row_max)
        total = jnp.sum(exps, axis=0, keepdims=True)
        lse_ref[h : h + 1, :] = row_max + jnp.log(total)
        prob = (exps * (1.0 / total)).astype(jnp.bfloat16)
        att_ref[:, cols] = join_heads(dot(prob, v_ref[h], 0, 0)).astype(jnp.bfloat16)
    out_copies += start_copies([(q_ref, q_out)], out_sems.at[pl.ds(3, 1)])
    wait_all(copies[1:])
    hidden = tokens_ref[...].astype(jnp.float32) + dot(att_ref[...], wo_held[...])
    hid_ref[...] = hidden
    n2_ref[...] = norm_forward(hidden, gain_two_ref[...])[0].astype(jnp.bfloat16)
    wait_all(out_copies)


def start_copies(pairs, sems):
    copies = describe(pairs, sems)
    for c in copies:
        c.start()
    return copies


def wait_all(copies):
    for c in copies:
        c.wait()


def own_half(info_ref, fh):
    return pl.ds(pl.multiple_of(info_ref[2] * fh, fh), fh)


def expert_parts(info_ref, wg_ref, wu_ref, w_ref, e):
    fh = wg_ref.shape[2] // 2
    mine = own_half(info_ref, fh)
    return [
        (wg_ref.at[e, :, mine], w_ref.at[e, :, pl.ds(0, fh)]),
        (wu_ref.at[e, :, mine], w_ref.at[e, :, pl.ds(fh, fh)]),
    ]


def down_part(info_ref, wd_ref, down_ref, e):
    mine = own_half(info_ref, wd_ref.shape[1] // 2)
    return [(wd_ref.at[e, mine, :], down_ref.at[e])]


def describe(pairs, sems):
    return [pltpu.make_async_copy(src, dst, sems.at[n]) for n, (src, dst) in enumerate(pairs)]


def row_parts(blocks, into, cols):
    rows = blocks[0].shape[0]
    return [(b.at[:, cols], into.at[pl.ds(n * rows, rows), :]) for n, b in enumerate(blocks)]


def widen(router_ref, wide_ref):
    wide_ref[...] = jnp.zeros_like(wide_ref)
    wide_ref[:, : router_ref.shape[1]] = router_ref[...]


def routing(routed, logits):
    logits = jnp.where(routed, logits, masked_score)
    exps = jnp.where(routed, jnp.exp(logits - jnp.max(logits, axis=-1, keepdims=True)), 0.0)
    return exps / jnp.sum(exps, axis=-1, keepdims=True)


def experts_kernel(
    info_ref, router_ref, wg_ref, wu_ref, wd_ref, *rest, n_blocks, experts, tiles
):
    cot_blocks, n2_blocks = rest[:n_blocks], rest[n_blocks : 2 * n_blocks]
    sums_out, acts_out = rest[2 * n_blocks : 2 * n_blocks + 2]
    (
        n2_ref, g_ref, routed_ref, w_ref, down_ref, acts_ref, sums_ref, probs_ref, router_wide,
        extra_ref,
    ) = rest[2 * n_blocks + 2 : 2 * n_blocks + 12]
    n2_sems, routed_sems, g_sems, w_sems, out_sems = rest[2 * n_blocks + 12 :]
    exp_dev, width, units = wg_ref.shape
    rows = n2_blocks[0].shape[0]
    fh = units // 2
    n2_copies = start_copies(row_parts(n2_blocks, n2_ref, pl.ds(0, width)), n2_sems)
    routed_copies = start_copies(row_parts(cot_blocks, routed_ref, pl.ds(width, LANES)), routed_sems)

    def weights(e):
        pairs = expert_parts(info_ref, wg_ref, wu_ref, w_ref, e)
        return describe(pairs + down_part(info_ref, wd_ref, down_ref, e), w_sems.at[e])

    def results(e):
        two = pl.ds(pl.multiple_of(e * 3 * fh, fh), 2 * fh)
        one = pl.ds(pl.multiple_of((3 * e + 2) * fh, fh), fh)
        return describe(
            [
                (acts_ref.at[e], acts_out.at[e]),
                (sums_ref.at[e, :, pl.ds(0, 2 * fh)], sums_out.at[:, two]),
                (sums_ref.at[e, :, pl.ds(2 * fh, fh)], sums_out.at[:, one]),
            ],
            out_sems.at[e],
        )

    for c in weights(0):
        c.start()
    widen(router_ref, router_wide)
    extra_ref[...] = jnp.zeros_like(extra_ref)
    wait_all(n2_copies)
    wait_all(routed_copies)
    g_copies = start_copies(row_parts(cot_blocks, g_ref, pl.ds(0, width)), g_sems)
    probs_ref[...] = routing(
        routed_ref[...].astype(jnp.float32) > 0.5, dot(n2_ref[...], router_wide[...])
    )
    wait_all(g_copies)
    step = n2_ref.shape[0] // tiles

    def one_expert(e, carry):
        wait_all(weights(e))

        @pl.when(e + 1 < exp_dev)
        def _():
            for c in weights(e + 1):
                c.start()

        spot = info_ref[0] * exp_dev + e
        for t in range(tiles):
            part = slice(t * step, (t + 1) * step)
            pre = dot(n2_ref[part, :], w_ref[e])
            gate_pre, up_pre = pre[:, :fh], pre[:, fh:]
            back = dot(g_ref[part, :], down_ref[e], 1, 1)
            sig = 0.5 * jnp.tanh(0.5 * gate_pre) + 0.5
            silu = gate_pre * sig
            act = silu * up_pre
            here = lane_of((step, LANES)) == spot
            weight = jnp.sum(jnp.where(here, probs_ref[part, :], 0.0), axis=1, keepdims=True)
            extra_ref[part, :] += jnp.where(here, jnp.sum(act * back, axis=1, keepdims=True), 0.0)
            grad_active = weight * back
            acts_ref[e, part, :fh] = (
                grad_active * up_pre * (sig + silu * (1.0 - sig))
            ).astype(jnp.bfloat16)
            acts_ref[e, part, fh : 2 * fh] = (grad_active * silu).astype(jnp.bfloat16)
            acts_ref[e, part, 2 * fh : 3 * fh] = (weight * act).astype(jnp.bfloat16)
            found = extra_ref[part, :]
            high = found.astype(jnp.bfloat16).astype(jnp.float32)
            lower = (found - high).astype(jnp.bfloat16).astype(jnp.float32)
            acts_ref[e, part, 3 * fh :] = (high + pltpu.roll(lower, experts, 1)).astype(
                jnp.bfloat16
            )
        leaving = results(e)
        leaving[0].start()
        sums_ref[e, :, : 2 * fh] = dot(n2_ref[...], acts_ref[e, :, : 2 * fh], 0, 0).astype(
            jnp.bfloat16
        )
        leaving[1].start()
        sums_ref[e, :, 2 * fh :] = dot(g_ref[...], acts_ref[e, :, 2 * fh : 3 * fh], 0, 0).astype(
            jnp.bfloat16
        )
        leaving[2].start()
        return carry

    lax.fori_loop(0, exp_dev, one_expert, 0)
    for e in range(exp_dev):
        wait_all(results(e))


def put_rows(values, t, odd_ref, even_ref, cols):
    rows = odd_ref.shape[1]
    count = values.shape[0] // rows
    for i in range(count):
        n = t * count + i
        out = odd_ref if n % 2 else even_ref
        out[n // 2, :, cols] = values[i * rows : (i + 1) * rows].astype(out.dtype)


def rows_kernel(
    info_ref, wg_ref, wu_ref, acts_in, odd_out, even_out, w_ref, gu_ref, total_ref, extra_ref,
    odd_ref, even_ref, w_sems, out_sems, extra_sems
):
    exp_dev, width, _ = wg_ref.shape
    all_rows, two = gu_ref.shape[1:]
    extra_part = pl.ds(3 * two // 2, LANES)
    extra_copy = start_copies([(acts_in.at[exp_dev - 1, :, extra_part], extra_ref)], extra_sems)

    def operands(e):
        pairs = expert_parts(info_ref, wg_ref, wu_ref, w_ref, e)
        acts = acts_in.at[e, :, pl.ds(0, two)]
        return describe(pairs + [(acts, gu_ref.at[e])], w_sems.at[e])

    for c in operands(0):
        c.start()
    wait_all(extra_copy)
    put_rows(
        extra_ref[...].astype(jnp.float32), 0, odd_ref, even_ref, slice(width, width + LANES)
    )
    total_ref[...] = jnp.zeros_like(total_ref)

    def one_expert(e, carry):
        wait_all(operands(e))
        for c in operands(e + 1):
            c.start()
        total_ref[...] += dot(gu_ref[e], w_ref[e], 1, 1)
        return carry

    lax.fori_loop(0, exp_dev - 1, one_expert, 0)
    wait_all(operands(exp_dev - 1))
    out_copies = []
    for t in range(2):
        part = slice(t * all_rows // 2, (t + 1) * all_rows // 2)
        new = total_ref[part, :] + dot(gu_ref[exp_dev - 1, part, :], w_ref[exp_dev - 1], 1, 1)
        put_rows(new, t, odd_ref, even_ref, slice(0, width))
        share = pl.ds(t * odd_ref.shape[0] // 2, odd_ref.shape[0] // 2)
        out_copies += start_copies(
            [(odd_ref.at[share], odd_out.at[share]), (even_ref.at[share], even_out.at[share])],
            out_sems.at[pl.ds(2 * t, 2)],
        )
    wait_all(out_copies)


def final_kernel(
    info_ref, sums_ref, arrived_ref, early_ref, late_ref, *rest, n_early, n_late
):
    dense = rest[:-10]
    gate_ref, up_ref, down_ref, wq_ref, wk_ref, wv_ref, wo_ref, router_ref, one_ref, two_ref = rest[-10:]
    exp_dev, rows, units = gate_ref.shape
    fh = units // 2
    half = info_ref[2]
    kept = sums_ref[pl.ds(pl.multiple_of(half * rows, rows), rows), :]
    got = arrived_ref[...]
    first = jnp.where(half == 0, kept, got).astype(jnp.float32)
    second = jnp.where(half == 0, got, kept).astype(jnp.float32)
    for e in range(exp_dev):
        at = 3 * e * fh
        gate_ref[e, :, :fh] = first[:, at : at + fh]
        gate_ref[e, :, fh:] = second[:, at : at + fh]
        up_ref[e, :, :fh] = first[:, at + fh : at + 2 * fh]
        up_ref[e, :, fh:] = second[:, at + fh : at + 2 * fh]
        at = (3 * e + 2) * fh
        down_ref[e, :fh, :] = first[:, at : at + fh].T
        down_ref[e, fh:, :] = second[:, at : at + fh].T
    early, late = early_ref[0], late_ref[0]
    late_kv = late[:, : 2 * wk_ref.shape[1]]
    for d in dense:
        early = early + d[:, :n_early].astype(jnp.float32)
        late_kv = late_kv + d[:, n_early:].astype(jnp.float32)
    width, k_cols = wo_ref.shape[1], wk_ref.shape[1]
    wo_ref[...] = early[:, :width]
    wq_ref[...] = early[:, width + LANES :]
    wk_ref[...] = late_kv[:, :k_cols]
    wv_ref[...] = late_kv[:, k_cols:]
    small = early[:, width : width + LANES] + late[:, 2 * k_cols :]
    small = small.T
    router_ref[...] = small[1 : 1 + router_ref.shape[0], :]
    two_ref[...] = small[:1, :]
    one = 1 + router_ref.shape[0]
    one_ref[...] = small[one : one + 1, :]


def selection(info_ref, select_ref, own_rows):
    count, width = select_ref.shape
    groups = width // count
    row = lax.broadcasted_iota(jnp.int32, (count, width), 0)
    col = lax.broadcasted_iota(jnp.int32, (count, width), 1)
    want = ((row // own_rows) ^ info_ref[3]) * (own_rows * groups) + (
        info_ref[0] * own_rows + row % own_rows
    )
    select_ref[...] = jnp.where(col == want, 1.0, 0.0).astype(jnp.bfloat16)


def pick_small(blocks, rows, count, select):
    total = blocks[0][rows : rows + 2 * count].astype(jnp.float32)
    for b in blocks[1:]:
        total = total + b[rows : rows + 2 * count].astype(jnp.float32)
    total = jnp.concatenate(
        [total[:count] + total[count:], jnp.zeros((LANES - count, total.shape[1]), jnp.float32)],
        axis=0,
    )
    high = total.astype(jnp.bfloat16)
    lower = (total - high.astype(jnp.float32)).astype(jnp.bfloat16)
    return dot(select, high, 1, 1) + dot(select, lower, 1, 1)


def put_shares(values, odd_ref, even_ref, at):
    rows = odd_ref.shape[1]
    for n in range(2 * odd_ref.shape[0]):
        out = odd_ref if n % 2 else even_ref
        out[n // 2, :, at : at + values.shape[1]] = values[n * rows : (n + 1) * rows].astype(
            out.dtype
        )


def early_dense_kernel(info_ref, *rest, groups, count):
    attended, branch, query = (rest[1 + n * groups : 1 + (n + 1) * groups] for n in range(3))
    odd_ref, even_ref, normed_t_ref, select_ref = rest[1 + 3 * groups :]
    rows, width = attended[0].shape
    selection(info_ref, select_ref, odd_ref.shape[1])
    select = select_ref[...]

    def seq(blocks):
        return jnp.concatenate([b[:rows] for b in blocks], axis=0)

    normed_t = dot(select, rest[0][...], 1, 1).astype(jnp.bfloat16)
    normed_t_ref[...] = normed_t
    attended_t = dot(select, seq(attended), 1, 1).astype(jnp.bfloat16)
    put_shares(dot(attended_t, seq(branch)), odd_ref, even_ref, 0)
    put_shares(pick_small(branch, rows, count, select), odd_ref, even_ref, width)
    put_shares(dot(normed_t, seq(query)), odd_ref, even_ref, width + LANES)


def late_dense_kernel(info_ref, normed_t_ref, *rest, lane):
    blocks = rest[:-3]
    odd_ref, even_ref, select_ref = rest[-3:]
    rows = normed_t_ref.shape[1] // len(blocks)
    selection(info_ref, select_ref, odd_ref.shape[1])
    kv = jnp.concatenate([b[:rows] for b in blocks], axis=0)
    put_shares(dot(normed_t_ref[...], kv), odd_ref, even_ref, 0)
    small = pltpu.roll(pick_small(blocks, rows, 1, select_ref[...]), lane, 1)
    put_shares(small, odd_ref, even_ref, kv.shape[1])


def small_rows(count):
    return -(-2 * count // 16) * 16


def put_small(ref, start, values):
    count = values.shape[0]
    high = values.astype(jnp.bfloat16).astype(jnp.float32)
    fill = jnp.zeros((small_rows(count) - 2 * count, values.shape[1]), jnp.float32)
    ref[start:] = jnp.concatenate([high, values - high, fill], axis=0).astype(jnp.bfloat16)


def backward_kernel(
    info_ref, own_ref, cot_ref, n2_ref, hid_ref, router_ref, gain_ref, wo_ref, q_ref,
    lse_ref, cos_ref, sin_ref, k_hbm, v_hbm, wq_hbm, acts_hbm, wd_hbm, *rest, experts
):
    arrived, outs = rest[:-18], rest[-18:]
    ghid_ref, branch_ref, dq_ref, odd_ref, even_ref, gn_ref, mix_odd_out, mix_even_out = outs[:8]
    (
        router_wide, k_ref, v_ref, wq_ref, scaled_ref, down_ref, mix_odd_ref, mix_even_ref, sems,
        mix_sems,
    ) = outs[8:]
    late = start_copies([(k_hbm, k_ref), (v_hbm, v_ref), (wq_hbm, wq_ref)], sems)
    exp_dev, units, _ = wd_hbm.shape
    fh = units // 2
    pairs = []
    for e in range(exp_dev):
        part = pl.ds(e * fh, fh)
        pairs += [(wd_hbm.at[e, own_half(info_ref, fh), :], down_ref.at[part, :])]
        pairs += [(acts_hbm.at[e, :, pl.ds(2 * fh, fh)], scaled_ref.at[:, part])]
    mix_copies = start_copies(pairs, mix_sems)
    widen(router_ref, router_wide)
    rows, width = hid_ref.shape
    summed = own_ref[...]
    for a in arrived:
        summed = summed + a[...].astype(jnp.float32)
    extra = summed[:, width:]
    gate_grads = extra + pltpu.roll(extra, LANES - experts, 1)
    routed = cot_ref[:, width:].astype(jnp.float32) > 0.5
    gate = routing(routed, dot(n2_ref[...], router_wide[...]))
    grad_logits = (
        gate * (gate_grads - jnp.sum(gate * gate_grads, axis=-1, keepdims=True))
    ).astype(jnp.bfloat16)
    router_grad = dot(grad_logits, n2_ref[...], 0, 0)
    grad_normed = summed[:, :width] + dot(grad_logits, router_wide[...], 1, 1)
    hidden = hid_ref[...]
    inverse = lax.rsqrt(jnp.mean(hidden * hidden, axis=-1, keepdims=True) + norm_eps)
    back, norm_grad = norm_backward(hidden, inverse, gain_ref[...], grad_normed)
    grad_hidden = cot_ref[:, :width].astype(jnp.float32) + back
    ghid_ref[...] = grad_hidden
    branch = grad_hidden.astype(jnp.bfloat16)
    branch_ref[:rows] = branch
    put_small(branch_ref, rows, jnp.concatenate([norm_grad, router_grad[:experts]], axis=0))
    grad_attended = dot(branch, wo_ref[...], 1, 1).astype(jnp.bfloat16)
    wait_all(late[:2])
    seq_len = k_ref.shape[1]
    allowed = allowed_mask(info_ref, seq_len, rows)
    cosine, sine = cos_ref[:rows, :], sin_ref[:rows, :]
    lane = lane_of((seq_len, LANES))
    kept = [None, None]
    for h in range(KV):
        cols = slice(h * LANES, (h + 1) * LANES)
        stacked = stack_heads(q_ref[:, cols])
        grad_stacked = stack_heads(grad_attended[:, cols])
        keys = k_ref[h]
        scores = jnp.where(allowed, dot(keys, stacked, 1, 1), masked_score)
        prob = jnp.exp(scores - lse_ref[h : h + 1, :])
        grad_prob = dot(v_ref[h], grad_stacked, 1, 1)
        delta = jnp.sum(prob * grad_prob, axis=0, keepdims=True)
        grad_scores = (prob * (grad_prob - delta)).astype(jnp.bfloat16)
        dq = join_heads(dot(grad_scores, keys, 0, 0)) * (1.0 / math.sqrt(HD))
        dq_ref[:, cols] = unrope(dq, cosine, sine).astype(jnp.bfloat16)
        parts = (dot(grad_scores, stacked), dot(prob.astype(jnp.bfloat16), grad_stacked))
        for n in range(2):
            both = parts[n] + pltpu.roll(parts[n], HD, 1)
            if h % 2 == 0:
                kept[n] = both
                continue
            pair = jnp.where(lane < HD, kept[n], both)
            start = (n * KV // 2 + h // 2) * LANES
            put_rows(pair, 0, odd_ref, even_ref, slice(start, start + LANES))
    wait_all(mix_copies)
    tokens = scaled_ref.shape[0] // 2
    out_copies = []
    for t in range(2):
        mix = dot(scaled_ref[t * tokens : (t + 1) * tokens, :], down_ref[...])
        put_rows(mix, t, mix_odd_ref, mix_even_ref, slice(0, width))
        share = pl.ds(t * mix_odd_ref.shape[0] // 2, mix_odd_ref.shape[0] // 2)
        out_copies += start_copies(
            [
                (mix_odd_ref.at[share], mix_odd_out.at[share]),
                (mix_even_ref.at[share], mix_even_out.at[share]),
            ],
            mix_sems.at[pl.ds(2 * t, 2)],
        )
    wait_all(late[2:])
    gn_ref[...] = dot(dq_ref[...], wq_ref[...], 1, 1)
    wait_all(out_copies)


def tokens_kernel(
    own_ref, gn_ref, wk_ref, wv_ref, tokens_ref, gain_ref, ghid_ref, cos_ref, sin_ref, *rest
):
    arrived, (kv_ref, out_ref) = rest[:-2], rest[-2:]
    rows = tokens_ref.shape[0]
    summed = own_ref[...]
    for a in arrived:
        summed = summed + a[...].astype(jnp.float32)
    k_cols = KV * HD
    for c in range(k_cols // LANES):
        cols = slice(c * LANES, (c + 1) * LANES)
        kv_ref[:rows, cols] = unrope(summed[:, cols], cos_ref[:rows, :], sin_ref[:rows, :]).astype(
            jnp.bfloat16
        )
    kv_ref[:rows, k_cols:] = summed[:, k_cols:].astype(jnp.bfloat16)
    grad_normed = (
        gn_ref[...]
        + dot(kv_ref[:rows, :k_cols], wk_ref[...], 1, 1)
        + dot(kv_ref[:rows, k_cols:], wv_ref[...], 1, 1)
    )
    source = tokens_ref[...].astype(jnp.float32)
    inverse = lax.rsqrt(jnp.mean(source * source, axis=-1, keepdims=True) + norm_eps)
    back, norm_grad = norm_backward(source, inverse, gain_ref[...], grad_normed)
    put_small(kv_ref, rows, norm_grad)
    out_ref[...] = (ghid_ref[...] + back).astype(jnp.bfloat16)


def call(kernel, out_shape, name, hbm=(), hbm_out=(), scratch=(), smem=True, limit=LIMIT_MIB):
    def run(*args):
        specs = [
            pl.BlockSpec(memory_space=pl.ANY if n in hbm else pltpu.VMEM)
            for n in range(len(args))
        ]
        if smem:
            specs[0] = pl.BlockSpec(memory_space=pltpu.SMEM)
        return pl.pallas_call(
            kernel,
            out_shape=out_shape,
            in_specs=specs,
            out_specs=[
                pl.BlockSpec(memory_space=pl.ANY if n in hbm_out else pltpu.VMEM)
                for n in range(len(out_shape))
            ],
            scratch_shapes=list(scratch),
            compiler_params=pltpu.CompilerParams(vmem_limit_bytes=limit * 1024 * 1024),
            name=name,
        )(*args)

    return run


def shape(*dims, dtype=jnp.bfloat16):
    return jax.ShapeDtypeStruct(dims, dtype)


def shards(
    tokens,
    prefix_len,
    routes,
    norm1_gain,
    w_query,
    w_key,
    w_value,
    w_output,
    norm2_gain,
    w_router,
    w_gate,
    w_up,
    w_down,
    cotangent,
):
    tok_rows, model_width = tokens.shape
    groups = lax.axis_size("expert")
    copies = lax.axis_size("dp")
    me = lax.axis_index("expert")
    half = lax.axis_index("dp") % 2
    exp_dev, _, hidden_units = w_gate.shape
    half_units = hidden_units // 2
    experts = exp_dev * groups
    f32 = jnp.float32
    seq_len = tok_rows * groups
    low = jnp.bfloat16

    def send(block, pair_flip, flip):
        return lax.ppermute(
            block,
            ("dp", "expert"),
            [
                (i * groups + j, (i ^ pair_flip) * groups + (j ^ flip))
                for i in range(copies)
                for j in range(groups)
            ],
        )

    def gather_even(block, pairs):
        return [
            block if (s, r) == (0, 0) else send(block, s, r)
            for s in range(pairs)
            for r in range(0, groups, 2)
        ]

    def gather_odd(even):
        out = []
        for b in even:
            out += [b, send(b, 0, 1)]
        return out

    def gather(block, pairs):
        return gather_odd(gather_even(block, pairs))

    def core_sum(odd, even):
        return even + send(odd, 0, 1).astype(jnp.float32)

    def swap(mine, pairs):
        mine = mine.astype(low)
        spots = [(s, r) for s in range(pairs) for r in range(0, groups, 2)]
        return [send(mine[n], *spots[n]) for n in range(1, len(spots))]

    tokens_even = gather_even(tokens, 1)
    cosine, sine = rope_tables(me, tok_rows, groups)
    cosine, sine, *tokens_even = lax.optimization_barrier((cosine, sine, *tokens_even))
    tokens_blocks = gather_odd(tokens_even)
    routed = jnp.any(
        routes[:, :, None] == jnp.arange(experts, dtype=jnp.int32)[None, None, :], axis=1
    )
    cot_mask = jnp.concatenate(
        [cotangent, jnp.pad(routed.astype(low), ((0, 0), (0, LANES - experts)))], axis=1
    )
    first_cot = cot_mask
    cot_mask, *tokens_even = lax.optimization_barrier((cot_mask, *tokens_even))
    cot_even = [
        cot_mask if q == (0, 0) else send(first_cot if q == (1, 0) else cot_mask, *q)
        for q in [(s, r) for s in range(2) for r in range(0, groups, 2)]
    ]
    my_dp = lax.axis_index("dp")
    info = jnp.stack([me, prefix_len[0], half, my_dp]).astype(jnp.int32)
    gain_one, gain_two = norm1_gain[None], norm2_gain[None]

    q_low, k_two, v_two, lse, attended, hidden_state, normed2, normed1_all = call(
        forward_kernel,
        (
            shape(tok_rows, H * HD),
            shape(KV, seq_len, LANES),
            shape(KV, seq_len, LANES),
            shape(KV, 2 * tok_rows, dtype=f32),
            shape(tok_rows, H * HD),
            shape(tok_rows, model_width, dtype=f32),
            shape(tok_rows, model_width),
            shape(seq_len, model_width),
        ),
        "attention_forward",
        hbm=(1, 4),
        hbm_out=(0, 1, 2, 7),
        scratch=(
            pltpu.VMEM((model_width, H * HD), low),
            pltpu.VMEM((H * HD, model_width), low),
            pltpu.VMEM((tok_rows, H * HD), low),
            pltpu.VMEM((KV, seq_len, LANES), low),
            pltpu.VMEM((KV, seq_len, LANES), low),
            pltpu.VMEM((seq_len, model_width), low),
            pltpu.SemaphoreType.DMA((2,)),
            pltpu.SemaphoreType.DMA((4,)),
        ),
    )(
        info, w_query, w_key, w_value, w_output, gain_one, gain_two, cosine, sine, *tokens_blocks,
    )

    normed2, *cot_even = lax.optimization_barrier((normed2, *cot_even))
    cot_blocks = gather_odd(cot_even)
    n2_blocks = gather(normed2, 2)
    attended_even = gather_even(attended, 1)
    n_blocks = 2 * groups
    all_rows = n_blocks * tok_rows
    wide = model_width + LANES

    dma = pltpu.SemaphoreType.DMA
    units = half_units * exp_dev
    wide_acts = 3 * half_units + LANES
    sums, acts = call(
        lambda *refs: experts_kernel(*refs, n_blocks=n_blocks, experts=experts, tiles=2),
        (
            shape(model_width, 3 * units),
            shape(exp_dev, all_rows, wide_acts),
        ),
        "experts",
        limit=48 if all_rows <= 1024 else LIMIT_MIB,
        hbm=tuple(range(2, 5 + 2 * n_blocks)),
        hbm_out=(0, 1),
        scratch=(
            pltpu.VMEM((all_rows, model_width), low),
            pltpu.VMEM((all_rows, model_width), low),
            pltpu.VMEM((all_rows, LANES), low),
            pltpu.VMEM((exp_dev, model_width, 2 * half_units), low),
            pltpu.VMEM((exp_dev, half_units, model_width), low),
            pltpu.VMEM((exp_dev, all_rows, wide_acts), low),
            pltpu.VMEM((exp_dev, model_width, 3 * half_units), low),
            pltpu.VMEM((all_rows, LANES), f32),
            pltpu.VMEM((model_width, LANES), low),
            pltpu.VMEM((all_rows, LANES), f32),
            dma((n_blocks,)),
            dma((n_blocks,)),
            dma((n_blocks,)),
            dma((exp_dev, 3)),
            dma((exp_dev, 3)),
        ),
    )(info, w_router, w_gate, w_up, w_down, *cot_blocks, *n2_blocks)
    outer = copies // 2
    shard_rows = model_width // copies
    reduced = lax.psum_scatter(
        sums,
        "dp",
        scatter_dimension=0,
        axis_index_groups=[[2 * o + p for o in range(outer)] for p in range(2)],
        tiled=True,
    )

    odd, even = call(
        rows_kernel,
        (shape(groups, tok_rows, wide), shape(groups, tok_rows, wide, dtype=f32)),
        "experts_rows",
        hbm=(1, 2, 3),
        hbm_out=(0, 1),
        scratch=(
            pltpu.VMEM((exp_dev, model_width, 2 * half_units), low),
            pltpu.VMEM((exp_dev, all_rows, 2 * half_units), low),
            pltpu.VMEM((all_rows, model_width), f32),
            pltpu.VMEM((all_rows, LANES), low),
            pltpu.VMEM((groups, tok_rows, wide), low),
            pltpu.VMEM((groups, tok_rows, wide), f32),
            dma((exp_dev, 3)),
            dma((4,)),
            dma((1,)),
        ),
    )(info, w_gate, w_up, acts)
    odd, *attended_even = lax.optimization_barrier((odd, *attended_even))
    mine = core_sum(odd, even)
    arrived = swap(mine, 2)
    attended_blocks = gather_odd(attended_even)

    (
        grad_hidden, grad_branch, grad_query, kv_odd, kv_even, grad_normed_q, mix_odd, mix_even
    ) = call(
        lambda *refs: backward_kernel(*refs, experts=experts),
        (
            shape(tok_rows, model_width, dtype=f32),
            shape(tok_rows + small_rows(experts + 1), model_width),
            shape(tok_rows, H * HD),
            shape(groups // 2, tok_rows, 2 * KV * HD),
            shape(groups // 2, tok_rows, 2 * KV * HD, dtype=f32),
            shape(tok_rows, model_width, dtype=f32),
            shape(groups, tok_rows, model_width),
            shape(groups, tok_rows, model_width, dtype=f32),
        ),
        "attention_backward",
        hbm=(12, 13, 14, 15, 16),
        hbm_out=(6, 7),
        scratch=(
            pltpu.VMEM((model_width, LANES), low),
            pltpu.VMEM((KV, seq_len, LANES), low),
            pltpu.VMEM((KV, seq_len, LANES), low),
            pltpu.VMEM((model_width, H * HD), low),
            pltpu.VMEM((all_rows, units), low),
            pltpu.VMEM((units, model_width), low),
            pltpu.VMEM((groups, tok_rows, model_width), low),
            pltpu.VMEM((groups, tok_rows, model_width), f32),
            dma((3,)),
            dma((2 * exp_dev,)),
        ),
    )(
        info, mine[0], cot_mask, normed2, hidden_state, w_router, gain_two, w_output,
        q_low, lse, cosine, sine, k_two, v_two, w_query, acts, w_down, *arrived,
    )
    kv_mine = core_sum(kv_odd, kv_even)
    kv_arrived = swap(kv_mine, 1)
    mix_odd, kv_mine = lax.optimization_barrier((mix_odd, kv_mine))
    mix_got = send(mix_odd, 0, 1)
    n_own = groups // 2
    mix_got_pair = send(
        (mix_even[n_own:] + mix_got[n_own:].astype(f32)).astype(low), 1, 0
    )
    query_later, grad_branch, *kv_arrived = lax.optimization_barrier(
        (grad_query, grad_branch, *kv_arrived)
    )
    branch_even = gather_even(grad_branch, 1)
    query_even = gather_even(query_later, 1)
    grad_kv, grad_tokens = call(
        tokens_kernel,
        (
            shape(tok_rows + small_rows(1), 2 * KV * HD),
            shape(tok_rows, model_width),
        ),
        "tokens_backward",
        smem=False,
    )(
        kv_mine[0], grad_normed_q, w_key, w_value, tokens, gain_one, grad_hidden, cosine, sine,
        *kv_arrived,
    )
    grad_kv, mix_got_pair, *later = lax.optimization_barrier(
        (grad_kv, mix_got_pair, *branch_even, *query_even)
    )
    kv_even_blocks = gather_even(grad_kv, 1)
    branch_blocks = gather_odd(later[: len(branch_even)])
    query_blocks = gather_odd(later[len(branch_even) :])
    own_rows = model_width // (copies * groups)
    n_early, n_late = model_width + LANES + H * HD, 2 * KV * HD + LANES
    select = pltpu.VMEM((copies * own_rows, model_width), low)
    early_odd, early_even, normed1_t = call(
        lambda *refs: early_dense_kernel(*refs, groups=groups, count=experts + 1),
        (
            shape(outer, own_rows, n_early),
            shape(outer, own_rows, n_early, dtype=f32),
            shape(copies * own_rows, seq_len),
        ),
        "dense_early",
        scratch=(select,),
    )(info, normed1_all, *attended_blocks, *branch_blocks, *query_blocks)
    early = early_even + send(early_odd, 1, 0).astype(f32)
    _, *kv_even_blocks = lax.optimization_barrier((early_odd, *kv_even_blocks))
    kv_blocks = gather_odd(kv_even_blocks)
    late_odd, late_even = call(
        lambda *refs: late_dense_kernel(*refs, lane=experts + 1),
        (shape(outer, own_rows, n_late), shape(outer, own_rows, n_late, dtype=f32)),
        "dense_late",
        scratch=(select,),
    )(info, normed1_t, *kv_blocks)
    mix_got_pair, late_odd = lax.optimization_barrier((mix_got_pair, late_odd))
    mix_pair = mix_even[:n_own] + mix_got[:n_own].astype(f32) + mix_got_pair.astype(f32)
    mixture = mix_pair[0]
    for a in swap(mix_pair, 1):
        mixture = mixture + a.astype(f32)
    block_out = (hidden_state + mixture).astype(low)
    late = late_even + send(late_odd, 1, 0).astype(f32)
    o_end, k_end = model_width + LANES, 2 * KV * HD
    dense_send = jnp.concatenate(
        [
            early[1:, :, :model_width],
            early[1:, :, model_width:o_end] + late[1:, :, k_end:],
            early[1:, :, o_end:],
            late[1:, :, :k_end],
        ],
        axis=2,
    ).astype(low)

    swapped = send(
        lax.dynamic_slice_in_dim(reduced, (1 - half) * shard_rows, shard_rows, 0), 1, 0
    )
    _, dense_send = lax.optimization_barrier((reduced, dense_send))
    dense_arrived = [send(dense_send[o - 1], 2 * o, 0) for o in range(1, outer)]
    k_cols = KV * HD
    (
        grad_gate_w, grad_up_w, grad_down_w, grad_query_w, grad_key_w, grad_value_w,
        grad_output_w, grad_router, grad_norm1, grad_norm2,
    ) = call(
        lambda *refs: final_kernel(*refs, n_early=n_early, n_late=n_late),
        (
            shape(exp_dev, shard_rows, hidden_units, dtype=f32),
            shape(exp_dev, shard_rows, hidden_units, dtype=f32),
            shape(exp_dev, hidden_units, shard_rows, dtype=f32),
            shape(own_rows, H * HD, dtype=f32),
            shape(own_rows, k_cols, dtype=f32),
            shape(own_rows, k_cols, dtype=f32),
            shape(own_rows, model_width, dtype=f32),
            shape(experts, own_rows, dtype=f32),
            shape(1, own_rows, dtype=f32),
            shape(1, own_rows, dtype=f32),
        ),
        "place",
        limit=48,
    )(info, reduced, swapped, early, late, *dense_arrived)
    return (
        block_out,
        grad_tokens,
        grad_norm1[0],
        grad_query_w,
        grad_key_w,
        grad_value_w,
        grad_output_w,
        grad_norm2[0],
        grad_router.T,
        grad_gate_w,
        grad_up_w,
        grad_down_w,
    )


def solution(mesh):
    return jax.shard_map(
        shards,
        mesh=mesh,
        in_specs=(
            P(("dp", "expert"), None),
            P("dp"),
            P(("dp", "expert"), None),
            P(),
            P(),
            P(),
            P(),
            P(),
            P(),
            P(),
            P("expert", None, None),
            P("expert", None, None),
            P("expert", None, None),
            P(("dp", "expert"), None),
        ),
        out_specs=(
            P(("dp", "expert"), None),
            P(("dp", "expert"), None),
            P(("dp", "expert")),
            P(("dp", "expert"), None),
            P(("dp", "expert"), None),
            P(("dp", "expert"), None),
            P(("dp", "expert"), None),
            P(("dp", "expert")),
            P(("dp", "expert"), None),
            P("expert", "dp", None),
            P("expert", "dp", None),
            P("expert", None, "dp"),
        ),
        check_vma=False,
    )
```

```python
import math

import jax
import jax.numpy as jnp
from jax import lax
from jax.experimental import pallas as pl
from jax.experimental.pallas import tpu as pltpu
from jax.sharding import PartitionSpec as P

H = 16
KV = 8
HD = 64


norm_eps = 1e-05
masked_score = -1e30


def rope_tables(me, tok_rows, groups):
    lane = lax.broadcasted_iota(jnp.int32, (1, LANES), 1)
    frequency = jnp.exp((lane % (HD // 2)).astype(jnp.float32) * (-2.0 * math.log(10000.0) / HD))
    place = lax.broadcasted_iota(jnp.int32, (tok_rows, LANES), 0).astype(jnp.float32)
    start = (lax.broadcasted_iota(jnp.int32, (groups, LANES), 0) ^ me) * tok_rows
    inner, outer = place * frequency, start.astype(jnp.float32) * frequency
    cos_in, sin_in = jnp.cos(inner)[None], jnp.sin(inner)[None]
    cos_out, sin_out = jnp.cos(outer)[:, None], jnp.sin(outer)[:, None]
    cosine = (cos_out * cos_in - sin_out * sin_in).reshape(groups * tok_rows, LANES)
    sine = (sin_out * cos_in + cos_out * sin_in).reshape(groups * tok_rows, LANES)
    return cosine, jnp.where(lane % HD < HD // 2, -sine, sine)


LANES = 128
LIMIT_MIB = 63


def norm_forward(source, gain_vec):
    inverse = lax.rsqrt(jnp.mean(source * source, axis=-1, keepdims=True) + norm_eps)
    return (source * inverse * gain_vec, inverse)


def norm_backward(source, inverse, gain_vec, upstream):
    weighted = upstream * gain_vec
    cubed = inverse * inverse * inverse
    back = inverse * weighted - source * cubed * jnp.mean(weighted * source, axis=-1, keepdims=True)
    return (back, jnp.sum(upstream * source * inverse, axis=0, keepdims=True))


def dot(left, right, left_dim=1, right_dim=0):
    return lax.dot_general(
        left, right, (((left_dim,), (right_dim,)), ((), ())), preferred_element_type=jnp.float32
    )


def lane_of(shape):
    return lax.broadcasted_iota(jnp.int32, shape, 1)


def swap_halves(source):
    lane = lane_of(source.shape)
    return jnp.where(
        lane % HD < HD // 2,
        pltpu.roll(source, LANES - HD // 2, 1),
        pltpu.roll(source, HD // 2, 1),
    )


def rope(source, cosine_table, sine_table):
    return source * cosine_table + swap_halves(source) * sine_table


def unrope(upstream, cosine_table, sine_table):
    return upstream * cosine_table - swap_halves(upstream) * sine_table


def twice(pair):
    lane = lane_of(pair.shape)
    other = pltpu.roll(pair, HD, 1)
    return (jnp.where(lane < HD, pair, other), jnp.where(lane < HD, other, pair))


def stack_heads(pair):
    lane = lane_of(pair.shape)
    zero = jnp.zeros_like(pair)
    return jnp.concatenate(
        [jnp.where(lane < HD, pair, zero), jnp.where(lane < HD, zero, pair)], axis=0
    )


def join_heads(stacked):
    rows = stacked.shape[0] // 2
    lane = lane_of((rows, LANES))
    return jnp.where(lane < HD, stacked[:rows], stacked[rows:])


def allowed_mask(info_ref, seq_len, rows):
    me, prefix = info_ref[0], info_ref[1]
    key = lax.broadcasted_iota(jnp.int32, (seq_len, 2 * rows), 0)
    query = lax.broadcasted_iota(jnp.int32, (seq_len, 2 * rows), 1) % rows + me * rows
    key_pos = ((key // rows) ^ me) * rows + key % rows
    return (key_pos <= query) | (key_pos < prefix)


def forward_kernel(
    info_ref, wq_ref, wk_ref, wv_ref, wo_ref, gain_one_ref, gain_two_ref, cos_ref, sin_ref, *rest
):
    blocks, outs = rest[:-16], rest[-16:]
    q_out, k_out, v_out, lse_ref, att_ref, hid_ref, n2_ref, n1_out = outs[:8]
    wq_held, wo_held, q_ref, k_ref, v_ref, n1_ref, sems, out_sems = outs[8:]
    copies = start_copies([(wq_ref, wq_held), (wo_ref, wo_held)], sems)
    tokens_ref = blocks[0]
    rows = tokens_ref.shape[0]
    seq_len = rows * len(blocks)
    for n, b in enumerate(blocks):
        n1_ref[n * rows : (n + 1) * rows, :] = norm_forward(
            b[...].astype(jnp.float32), gain_one_ref[...]
        )[0].astype(jnp.bfloat16)
    normed = n1_ref[...]
    out_copies = start_copies([(n1_ref, n1_out)], out_sems)
    cosine, sine = cos_ref[...], sin_ref[...]
    keys = dot(normed, wk_ref[...])
    values = dot(normed, wv_ref[...])
    for c in range(KV // 2):
        cols = slice(c * LANES, (c + 1) * LANES)
        first, second = twice(rope(keys[:, cols], cosine, sine))
        k_ref[2 * c] = first.astype(jnp.bfloat16)
        k_ref[2 * c + 1] = second.astype(jnp.bfloat16)
        first, second = twice(values[:, cols])
        v_ref[2 * c] = first.astype(jnp.bfloat16)
        v_ref[2 * c + 1] = second.astype(jnp.bfloat16)
    out_copies += start_copies([(k_ref, k_out), (v_ref, v_out)], out_sems.at[pl.ds(1, 2)])
    allowed = allowed_mask(info_ref, seq_len, rows)
    wait_all(copies[:1])
    query_pre = dot(n1_ref[:rows, :], wq_held[...])
    for h in range(KV):
        cols = slice(h * LANES, (h + 1) * LANES)
        query = rope(query_pre[:, cols], cosine[:rows], sine[:rows]) * (1.0 / math.sqrt(HD))
        q_ref[:, cols] = query.astype(jnp.bfloat16)
        stacked = stack_heads(query).astype(jnp.bfloat16)
        scores = jnp.where(allowed, dot(k_ref[h], stacked, 1, 1), masked_score)
        row_max = jnp.max(scores, axis=0, keepdims=True)
        exps = jnp.exp(scores - row_max)
        total = jnp.sum(exps, axis=0, keepdims=True)
        lse_ref[h : h + 1, :] = row_max + jnp.log(total)
        prob = (exps * (1.0 / total)).astype(jnp.bfloat16)
        att_ref[:, cols] = join_heads(dot(prob, v_ref[h], 0, 0)).astype(jnp.bfloat16)
    out_copies += start_copies([(q_ref, q_out)], out_sems.at[pl.ds(3, 1)])
    wait_all(copies[1:])
    hidden = tokens_ref[...].astype(jnp.float32) + dot(att_ref[...], wo_held[...])
    hid_ref[...] = hidden
    n2_ref[...] = norm_forward(hidden, gain_two_ref[...])[0].astype(jnp.bfloat16)
    wait_all(out_copies)


def start_copies(pairs, sems):
    copies = describe(pairs, sems)
    for c in copies:
        c.start()
    return copies


def wait_all(copies):
    for c in copies:
        c.wait()


def own_half(info_ref, fh):
    return pl.ds(pl.multiple_of(info_ref[2] * fh, fh), fh)


def expert_parts(info_ref, wg_ref, wu_ref, w_ref, e):
    fh = wg_ref.shape[2] // 2
    mine = own_half(info_ref, fh)
    return [
        (wg_ref.at[e, :, mine], w_ref.at[e, :, pl.ds(0, fh)]),
        (wu_ref.at[e, :, mine], w_ref.at[e, :, pl.ds(fh, fh)]),
    ]


def down_part(info_ref, wd_ref, down_ref, e):
    mine = own_half(info_ref, wd_ref.shape[1] // 2)
    return [(wd_ref.at[e, mine, :], down_ref.at[e])]


def describe(pairs, sems):
    return [pltpu.make_async_copy(src, dst, sems.at[n]) for n, (src, dst) in enumerate(pairs)]


def row_parts(blocks, into, cols):
    rows = blocks[0].shape[0]
    return [(b.at[:, cols], into.at[pl.ds(n * rows, rows), :]) for n, b in enumerate(blocks)]


def widen(router_ref, wide_ref):
    wide_ref[...] = jnp.zeros_like(wide_ref)
    wide_ref[:, : router_ref.shape[1]] = router_ref[...]


def routing(routed, logits):
    logits = jnp.where(routed, logits, masked_score)
    exps = jnp.where(routed, jnp.exp(logits - jnp.max(logits, axis=-1, keepdims=True)), 0.0)
    return exps / jnp.sum(exps, axis=-1, keepdims=True)


def experts_kernel(
    info_ref, router_ref, wg_ref, wu_ref, wd_ref, *rest, n_blocks, experts, tiles
):
    cot_blocks, n2_blocks = rest[:n_blocks], rest[n_blocks : 2 * n_blocks]
    sums_out, acts_out = rest[2 * n_blocks : 2 * n_blocks + 2]
    (
        n2_ref, g_ref, routed_ref, w_ref, down_ref, acts_ref, sums_ref, probs_ref, router_wide,
        extra_ref,
    ) = rest[2 * n_blocks + 2 : 2 * n_blocks + 12]
    n2_sems, routed_sems, g_sems, w_sems, out_sems = rest[2 * n_blocks + 12 :]
    exp_dev, width, units = wg_ref.shape
    rows = n2_blocks[0].shape[0]
    fh = units // 2
    n2_copies = start_copies(row_parts(n2_blocks, n2_ref, pl.ds(0, width)), n2_sems)
    routed_copies = start_copies(row_parts(cot_blocks, routed_ref, pl.ds(width, LANES)), routed_sems)

    def weights(e):
        pairs = expert_parts(info_ref, wg_ref, wu_ref, w_ref, e)
        return describe(pairs + down_part(info_ref, wd_ref, down_ref, e), w_sems.at[e])

    def results(e):
        two = pl.ds(pl.multiple_of(e * 3 * fh, fh), 2 * fh)
        one = pl.ds(pl.multiple_of((3 * e + 2) * fh, fh), fh)
        return describe(
            [
                (acts_ref.at[e], acts_out.at[e]),
                (sums_ref.at[e, :, pl.ds(0, 2 * fh)], sums_out.at[:, two]),
                (sums_ref.at[e, :, pl.ds(2 * fh, fh)], sums_out.at[:, one]),
            ],
            out_sems.at[e],
        )

    for c in weights(0):
        c.start()
    widen(router_ref, router_wide)
    extra_ref[...] = jnp.zeros_like(extra_ref)
    wait_all(n2_copies)
    wait_all(routed_copies)
    g_copies = start_copies(row_parts(cot_blocks, g_ref, pl.ds(0, width)), g_sems)
    probs_ref[...] = routing(
        routed_ref[...].astype(jnp.float32) > 0.5, dot(n2_ref[...], router_wide[...])
    )
    wait_all(g_copies)
    step = n2_ref.shape[0] // tiles

    def one_expert(e, carry):
        wait_all(weights(e))

        @pl.when(e + 1 < exp_dev)
        def _():
            for c in weights(e + 1):
                c.start()

        spot = info_ref[0] * exp_dev + e
        for t in range(tiles):
            part = slice(t * step, (t + 1) * step)
            pre = dot(n2_ref[part, :], w_ref[e])
            gate_pre, up_pre = pre[:, :fh], pre[:, fh:]
            back = dot(g_ref[part, :], down_ref[e], 1, 1)
            sig = 0.5 * jnp.tanh(0.5 * gate_pre) + 0.5
            silu = gate_pre * sig
            act = silu * up_pre
            here = lane_of((step, LANES)) == spot
            weight = jnp.sum(jnp.where(here, probs_ref[part, :], 0.0), axis=1, keepdims=True)
            extra_ref[part, :] += jnp.where(here, jnp.sum(act * back, axis=1, keepdims=True), 0.0)
            grad_active = weight * back
            acts_ref[e, part, :fh] = (
                grad_active * up_pre * (sig + silu * (1.0 - sig))
            ).astype(jnp.bfloat16)
            acts_ref[e, part, fh : 2 * fh] = (grad_active * silu).astype(jnp.bfloat16)
            acts_ref[e, part, 2 * fh : 3 * fh] = (weight * act).astype(jnp.bfloat16)
            found = extra_ref[part, :]
            high = found.astype(jnp.bfloat16).astype(jnp.float32)
            lower = (found - high).astype(jnp.bfloat16).astype(jnp.float32)
            acts_ref[e, part, 3 * fh :] = (high + pltpu.roll(lower, experts, 1)).astype(
                jnp.bfloat16
            )
        leaving = results(e)
        leaving[0].start()
        sums_ref[e, :, : 2 * fh] = dot(n2_ref[...], acts_ref[e, :, : 2 * fh], 0, 0).astype(
            jnp.bfloat16
        )
        leaving[1].start()
        sums_ref[e, :, 2 * fh :] = dot(g_ref[...], acts_ref[e, :, 2 * fh : 3 * fh], 0, 0).astype(
            jnp.bfloat16
        )
        leaving[2].start()
        return carry

    lax.fori_loop(0, exp_dev, one_expert, 0)
    for e in range(exp_dev):
        wait_all(results(e))


def put_rows(values, t, odd_ref, even_ref, cols):
    rows = odd_ref.shape[1]
    count = values.shape[0] // rows
    for i in range(count):
        n = t * count + i
        out = odd_ref if n % 2 else even_ref
        out[n // 2, :, cols] = values[i * rows : (i + 1) * rows].astype(out.dtype)


def rows_kernel(
    info_ref, wg_ref, wu_ref, acts_in, odd_out, even_out, w_ref, gu_ref, total_ref, extra_ref,
    odd_ref, even_ref, w_sems, out_sems, extra_sems
):
    exp_dev, width, _ = wg_ref.shape
    all_rows, two = gu_ref.shape[1:]
    extra_part = pl.ds(3 * two // 2, LANES)
    extra_copy = start_copies([(acts_in.at[exp_dev - 1, :, extra_part], extra_ref)], extra_sems)

    def operands(e):
        pairs = expert_parts(info_ref, wg_ref, wu_ref, w_ref, e)
        acts = acts_in.at[e, :, pl.ds(0, two)]
        return describe(pairs + [(acts, gu_ref.at[e])], w_sems.at[e])

    for c in operands(0):
        c.start()
    wait_all(extra_copy)
    put_rows(
        extra_ref[...].astype(jnp.float32), 0, odd_ref, even_ref, slice(width, width + LANES)
    )
    total_ref[...] = jnp.zeros_like(total_ref)

    def one_expert(e, carry):
        wait_all(operands(e))
        for c in operands(e + 1):
            c.start()
        total_ref[...] += dot(gu_ref[e], w_ref[e], 1, 1)
        return carry

    lax.fori_loop(0, exp_dev - 1, one_expert, 0)
    wait_all(operands(exp_dev - 1))
    out_copies = []
    for t in range(2):
        part = slice(t * all_rows // 2, (t + 1) * all_rows // 2)
        new = total_ref[part, :] + dot(gu_ref[exp_dev - 1, part, :], w_ref[exp_dev - 1], 1, 1)
        put_rows(new, t, odd_ref, even_ref, slice(0, width))
        share = pl.ds(t * odd_ref.shape[0] // 2, odd_ref.shape[0] // 2)
        out_copies += start_copies(
            [(odd_ref.at[share], odd_out.at[share]), (even_ref.at[share], even_out.at[share])],
            out_sems.at[pl.ds(2 * t, 2)],
        )
    wait_all(out_copies)


def final_kernel(
    info_ref, sums_ref, arrived_ref, early_ref, late_ref, *rest, n_early, n_late
):
    dense = rest[:-10]
    gate_ref, up_ref, down_ref, wq_ref, wk_ref, wv_ref, wo_ref, router_ref, one_ref, two_ref = rest[-10:]
    exp_dev, rows, units = gate_ref.shape
    fh = units // 2
    half = info_ref[2]
    kept = sums_ref[pl.ds(pl.multiple_of(half * rows, rows), rows), :]
    got = arrived_ref[...]
    first = jnp.where(half == 0, kept, got).astype(jnp.float32)
    second = jnp.where(half == 0, got, kept).astype(jnp.float32)
    for e in range(exp_dev):
        at = 3 * e * fh
        gate_ref[e, :, :fh] = first[:, at : at + fh]
        gate_ref[e, :, fh:] = second[:, at : at + fh]
        up_ref[e, :, :fh] = first[:, at + fh : at + 2 * fh]
        up_ref[e, :, fh:] = second[:, at + fh : at + 2 * fh]
        at = (3 * e + 2) * fh
        down_ref[e, :fh, :] = first[:, at : at + fh].T
        down_ref[e, fh:, :] = second[:, at : at + fh].T
    early, late = early_ref[0], late_ref[0]
    late_kv = late[:, : 2 * wk_ref.shape[1]]
    for d in dense:
        early = early + d[:, :n_early].astype(jnp.float32)
        late_kv = late_kv + d[:, n_early:].astype(jnp.float32)
    width, k_cols = wo_ref.shape[1], wk_ref.shape[1]
    wo_ref[...] = early[:, :width]
    wq_ref[...] = early[:, width + LANES :]
    wk_ref[...] = late_kv[:, :k_cols]
    wv_ref[...] = late_kv[:, k_cols:]
    small = early[:, width : width + LANES] + late[:, 2 * k_cols :]
    small = small.T
    router_ref[...] = small[1 : 1 + router_ref.shape[0], :]
    two_ref[...] = small[:1, :]
    one = 1 + router_ref.shape[0]
    one_ref[...] = small[one : one + 1, :]


def selection(info_ref, select_ref, own_rows):
    count, width = select_ref.shape
    groups = width // count
    row = lax.broadcasted_iota(jnp.int32, (count, width), 0)
    col = lax.broadcasted_iota(jnp.int32, (count, width), 1)
    want = ((row // own_rows) ^ info_ref[3]) * (own_rows * groups) + (
        info_ref[0] * own_rows + row % own_rows
    )
    select_ref[...] = jnp.where(col == want, 1.0, 0.0).astype(jnp.bfloat16)


def pick_small(blocks, rows, count, select):
    total = blocks[0][rows : rows + 2 * count].astype(jnp.float32)
    for b in blocks[1:]:
        total = total + b[rows : rows + 2 * count].astype(jnp.float32)
    total = jnp.concatenate(
        [total[:count] + total[count:], jnp.zeros((LANES - count, total.shape[1]), jnp.float32)],
        axis=0,
    )
    high = total.astype(jnp.bfloat16)
    lower = (total - high.astype(jnp.float32)).astype(jnp.bfloat16)
    return dot(select, high, 1, 1) + dot(select, lower, 1, 1)


def put_shares(values, odd_ref, even_ref, at):
    rows = odd_ref.shape[1]
    for n in range(2 * odd_ref.shape[0]):
        out = odd_ref if n % 2 else even_ref
        out[n // 2, :, at : at + values.shape[1]] = values[n * rows : (n + 1) * rows].astype(
            out.dtype
        )


def early_dense_kernel(info_ref, *rest, groups, count):
    attended, branch, query = (rest[1 + n * groups : 1 + (n + 1) * groups] for n in range(3))
    odd_ref, even_ref, normed_t_ref, select_ref = rest[1 + 3 * groups :]
    rows, width = attended[0].shape
    selection(info_ref, select_ref, odd_ref.shape[1])
    select = select_ref[...]

    def seq(blocks):
        return jnp.concatenate([b[:rows] for b in blocks], axis=0)

    normed_t = dot(select, rest[0][...], 1, 1).astype(jnp.bfloat16)
    normed_t_ref[...] = normed_t
    attended_t = dot(select, seq(attended), 1, 1).astype(jnp.bfloat16)
    put_shares(dot(attended_t, seq(branch)), odd_ref, even_ref, 0)
    put_shares(pick_small(branch, rows, count, select), odd_ref, even_ref, width)
    put_shares(dot(normed_t, seq(query)), odd_ref, even_ref, width + LANES)


def late_dense_kernel(info_ref, normed_t_ref, *rest, lane):
    blocks = rest[:-3]
    odd_ref, even_ref, select_ref = rest[-3:]
    rows = normed_t_ref.shape[1] // len(blocks)
    selection(info_ref, select_ref, odd_ref.shape[1])
    kv = jnp.concatenate([b[:rows] for b in blocks], axis=0)
    put_shares(dot(normed_t_ref[...], kv), odd_ref, even_ref, 0)
    small = pltpu.roll(pick_small(blocks, rows, 1, select_ref[...]), lane, 1)
    put_shares(small, odd_ref, even_ref, kv.shape[1])


def small_rows(count):
    return -(-2 * count // 16) * 16


def put_small(ref, start, values):
    count = values.shape[0]
    high = values.astype(jnp.bfloat16).astype(jnp.float32)
    fill = jnp.zeros((small_rows(count) - 2 * count, values.shape[1]), jnp.float32)
    ref[start:] = jnp.concatenate([high, values - high, fill], axis=0).astype(jnp.bfloat16)


def backward_kernel(
    info_ref, own_ref, cot_ref, n2_ref, hid_ref, router_ref, gain_ref, wo_ref, q_ref,
    lse_ref, cos_ref, sin_ref, k_hbm, v_hbm, wq_hbm, acts_hbm, wd_hbm, *rest, experts
):
    arrived, outs = rest[:-18], rest[-18:]
    ghid_ref, branch_ref, dq_ref, odd_ref, even_ref, gn_ref, mix_odd_out, mix_even_out = outs[:8]
    (
        router_wide, k_ref, v_ref, wq_ref, scaled_ref, down_ref, mix_odd_ref, mix_even_ref, sems,
        mix_sems,
    ) = outs[8:]
    late = start_copies([(k_hbm, k_ref), (v_hbm, v_ref), (wq_hbm, wq_ref)], sems)
    exp_dev, units, _ = wd_hbm.shape
    fh = units // 2
    pairs = []
    for e in range(exp_dev):
        part = pl.ds(e * fh, fh)
        pairs += [(wd_hbm.at[e, own_half(info_ref, fh), :], down_ref.at[part, :])]
        pairs += [(acts_hbm.at[e, :, pl.ds(2 * fh, fh)], scaled_ref.at[:, part])]
    mix_copies = start_copies(pairs, mix_sems)
    widen(router_ref, router_wide)
    rows, width = hid_ref.shape
    summed = own_ref[...]
    for a in arrived:
        summed = summed + a[...].astype(jnp.float32)
    extra = summed[:, width:]
    gate_grads = extra + pltpu.roll(extra, LANES - experts, 1)
    routed = cot_ref[:, width:].astype(jnp.float32) > 0.5
    gate = routing(routed, dot(n2_ref[...], router_wide[...]))
    grad_logits = (
        gate * (gate_grads - jnp.sum(gate * gate_grads, axis=-1, keepdims=True))
    ).astype(jnp.bfloat16)
    router_grad = dot(grad_logits, n2_ref[...], 0, 0)
    grad_normed = summed[:, :width] + dot(grad_logits, router_wide[...], 1, 1)
    hidden = hid_ref[...]
    inverse = lax.rsqrt(jnp.mean(hidden * hidden, axis=-1, keepdims=True) + norm_eps)
    back, norm_grad = norm_backward(hidden, inverse, gain_ref[...], grad_normed)
    grad_hidden = cot_ref[:, :width].astype(jnp.float32) + back
    ghid_ref[...] = grad_hidden
    branch = grad_hidden.astype(jnp.bfloat16)
    branch_ref[:rows] = branch
    put_small(branch_ref, rows, jnp.concatenate([norm_grad, router_grad[:experts]], axis=0))
    grad_attended = dot(branch, wo_ref[...], 1, 1).astype(jnp.bfloat16)
    wait_all(late[:2])
    seq_len = k_ref.shape[1]
    allowed = allowed_mask(info_ref, seq_len, rows)
    cosine, sine = cos_ref[:rows, :], sin_ref[:rows, :]
    lane = lane_of((seq_len, LANES))
    kept = [None, None]
    for h in range(KV):
        cols = slice(h * LANES, (h + 1) * LANES)
        stacked = stack_heads(q_ref[:, cols])
        grad_stacked = stack_heads(grad_attended[:, cols])
        keys = k_ref[h]
        scores = jnp.where(allowed, dot(keys, stacked, 1, 1), masked_score)
        prob = jnp.exp(scores - lse_ref[h : h + 1, :])
        grad_prob = dot(v_ref[h], grad_stacked, 1, 1)
        delta = jnp.sum(prob * grad_prob, axis=0, keepdims=True)
        grad_scores = (prob * (grad_prob - delta)).astype(jnp.bfloat16)
        dq = join_heads(dot(grad_scores, keys, 0, 0)) * (1.0 / math.sqrt(HD))
        dq_ref[:, cols] = unrope(dq, cosine, sine).astype(jnp.bfloat16)
        parts = (dot(grad_scores, stacked), dot(prob.astype(jnp.bfloat16), grad_stacked))
        for n in range(2):
            both = parts[n] + pltpu.roll(parts[n], HD, 1)
            if h % 2 == 0:
                kept[n] = both
                continue
            pair = jnp.where(lane < HD, kept[n], both)
            start = (n * KV // 2 + h // 2) * LANES
            put_rows(pair, 0, odd_ref, even_ref, slice(start, start + LANES))
    wait_all(mix_copies)
    tokens = scaled_ref.shape[0] // 2
    out_copies = []
    for t in range(2):
        mix = dot(scaled_ref[t * tokens : (t + 1) * tokens, :], down_ref[...])
        put_rows(mix, t, mix_odd_ref, mix_even_ref, slice(0, width))
        share = pl.ds(t * mix_odd_ref.shape[0] // 2, mix_odd_ref.shape[0] // 2)
        out_copies += start_copies(
            [
                (mix_odd_ref.at[share], mix_odd_out.at[share]),
                (mix_even_ref.at[share], mix_even_out.at[share]),
            ],
            mix_sems.at[pl.ds(2 * t, 2)],
        )
    wait_all(late[2:])
    gn_ref[...] = dot(dq_ref[...], wq_ref[...], 1, 1)
    wait_all(out_copies)


def tokens_kernel(
    own_ref, gn_ref, wk_ref, wv_ref, tokens_ref, gain_ref, ghid_ref, cos_ref, sin_ref, *rest
):
    arrived, (kv_ref, out_ref) = rest[:-2], rest[-2:]
    rows = tokens_ref.shape[0]
    summed = own_ref[...]
    for a in arrived:
        summed = summed + a[...].astype(jnp.float32)
    k_cols = KV * HD
    for c in range(k_cols // LANES):
        cols = slice(c * LANES, (c + 1) * LANES)
        kv_ref[:rows, cols] = unrope(summed[:, cols], cos_ref[:rows, :], sin_ref[:rows, :]).astype(
            jnp.bfloat16
        )
    kv_ref[:rows, k_cols:] = summed[:, k_cols:].astype(jnp.bfloat16)
    grad_normed = (
        gn_ref[...]
        + dot(kv_ref[:rows, :k_cols], wk_ref[...], 1, 1)
        + dot(kv_ref[:rows, k_cols:], wv_ref[...], 1, 1)
    )
    source = tokens_ref[...].astype(jnp.float32)
    inverse = lax.rsqrt(jnp.mean(source * source, axis=-1, keepdims=True) + norm_eps)
    back, norm_grad = norm_backward(source, inverse, gain_ref[...], grad_normed)
    put_small(kv_ref, rows, norm_grad)
    out_ref[...] = (ghid_ref[...] + back).astype(jnp.bfloat16)


def call(kernel, out_shape, name, hbm=(), hbm_out=(), scratch=(), smem=True, limit=LIMIT_MIB):
    def run(*args):
        specs = [
            pl.BlockSpec(memory_space=pl.ANY if n in hbm else pltpu.VMEM)
            for n in range(len(args))
        ]
        if smem:
            specs[0] = pl.BlockSpec(memory_space=pltpu.SMEM)
        return pl.pallas_call(
            kernel,
            out_shape=out_shape,
            in_specs=specs,
            out_specs=[
                pl.BlockSpec(memory_space=pl.ANY if n in hbm_out else pltpu.VMEM)
                for n in range(len(out_shape))
            ],
            scratch_shapes=list(scratch),
            compiler_params=pltpu.CompilerParams(vmem_limit_bytes=limit * 1024 * 1024),
            name=name,
        )(*args)

    return run


def shape(*dims, dtype=jnp.bfloat16):
    return jax.ShapeDtypeStruct(dims, dtype)


def shards(
    tokens,
    prefix_len,
    routes,
    norm1_gain,
    w_query,
    w_key,
    w_value,
    w_output,
    norm2_gain,
    w_router,
    w_gate,
    w_up,
    w_down,
    cotangent,
):
    tok_rows, model_width = tokens.shape
    groups = lax.axis_size("expert")
    copies = lax.axis_size("dp")
    me = lax.axis_index("expert")
    half = lax.axis_index("dp") % 2
    exp_dev, _, hidden_units = w_gate.shape
    half_units = hidden_units // 2
    experts = exp_dev * groups
    f32 = jnp.float32
    seq_len = tok_rows * groups
    low = jnp.bfloat16

    def send(block, pair_flip, flip):
        return lax.ppermute(
            block,
            ("dp", "expert"),
            [
                (i * groups + j, (i ^ pair_flip) * groups + (j ^ flip))
                for i in range(copies)
                for j in range(groups)
            ],
        )

    def gather_even(block, pairs):
        return [
            block if (s, r) == (0, 0) else send(block, s, r)
            for s in range(pairs)
            for r in range(0, groups, 2)
        ]

    def gather_odd(even):
        out = []
        for b in even:
            out += [b, send(b, 0, 1)]
        return out

    def gather(block, pairs):
        return gather_odd(gather_even(block, pairs))

    def core_sum(odd, even):
        return even + send(odd, 0, 1).astype(jnp.float32)

    def swap(mine, pairs):
        mine = mine.astype(low)
        spots = [(s, r) for s in range(pairs) for r in range(0, groups, 2)]
        return [send(mine[n], *spots[n]) for n in range(1, len(spots))]

    tokens_even = gather_even(tokens, 1)
    cosine, sine = rope_tables(me, tok_rows, groups)
    cosine, sine, *tokens_even = lax.optimization_barrier((cosine, sine, *tokens_even))
    tokens_blocks = gather_odd(tokens_even)
    routed = jnp.any(
        routes[:, :, None] == jnp.arange(experts, dtype=jnp.int32)[None, None, :], axis=1
    )
    cot_mask = jnp.concatenate(
        [cotangent, jnp.pad(routed.astype(low), ((0, 0), (0, LANES - experts)))], axis=1
    )
    first_cot = cot_mask
    cot_mask, *tokens_even = lax.optimization_barrier((cot_mask, *tokens_even))
    cot_even = [
        cot_mask if q == (0, 0) else send(first_cot if q == (1, 0) else cot_mask, *q)
        for q in [(s, r) for s in range(2) for r in range(0, groups, 2)]
    ]
    my_dp = lax.axis_index("dp")
    info = jnp.stack([me, prefix_len[0], half, my_dp]).astype(jnp.int32)
    gain_one, gain_two = norm1_gain[None], norm2_gain[None]

    q_low, k_two, v_two, lse, attended, hidden_state, normed2, normed1_all = call(
        forward_kernel,
        (
            shape(tok_rows, H * HD),
            shape(KV, seq_len, LANES),
            shape(KV, seq_len, LANES),
            shape(KV, 2 * tok_rows, dtype=f32),
            shape(tok_rows, H * HD),
            shape(tok_rows, model_width, dtype=f32),
            shape(tok_rows, model_width),
            shape(seq_len, model_width),
        ),
        "attention_forward",
        hbm=(1, 4),
        hbm_out=(0, 1, 2, 7),
        scratch=(
            pltpu.VMEM((model_width, H * HD), low),
            pltpu.VMEM((H * HD, model_width), low),
            pltpu.VMEM((tok_rows, H * HD), low),
            pltpu.VMEM((KV, seq_len, LANES), low),
            pltpu.VMEM((KV, seq_len, LANES), low),
            pltpu.VMEM((seq_len, model_width), low),
            pltpu.SemaphoreType.DMA((2,)),
            pltpu.SemaphoreType.DMA((4,)),
        ),
    )(
        info, w_query, w_key, w_value, w_output, gain_one, gain_two, cosine, sine, *tokens_blocks,
    )

    normed2, *cot_even = lax.optimization_barrier((normed2, *cot_even))
    cot_blocks = gather_odd(cot_even)
    n2_blocks = gather(normed2, 2)
    attended_even = gather_even(attended, 1)
    n_blocks = 2 * groups
    all_rows = n_blocks * tok_rows
    wide = model_width + LANES

    dma = pltpu.SemaphoreType.DMA
    units = half_units * exp_dev
    wide_acts = 3 * half_units + LANES
    sums, acts = call(
        lambda *refs: experts_kernel(*refs, n_blocks=n_blocks, experts=experts, tiles=2),
        (
            shape(model_width, 3 * units),
            shape(exp_dev, all_rows, wide_acts),
        ),
        "experts",
        limit=48 if all_rows <= 1024 else LIMIT_MIB,
        hbm=tuple(range(2, 5 + 2 * n_blocks)),
        hbm_out=(0, 1),
        scratch=(
            pltpu.VMEM((all_rows, model_width), low),
            pltpu.VMEM((all_rows, model_width), low),
            pltpu.VMEM((all_rows, LANES), low),
            pltpu.VMEM((exp_dev, model_width, 2 * half_units), low),
            pltpu.VMEM((exp_dev, half_units, model_width), low),
            pltpu.VMEM((exp_dev, all_rows, wide_acts), low),
            pltpu.VMEM((exp_dev, model_width, 3 * half_units), low),
            pltpu.VMEM((all_rows, LANES), f32),
            pltpu.VMEM((model_width, LANES), low),
            pltpu.VMEM((all_rows, LANES), f32),
            dma((n_blocks,)),
            dma((n_blocks,)),
            dma((n_blocks,)),
            dma((exp_dev, 3)),
            dma((exp_dev, 3)),
        ),
    )(info, w_router, w_gate, w_up, w_down, *cot_blocks, *n2_blocks)
    outer = copies // 2
    shard_rows = model_width // copies
    reduced = lax.psum_scatter(
        sums,
        "dp",
        scatter_dimension=0,
        axis_index_groups=[[2 * o + p for o in range(outer)] for p in range(2)],
        tiled=True,
    )

    odd, even = call(
        rows_kernel,
        (shape(groups, tok_rows, wide), shape(groups, tok_rows, wide, dtype=f32)),
        "experts_rows",
        hbm=(1, 2, 3),
        hbm_out=(0, 1),
        scratch=(
            pltpu.VMEM((exp_dev, model_width, 2 * half_units), low),
            pltpu.VMEM((exp_dev, all_rows, 2 * half_units), low),
            pltpu.VMEM((all_rows, model_width), f32),
            pltpu.VMEM((all_rows, LANES), low),
            pltpu.VMEM((groups, tok_rows, wide), low),
            pltpu.VMEM((groups, tok_rows, wide), f32),
            dma((exp_dev, 3)),
            dma((4,)),
            dma((1,)),
        ),
    )(info, w_gate, w_up, acts)
    odd, *attended_even = lax.optimization_barrier((odd, *attended_even))
    mine = core_sum(odd, even)
    arrived = swap(mine, 2)
    attended_blocks = gather_odd(attended_even)

    (
        grad_hidden, grad_branch, grad_query, kv_odd, kv_even, grad_normed_q, mix_odd, mix_even
    ) = call(
        lambda *refs: backward_kernel(*refs, experts=experts),
        (
            shape(tok_rows, model_width, dtype=f32),
            shape(tok_rows + small_rows(experts + 1), model_width),
            shape(tok_rows, H * HD),
            shape(groups // 2, tok_rows, 2 * KV * HD),
            shape(groups // 2, tok_rows, 2 * KV * HD, dtype=f32),
            shape(tok_rows, model_width, dtype=f32),
            shape(groups, tok_rows, model_width),
            shape(groups, tok_rows, model_width, dtype=f32),
        ),
        "attention_backward",
        hbm=(12, 13, 14, 15, 16),
        hbm_out=(6, 7),
        scratch=(
            pltpu.VMEM((model_width, LANES), low),
            pltpu.VMEM((KV, seq_len, LANES), low),
            pltpu.VMEM((KV, seq_len, LANES), low),
            pltpu.VMEM((model_width, H * HD), low),
            pltpu.VMEM((all_rows, units), low),
            pltpu.VMEM((units, model_width), low),
            pltpu.VMEM((groups, tok_rows, model_width), low),
            pltpu.VMEM((groups, tok_rows, model_width), f32),
            dma((3,)),
            dma((2 * exp_dev,)),
        ),
    )(
        info, mine[0], cot_mask, normed2, hidden_state, w_router, gain_two, w_output,
        q_low, lse, cosine, sine, k_two, v_two, w_query, acts, w_down, *arrived,
    )
    kv_mine = core_sum(kv_odd, kv_even)
    kv_arrived = swap(kv_mine, 1)
    mix_odd, kv_mine = lax.optimization_barrier((mix_odd, kv_mine))
    mix_got = send(mix_odd, 0, 1)
    n_own = groups // 2
    mix_got_pair = send(
        (mix_even[n_own:] + mix_got[n_own:].astype(f32)).astype(low), 1, 0
    )
    query_later, grad_branch, *kv_arrived = lax.optimization_barrier(
        (grad_query, grad_branch, *kv_arrived)
    )
    branch_even = gather_even(grad_branch, 1)
    query_even = gather_even(query_later, 1)
    grad_kv, grad_tokens = call(
        tokens_kernel,
        (
            shape(tok_rows + small_rows(1), 2 * KV * HD),
            shape(tok_rows, model_width),
        ),
        "tokens_backward",
        smem=False,
    )(
        kv_mine[0], grad_normed_q, w_key, w_value, tokens, gain_one, grad_hidden, cosine, sine,
        *kv_arrived,
    )
    grad_kv, mix_got_pair, *later = lax.optimization_barrier(
        (grad_kv, mix_got_pair, *branch_even, *query_even)
    )
    kv_even_blocks = gather_even(grad_kv, 1)
    branch_blocks = gather_odd(later[: len(branch_even)])
    query_blocks = gather_odd(later[len(branch_even) :])
    own_rows = model_width // (copies * groups)
    n_early, n_late = model_width + LANES + H * HD, 2 * KV * HD + LANES
    select = pltpu.VMEM((copies * own_rows, model_width), low)
    early_odd, early_even, normed1_t = call(
        lambda *refs: early_dense_kernel(*refs, groups=groups, count=experts + 1),
        (
            shape(outer, own_rows, n_early),
            shape(outer, own_rows, n_early, dtype=f32),
            shape(copies * own_rows, seq_len),
        ),
        "dense_early",
        scratch=(select,),
    )(info, normed1_all, *attended_blocks, *branch_blocks, *query_blocks)
    early = early_even + send(early_odd, 1, 0).astype(f32)
    _, *kv_even_blocks = lax.optimization_barrier((early_odd, *kv_even_blocks))
    kv_blocks = gather_odd(kv_even_blocks)
    late_odd, late_even = call(
        lambda *refs: late_dense_kernel(*refs, lane=experts + 1),
        (shape(outer, own_rows, n_late), shape(outer, own_rows, n_late, dtype=f32)),
        "dense_late",
        scratch=(select,),
    )(info, normed1_t, *kv_blocks)
    mix_got_pair, late_odd = lax.optimization_barrier((mix_got_pair, late_odd))
    mix_pair = mix_even[:n_own] + mix_got[:n_own].astype(f32) + mix_got_pair.astype(f32)
    mixture = mix_pair[0]
    for a in swap(mix_pair, 1):
        mixture = mixture + a.astype(f32)
    block_out = (hidden_state + mixture).astype(low)
    late = late_even + send(late_odd, 1, 0).astype(f32)
    o_end, k_end = model_width + LANES, 2 * KV * HD
    dense_send = jnp.concatenate(
        [
            early[1:, :, :model_width],
            early[1:, :, model_width:o_end] + late[1:, :, k_end:],
            early[1:, :, o_end:],
            late[1:, :, :k_end],
        ],
        axis=2,
    ).astype(low)

    swapped = send(
        lax.dynamic_slice_in_dim(reduced, (1 - half) * shard_rows, shard_rows, 0), 1, 0
    )
    _, dense_send = lax.optimization_barrier((reduced, dense_send))
    dense_arrived = [send(dense_send[o - 1], 2 * o, 0) for o in range(1, outer)]
    k_cols = KV * HD
    (
        grad_gate_w, grad_up_w, grad_down_w, grad_query_w, grad_key_w, grad_value_w,
        grad_output_w, grad_router, grad_norm1, grad_norm2,
    ) = call(
        lambda *refs: final_kernel(*refs, n_early=n_early, n_late=n_late),
        (
            shape(exp_dev, shard_rows, hidden_units, dtype=f32),
            shape(exp_dev, shard_rows, hidden_units, dtype=f32),
            shape(exp_dev, hidden_units, shard_rows, dtype=f32),
            shape(own_rows, H * HD, dtype=f32),
            shape(own_rows, k_cols, dtype=f32),
            shape(own_rows, k_cols, dtype=f32),
            shape(own_rows, model_width, dtype=f32),
            shape(experts, own_rows, dtype=f32),
            shape(1, own_rows, dtype=f32),
            shape(1, own_rows, dtype=f32),
        ),
        "place",
        limit=48,
    )(info, reduced, swapped, early, late, *dense_arrived)
    return (
        block_out,
        grad_tokens,
        grad_norm1[0],
        grad_query_w,
        grad_key_w,
        grad_value_w,
        grad_output_w,
        grad_norm2[0],
        grad_router.T,
        grad_gate_w,
        grad_up_w,
        grad_down_w,
    )


def solution(mesh):
    return jax.shard_map(
        shards,
        mesh=mesh,
        in_specs=(
            P(("dp", "expert"), None),
            P("dp"),
            P(("dp", "expert"), None),
            P(),
            P(),
            P(),
            P(),
            P(),
            P(),
            P(),
            P("expert", None, None),
            P("expert", None, None),
            P("expert", None, None),
            P(("dp", "expert"), None),
        ),
        out_specs=(
            P(("dp", "expert"), None),
            P(("dp", "expert"), None),
            P(("dp", "expert")),
            P(("dp", "expert"), None),
            P(("dp", "expert"), None),
            P(("dp", "expert"), None),
            P(("dp", "expert"), None),
            P(("dp", "expert")),
            P(("dp", "expert"), None),
            P("expert", "dp", None),
            P("expert", "dp", None),
            P("expert", None, "dp"),
        ),
        check_vma=False,
    )
```
